32 devices in a mesh: fsdp: 8 (over y, x, core), tp: 4 (over z).
Axes of the slice: x: 2, y: 2, z: 4, core: 2. Of those that a mesh axis runs over, the one named last changes fastest.
Arguments:
- inputs: bfloat16 [32, 448, 768], P(('fsdp', 'tp')), may hold values from -6 to 6
- encoder: bfloat16 [32, 1500, 768], P('fsdp', 'tp'), may hold values from -6 to 6
- lengths: int32 [32], P('fsdp'), may hold values from 56 to 448, as said below
- self_qkv: bfloat16 [3, 768, 768], P(None, 'fsdp', 'tp'), may hold values from -0.21875 to 0.21875
- self_out: bfloat16 [768, 768], P('tp', 'fsdp'), may hold values from -0.875 to 0.875
- cross_q: bfloat16 [768, 768], P('fsdp', 'tp'), may hold values from -0.21875 to 0.21875
- cross_kv: bfloat16 [2, 768, 768], P(None, 'fsdp', 'tp'), may hold values from -0.21875 to 0.21875
- cross_out: bfloat16 [768, 768], P('tp', 'fsdp'), may hold values from -1.25 to 1.25
- fc_in: bfloat16 [768, 3072], P('fsdp', 'tp'), may hold values from -0.21875 to 0.21875
- fc_out: bfloat16 [3072, 768], P('tp', 'fsdp'), may hold values from -0.109375 to 0.109375
- norm_gain: float32 [4, 768], P(None, ('fsdp', 'tp')), may hold values from 0.5 to 1.5
- norm_bias: float32 [4, 768], P(None, ('fsdp', 'tp')), may hold values from -4 to 4
- proj_bias: float32 [7, 768], P(None, ('fsdp', 'tp')), may hold values from -4 to 4
- fc_in_bias: float32 [3072], P(('fsdp', 'tp')), may hold values from -4 to 4
- cotangent: bfloat16 [32, 448, 768], P(('fsdp', 'tp')), may hold values from -6 to 6
Outputs:
- layer_out: bfloat16 [32, 448, 768], P(('fsdp', 'tp'))
- grad_inputs: float32 [32, 448, 768], P(('fsdp', 'tp'))
- grad_encoder: float32 [32, 1500, 768], P('fsdp', 'tp')
- grad_self_qkv: float32 [3, 768, 768], P(None, 'fsdp', 'tp')
- grad_self_out: float32 [768, 768], P('tp', 'fsdp')
- grad_cross_q: float32 [768, 768], P('fsdp', 'tp')
- grad_cross_kv: float32 [2, 768, 768], P(None, 'fsdp', 'tp')
- grad_cross_out: float32 [768, 768], P('tp', 'fsdp')
- grad_fc_in: float32 [768, 3072], P('fsdp', 'tp')
- grad_fc_out: float32 [3072, 768], P('tp', 'fsdp')
- grad_norm_gain: float32 [4, 768], P(None, ('fsdp', 'tp'))
- grad_norm_bias: float32 [4, 768], P(None, ('fsdp', 'tp'))
- grad_proj_bias: float32 [7, 768], P(None, ('fsdp', 'tp'))
- grad_fc_in_bias: float32 [3072], P(('fsdp', 'tp'))
The draws below stay inside these ranges and needn't reach their ends.
Inputs may be any that keep to these rules, and one draw needn't show every extreme that they name: `lengths`: valid tokens of each sequence; later positions are padding and never serve as keys.
All inputs are finite; a program needn't handle non-finite values.
Results may differ from the reference program's by a relative error of at most 0.035.
Values may be sent and summed in bfloat16 or wider, within the bound.
No kernel may reach another device: no remote copies, remote signals or barrier semaphores. Data moves between devices by JAX's collectives and lax.ppermute only.
A program may use at most 192 MiB of HBM per device.

```python
import jax
import jax.numpy as jnp
from jax import lax

D = 768
HEADS = 12
HD = 64
FF = 3072
FRAMES = 1500
SEQ_LEN = 448
SEQS = 32


def draw_lengths(key, part):
    key_lengths, key_places = jax.random.split(jax.random.fold_in(key, 11))
    drawn_lengths = jax.random.randint(key_lengths, (SEQS,), SEQ_LEN // 8, SEQ_LEN + 1)
    shuffled = jax.random.permutation(key_places, SEQS)
    drawn_lengths = drawn_lengths.at[shuffled[0]].set(SEQ_LEN)
    drawn_lengths = drawn_lengths.at[shuffled[1]].set(SEQ_LEN // 8)
    return drawn_lengths.astype(jnp.int32)


def block_levels(stream_key, shape, shards, low, top_value):
    def one(axis_at, blocks):
        heights = jax.random.uniform(jax.random.fold_in(jax.random.fold_in(stream_key, 6), axis_at), (blocks,), jnp.float32, low / len(shards), top_value / len(shards))
        return jnp.repeat(jnp.exp(heights), shape[axis_at] // blocks).reshape((-1,) + (1,) * (len(shape) - axis_at - 1))

    loudness = one(*shards[0])
    for cut in shards[1:]:
        loudness = loudness * one(*cut)
    return loudness


def centred(rng, shape, scale, reach, cuts=(), held_as=jnp.bfloat16):
    gain = block_levels(rng, shape, cuts, -0.22, 0.18) if cuts else 1.0
    values = jax.random.normal(rng, shape, jnp.float32) * scale * gain
    return jnp.minimum(jnp.maximum(values, -reach), reach).astype(held_as)


def setup_inputs(seed: int = 0) -> dict:
    arg_keys = jax.random.split(jax.random.key(seed), 16)
    return {
        "inputs": centred(arg_keys[0], (SEQS, SEQ_LEN, D), 1.0, 6.0, ((0, 32),)),
        "encoder": centred(arg_keys[1], (SEQS, FRAMES, D), 1.0, 6.0, ((0, 8), (1, 4))),
        "lengths": draw_lengths(jax.random.fold_in(arg_keys[15], 71), 0),
        "self_qkv": centred(arg_keys[3], (3, D, D), D ** -0.5, 0.21875, ((1, 8), (2, 4))),
        "self_out": centred(arg_keys[4], (D, D), (D // 16) ** -0.5, 0.875, ((0, 4), (1, 8))),
        "cross_q": centred(arg_keys[5], (D, D), D ** -0.5, 0.21875, ((0, 8), (1, 4))),
        "cross_kv": centred(arg_keys[6], (2, D, D), D ** -0.5, 0.21875, ((1, 8), (2, 4))),
        "cross_out": centred(arg_keys[7], (D, D), (D // 32) ** -0.5, 1.25, ((0, 4), (1, 8))),
        "fc_in": centred(arg_keys[8], (D, FF), D ** -0.5, 0.21875, ((0, 8), (1, 4))),
        "fc_out": centred(arg_keys[9], (FF, D), FF ** -0.5, 0.109375, ((0, 4), (1, 8))),
        "norm_gain": jnp.clip(1.0 + 0.1 * jax.random.normal(arg_keys[10], (4, D), jnp.float32), 0.5, 1.5),
        "norm_bias": centred(arg_keys[11], (4, D), 0.3, 4.0, ((1, 32),), jnp.float32),
        "proj_bias": centred(arg_keys[12], (7, D), 0.3, 4.0, ((1, 32),), jnp.float32),
        "fc_in_bias": centred(arg_keys[13], (FF,), 0.3, 4.0, ((0, 32),), jnp.float32),
        "cotangent": centred(arg_keys[14], (SEQS, SEQ_LEN, D), 1.0, 6.0, ((0, 32),)),
    }


EPSILON = 1e-05
NEGATIVE = -1e+30
HIGHEST = lax.Precision.HIGHEST

@jax.custom_vjp
def low(v):
    return lax.optimization_barrier(v.astype(jnp.bfloat16)).astype(jnp.float32)

@jax.custom_vjp
def low_back(v):
    return v

def low_keep(v):
    return (low(v), None)

def low_pass(kept, grad):
    return (grad,)

def back_keep(v):
    return (v, None)

def back_low(kept, grad):
    return (low(grad),)
low.defvjp(low_keep, low_pass)
low_back.defvjp(back_keep, back_low)

def layer_norm(values, gain_row, shift_row):
    center = values - lax.optimization_barrier(jnp.mean(values, -1, keepdims=True))
    inverse = lax.rsqrt(lax.optimization_barrier(jnp.mean(center * center, -1, keepdims=True)) + EPSILON)
    return center * inverse * gain_row + shift_row

def product(left_side, right_side):
    return jnp.matmul(left_side, right_side, precision=HIGHEST)

def attend(queries, keys, values, allowed):
    scores = low_back(jnp.einsum('qhd,khd->hqk', queries, keys, precision=HIGHEST))
    if allowed is not None:
        scores = jnp.where(allowed[None], scores, NEGATIVE)
    weights = low(jax.nn.softmax(scores, axis=-1))
    return jnp.einsum('hqk,khd->qhd', weights, values, precision=HIGHEST)

def layer(inputs, encoder, group_lengths, params):
    self_qkv, self_out, cross_q, cross_kv, cross_out, fc_in, fc_out, norm_gain, norm_bias, proj_bias, fc_in_bias = params
    seq_count = inputs.shape[0]
    head_scale = HD ** (-0.5)
    positions = jnp.arange(SEQ_LEN)

    def heads(flat, rows):
        return flat.reshape(seq_count, rows, HEADS, HD)
    normed_one = low(layer_norm(inputs, norm_gain[0], norm_bias[0]))
    queries_one = low(low_back((product(normed_one, self_qkv[0]) + proj_bias[0]) * head_scale))
    keys_one = low(low_back(product(normed_one, self_qkv[1])))
    values_one = low(low_back(product(normed_one, self_qkv[2]) + proj_bias[1]))

    def self_block(item):
        query_seq, key_seq, value_seq, length = item
        allowed = (positions[None, :] <= positions[:, None]) & (positions[None, :] < length)
        return attend(query_seq, key_seq, value_seq, allowed).reshape(SEQ_LEN, D)
    attended_one = lax.map(jax.checkpoint(self_block), (heads(queries_one, SEQ_LEN), heads(keys_one, SEQ_LEN), heads(values_one, SEQ_LEN), group_lengths))
    mixed_one = low(low_back(attended_one))
    first = inputs + low_back(product(mixed_one, self_out) + proj_bias[2])
    normed_two = low(layer_norm(first, norm_gain[1], norm_bias[1]))
    queries_two = low(low_back((product(normed_two, cross_q) + proj_bias[3]) * head_scale))
    keys_two = low(low_back(product(encoder, cross_kv[0])))
    values_two = low(low_back(product(encoder, cross_kv[1]) + proj_bias[4]))

    def cross_block(item):
        query_seq, key_seq, value_seq = item
        return attend(query_seq, key_seq, value_seq, None).reshape(SEQ_LEN, D)
    attended_two = lax.map(jax.checkpoint(cross_block), (heads(queries_two, SEQ_LEN), heads(keys_two, FRAMES), heads(values_two, FRAMES)))
    mixed_two = low(low_back(attended_two))
    second = first + low_back(product(mixed_two, cross_out) + proj_bias[5])
    normed_three = low(layer_norm(second, norm_gain[2], norm_bias[2]))
    before = low_back(product(normed_three, fc_in) + fc_in_bias)
    hidden = low(jax.nn.gelu(before, approximate=False))
    third = second + low_back(product(hidden, fc_out) + proj_bias[6])
    return layer_norm(third, norm_gain[3], norm_bias[3])

def reference(inputs, encoder, lengths, self_qkv, self_out, cross_q, cross_kv, cross_out, fc_in, fc_out, norm_gain, norm_bias, proj_bias, fc_in_bias, cotangent):
    params = tuple((matrix.astype(jnp.float32) for matrix in (self_qkv, self_out, cross_q, cross_kv, cross_out, fc_in, fc_out, norm_gain, norm_bias, proj_bias, fc_in_bias)))
    batches = SEQS // 8

    def one_group(totals, item):
        group_inputs, group_encoder, group_lengths, group_cot = item

        def forward(layer_inputs, layer_encoder, layer_params):
            return layer(layer_inputs, layer_encoder, group_lengths, layer_params)
        result, pullback = jax.vjp(forward, group_inputs.astype(jnp.float32), group_encoder.astype(jnp.float32), params)
        grad_in, grad_enc, grad_params = pullback(group_cot.astype(jnp.float32))
        totals = jax.tree.map(jnp.add, totals, grad_params)
        return (totals, (result.astype(jnp.bfloat16), grad_in, grad_enc))
    zero_params = jax.tree.map(jnp.zeros_like, params)
    totals, (results, grads_in, grads_enc) = lax.scan(one_group, zero_params, (inputs.reshape(batches, 8, SEQ_LEN, D), encoder.reshape(batches, 8, FRAMES, D), lengths.reshape(batches, 8), cotangent.reshape(batches, 8, SEQ_LEN, D)))
    return (results.reshape(SEQS, SEQ_LEN, D), grads_in.reshape(SEQS, SEQ_LEN, D), grads_enc.reshape(SEQS, FRAMES, D), totals[0], totals[1], totals[2], totals[3], totals[4], totals[5], totals[6], totals[7], totals[8], totals[9], totals[10])
```

```python
import functools

import jax
import jax.numpy as jnp
from jax import lax
from jax.experimental import pallas as pl
from jax.experimental.pallas import tpu as pltpu
from jax.sharding import PartitionSpec as P

HD = 64
EPSILON = 1e-05
NEGATIVE = -1e30
BF = jnp.bfloat16
F32 = jnp.float32


def dot(left, right, left_dim=1, right_dim=0):
    return lax.dot_general(
        left, right, (((left_dim,), (right_dim,)), ((), ())), preferred_element_type=F32
    )


def layer_norm_parts(rows):
    center = rows - jnp.mean(rows, -1, keepdims=True)
    inverse = lax.rsqrt(jnp.mean(center * center, -1, keepdims=True) + EPSILON)
    return center * inverse, inverse


def norm_back(grad_rows, unit, inverse, gain):
    scaled = grad_rows * gain
    return inverse * (
        scaled
        - jnp.mean(scaled, -1, keepdims=True)
        - unit * jnp.mean(scaled * unit, -1, keepdims=True)
    )


def column_sum(rows):
    return jnp.sum(rows, 0, keepdims=True)


def whole(shape):
    zeros = (0,) * len(shape)
    return pl.BlockSpec(shape, lambda t, *_: zeros)


def per_block(shape):
    rest = (0,) * (len(shape) - 1)
    return pl.BlockSpec((1,) + tuple(shape[1:]), lambda t, *_: (t,) + rest)


def packed(shape):
    return pl.BlockSpec((shape[0], 1) + tuple(shape[2:]), lambda t, *_: (0, t, 0, 0))


def sds(shape, dtype):
    return jax.ShapeDtypeStruct(tuple(shape), dtype)


def call(body, name, grid, ins, outs, scratch, flops, scalars=()):
    moved = sum(a.size * a.dtype.itemsize for a, _ in ins)
    moved += sum(o.size * o.dtype.itemsize for o, _ in outs)
    return pl.pallas_call(
        body,
        out_shape=[o for o, _ in outs],
        grid_spec=pltpu.PrefetchScalarGridSpec(
            num_scalar_prefetch=len(scalars),
            grid=(grid,),
            in_specs=[s for _, s in ins],
            out_specs=[s for _, s in outs],
            scratch_shapes=scratch,
        ),
        compiler_params=pltpu.CompilerParams(
            dimension_semantics=("arbitrary",), vmem_limit_bytes=60 * 2**20
        ),
        cost_estimate=pl.CostEstimate(flops=flops, bytes_accessed=moved, transcendentals=0),
        name=name,
    )(*scalars, *[a for a, _ in ins])


def head_lanes(rows, head, block):
    lane = lax.broadcasted_iota(jnp.int32, rows.shape, 1)
    return jnp.where((lane >= head * block) & (lane < (head + 1) * block), rows, jnp.zeros_like(rows))


def last_part(w, hw):
    start = (3 * hw) // 128 * 128
    return w[:, start:], 3 * hw - start


def project_out(mixed, w, hw):
    tail, extra = last_part(w, hw)
    if extra:
        mixed = jnp.concatenate([jnp.zeros((mixed.shape[0], extra), mixed.dtype), mixed], 1)
    return dot(mixed, tail, 1, 1)


def project_back(branch, w, hw):
    tail, extra = last_part(w, hw)
    return dot(branch, tail)[:, extra:]


def weight(ref, rows):
    parts = ref[:, 0, :rows, :]
    return parts.reshape(parts.shape[0] * rows, parts.shape[2])


def self_forward(length, rows, pack, own, params, head_bias, dims):
    seq, width, blocks, hw = dims
    heads = hw // HD

    def body(len_ref, x_ref, w_ref, prm_ref, hb_ref, n1_ref, q_ref, k_ref, v_ref, lse_ref, ot_ref,
             mix_ref, first_ref, n2_ref, bias_scr, acc_scr):
        t = pl.program_id(0)

        @pl.when(t == 0)
        def _():
            unit, _ = layer_norm_parts(x_ref[...].astype(F32))
            n1_ref[...] = (unit * prm_ref[0:1] + prm_ref[4:5]).astype(BF)
            key = lax.broadcasted_iota(jnp.int32, (seq, seq), 0)
            query = lax.broadcasted_iota(jnp.int32, (seq, seq), 1)
            bias_scr[...] = jnp.where((key <= query) & (key < len_ref[0]), 0.0, NEGATIVE)
            acc_scr[...] = x_ref[...].astype(F32) + prm_ref[10:11]

        w = weight(w_ref, own)
        qkv = dot(n1_ref[...], w[:, : 3 * hw])
        q = ((qkv[:, :hw] + hb_ref[0, 0:1]) * HD**-0.5).astype(BF)
        k = qkv[:, hw : 2 * hw].astype(BF)
        v = (qkv[:, 2 * hw :] + hb_ref[0, 1:2]).astype(BF)
        q_ref[0] = q
        k_ref[0] = k
        v_ref[0] = v
        vt = v.T
        for j in range(heads):
            s = dot(k, head_lanes(q, j, HD), 1, 1) + bias_scr[...]
            m = jnp.max(s, 0, keepdims=True)
            p = jnp.exp(s - m)
            total = jnp.sum(p, 0, keepdims=True)
            lse_ref[0, j : j + 1] = m + jnp.log(total)
            ot_ref[0, j * HD : (j + 1) * HD] = dot(vt[j * HD : (j + 1) * HD], p.astype(BF)) / total
        mixed = ot_ref[0].T.astype(BF)
        mix_ref[0] = mixed
        acc_scr[...] += project_out(mixed, w, hw)

        @pl.when(t == blocks - 1)
        def _():
            first = acc_scr[...]
            first_ref[...] = first
            unit, _ = layer_norm_parts(first)
            n2_ref[...] = (unit * prm_ref[1:2] + prm_ref[5:6]).astype(BF)

    full = whole((seq, width))
    hb = sds((blocks, seq, hw), BF)
    return call(
        body, "self_forward", blocks,
        [(rows, full), (pack, packed(pack.shape)), (params, whole(params.shape)),
         (head_bias, per_block(head_bias.shape))],
        [(sds((seq, width), BF), full)]
        + [(hb, per_block(hb.shape))] * 3
        + [(sds((blocks, 8, seq), F32), per_block((blocks, 8, seq))),
           (sds((blocks, hw, seq), F32), per_block((blocks, hw, seq))),
           (hb, per_block(hb.shape)),
           (sds((seq, width), F32), full),
           (sds((seq, width), BF), full)],
        [pltpu.VMEM((seq, seq), F32), pltpu.VMEM((seq, width), F32)],
        8 * seq * width * width + 16 * seq * seq * width,
        (length,),
    )


def frame_keys(frames, pack, own, head_bias, dims):
    seq, width, blocks, hw = dims
    pieces, piece, _ = frames.shape
    total = pieces * piece

    def body(e_ref, w_ref, hb_ref, k_ref, v_ref, kt_ref, vt_ref):
        w = weight(w_ref, own)[:, : 2 * hw]
        for c in range(pieces):
            kv = dot(e_ref[c], w)
            k = kv[:, :hw].astype(BF)
            v = (kv[:, hw:] + hb_ref[0, 3:4]).astype(BF)
            k_ref[0, c] = k
            v_ref[0, c] = v
            kt_ref[0, :, c * piece : (c + 1) * piece] = k.T
            vt_ref[0, :, c * piece : (c + 1) * piece] = v.T

    kv = sds((blocks, pieces, piece, hw), BF)
    kvt = sds((blocks, hw, total), BF)
    return call(
        body, "frame_keys", blocks,
        [(frames, whole(frames.shape)), (pack, packed(pack.shape)),
         (head_bias, per_block(head_bias.shape))],
        [(kv, per_block(kv.shape))] * 2 + [(kvt, per_block(kvt.shape))] * 2,
        [],
        4 * total * width * width,
    )


def cross_forward(n2, first, pack, own, params, head_bias, keys, values_t, valid, dims):
    seq, width, blocks, hw = dims
    heads = hw // HD
    _, pieces, piece, _ = keys.shape
    total_keys = pieces * piece

    def body(n2_ref, first_ref, w_ref, prm_ref, hb_ref, k_ref, vt_ref, q_ref, lse_ref, ot_ref,
             mix_ref, second_ref, n3_ref, s_scr, p_scr, acc_scr):
        t = pl.program_id(0)

        @pl.when(t == 0)
        def _():
            acc_scr[...] = first_ref[...] + prm_ref[13:14]

        q = ((dot(n2_ref[...], weight(w_ref, own)[:, 2 * hw : 3 * hw]) + hb_ref[0, 2:3]) * HD**-0.5).astype(BF)
        q_ref[0] = q
        row = lax.broadcasted_iota(jnp.int32, (piece, 1), 0)
        pad = jnp.where(row < valid, 0.0, NEGATIVE)

        for j in range(heads):
            qm = head_lanes(q, j, HD)

            def score(c, m):
                s = dot(k_ref[0, c], qm, 1, 1) + pad
                s_scr[c] = s
                return jnp.maximum(m, jnp.max(s, 0, keepdims=True))

            m = lax.fori_loop(0, pieces, score, jnp.full((1, seq), NEGATIVE, F32))

            def weigh(c, total):
                p = jnp.exp(s_scr[c] - m)
                p_scr[pl.ds(pl.multiple_of(c * piece, piece), piece)] = p.astype(BF)
                return total + jnp.sum(p, 0, keepdims=True)

            total = lax.fori_loop(0, pieces, weigh, jnp.zeros((1, seq), F32))
            lse_ref[0, j : j + 1] = m + jnp.log(total)
            at = j * HD
            ot_ref[0, at : at + HD] = dot(vt_ref[0, at : at + HD], p_scr[...]) / total

        mixed = ot_ref[0].T.astype(BF)
        mix_ref[0] = mixed
        acc_scr[...] += project_out(mixed, weight(w_ref, own), hw)

        @pl.when(t == blocks - 1)
        def _():
            second = acc_scr[...]
            second_ref[...] = second
            unit, _ = layer_norm_parts(second)
            n3_ref[...] = (unit * prm_ref[2:3] + prm_ref[6:7]).astype(BF)

    full = whole((seq, width))
    hb = sds((blocks, seq, hw), BF)
    return call(
        body, "cross_forward", blocks,
        [(n2, full), (first, full), (pack, packed(pack.shape)), (params, whole(params.shape)),
         (head_bias, per_block(head_bias.shape)), (keys, per_block(keys.shape)),
         (values_t, per_block(values_t.shape))],
        [(hb, per_block(hb.shape)),
         (sds((blocks, 8, seq), F32), per_block((blocks, 8, seq))),
         (sds((blocks, hw, seq), F32), per_block((blocks, hw, seq))),
         (hb, per_block(hb.shape)),
         (sds((seq, width), F32), full),
         (sds((seq, width), BF), full)],
        [pltpu.VMEM((pieces, piece, seq), F32), pltpu.VMEM((total_keys, seq), BF),
         pltpu.VMEM((seq, width), F32)],
        4 * seq * width * width + 16 * seq * total_keys * width,
    )


def feed_forward(n3, second, pack_in, pack_out, own, params, cotangent, dims):
    seq, width, blocks, hw = dims

    def body(n3_ref, second_ref, wi_ref, wo_ref, prm_ref, cot_ref, hid_ref, slope_ref, out_ref,
             g3_ref, b3_ref, sum_ref, acc_scr):
        t = pl.program_id(0)

        @pl.when(t == 0)
        def _():
            acc_scr[...] = second_ref[...] + prm_ref[14:15]

        before = dot(n3_ref[...], weight(wi_ref, own)) + prm_ref[pl.ds(15 + t, 1)]
        phi = 0.5 + 0.5 * lax.erf(before * 2**-0.5)
        hidden = (before * phi).astype(BF)
        hid_ref[0] = hidden
        slope_ref[0] = phi + before * (jnp.exp(-0.5 * before * before) * 0.3989422804014327)
        acc_scr[...] += dot(hidden, weight(wo_ref, own), 1, 1)

        @pl.when(t == blocks - 1)
        def _():
            unit, inverse = layer_norm_parts(acc_scr[...])
            out_ref[...] = (unit * prm_ref[3:4] + prm_ref[7:8]).astype(BF)
            cot = cot_ref[...].astype(F32)
            grad = norm_back(cot, unit, inverse, prm_ref[3:4])
            g3_ref[...] = grad
            branch = grad.astype(BF)
            b3_ref[...] = branch
            sum_ref[0:1] = column_sum(cot * unit)
            sum_ref[1:2] = column_sum(cot)
            sum_ref[2:3] = column_sum(branch.astype(F32))

    full = whole((seq, width))
    wide = (blocks, seq, width)
    return call(
        body, "feed_forward", blocks,
        [(n3, full), (second, full), (pack_in, packed(pack_in.shape)),
         (pack_out, packed(pack_out.shape)), (params, whole(params.shape)), (cotangent, full)],
        [(sds(wide, BF), per_block(wide)), (sds(wide, F32), per_block(wide)),
         (sds((seq, width), BF), full), (sds((seq, width), F32), full),
         (sds((seq, width), BF), full), (sds((8, width), F32), whole((8, width)))],
        [pltpu.VMEM((seq, width), F32)],
        16 * seq * width * width,
    )


def store_pack(ref, rows, value):
    ref[:, 0] = value.reshape(ref.shape[0], rows, value.shape[1]).astype(ref.dtype)


def feed_backward(b3, g3, hidden, slope, pack_in, pack_out, own, n3, second, params, grad_shape, dims):
    seq, width, blocks, hw = dims
    own_out = grad_shape[2]

    def body(b3_ref, g3_ref, hid_ref, slope_ref, wi_ref, wo_ref, n3_ref, second_ref, prm_ref,
             go_ref, gi_ref, fcb_ref, g2_ref, b2_ref, sum_ref, b3t_scr, n3t_scr, acc_scr):
        t = pl.program_id(0)

        @pl.when(t == 0)
        def _():
            b3t_scr[...] = b3_ref[...].T
            n3t_scr[...] = n3_ref[...].T
            acc_scr[...] = jnp.zeros_like(acc_scr)

        store_pack(go_ref, own_out, dot(b3t_scr[...], hid_ref[0]))
        grad_before = (dot(b3_ref[...], weight(wo_ref, own)) * slope_ref[0]).astype(BF)
        fcb_ref[0, 0:1] = column_sum(grad_before.astype(F32))
        store_pack(gi_ref, own_out, dot(n3t_scr[...], grad_before))
        acc_scr[...] += dot(grad_before, weight(wi_ref, own), 1, 1)

        @pl.when(t == blocks - 1)
        def _():
            grad = acc_scr[...]
            unit, inverse = layer_norm_parts(second_ref[...])
            sum_ref[0:1] = column_sum(grad * unit)
            sum_ref[1:2] = column_sum(grad)
            grad_second = g3_ref[...] + norm_back(grad, unit, inverse, prm_ref[2:3])
            g2_ref[...] = grad_second
            branch = grad_second.astype(BF)
            b2_ref[...] = branch
            sum_ref[2:3] = column_sum(branch.astype(F32))

    full = whole((seq, width))
    wide = (blocks, seq, width)
    grads = sds(grad_shape, BF)
    return call(
        body, "feed_backward", blocks,
        [(b3, full), (g3, full), (hidden, per_block(wide)), (slope, per_block(wide)),
         (pack_in, packed(pack_in.shape)), (pack_out, packed(pack_out.shape)), (n3, full),
         (second, full), (params, whole(params.shape))],
        [(grads, packed(grad_shape))] * 2
        + [(sds((blocks, 8, width), F32), per_block((blocks, 8, width))),
           (sds((seq, width), F32), full), (sds((seq, width), BF), full),
           (sds((8, width), F32), whole((8, width)))],
        [pltpu.VMEM((width, seq), BF), pltpu.VMEM((width, seq), BF), pltpu.VMEM((seq, width), F32)],
        32 * seq * width * width,
    )


def cross_backward(b2, g2, queries, keys, values, keys_t, lse, ot, mixed, frames, n2, first, pack,
                   own, params, valid, grad_shape, dims):
    seq, width, blocks, hw = dims
    heads = hw // HD
    _, pieces, piece, _ = keys.shape
    total_keys = pieces * piece
    own_out = grad_shape[2]

    def body(b2_ref, g2_ref, q_ref, k_ref, v_ref, kt_ref, lse_ref, ot_ref, mix_ref, e_ref, n2_ref,
             first_ref, w_ref, prm_ref, grad_ref, genc_ref, g1_ref, b1_ref, sum_ref, hsum_ref,
             et_scr, b2t_scr, n2t_scr, dk_scr, dv_scr, ds_scr, dqt_scr, genc_scr, acc_scr):
        t = pl.program_id(0)

        @pl.when(t == 0)
        def _():
            for c in range(pieces):
                et_scr[:, c * piece : (c + 1) * piece] = e_ref[c].T
            b2t_scr[...] = b2_ref[...].T
            n2t_scr[...] = n2_ref[...].T
            acc_scr[...] = jnp.zeros_like(acc_scr)
            genc_scr[...] = jnp.zeros_like(genc_scr)

        w = weight(w_ref, own)
        q = q_ref[0]
        gm = project_back(b2_ref[...], w, hw).astype(BF)
        weighted = gm.astype(F32).T * ot_ref[0]
        row = lax.broadcasted_iota(jnp.int32, (piece, 1), 0)
        pad = jnp.where(row < valid, 0.0, NEGATIVE)
        dk_scr[...] = jnp.zeros_like(dk_scr)
        dv_scr[...] = jnp.zeros_like(dv_scr)
        for j in range(heads):
            delta = jnp.sum(weighted[j * HD : (j + 1) * HD], 0, keepdims=True)
            shift = lse_ref[0, j : j + 1]
            qm = head_lanes(q, j, HD)
            gj = head_lanes(gm, j, HD)

            def one_piece(c, carry):
                s = dot(k_ref[0, c], qm, 1, 1) + pad
                p = jnp.exp(s - shift)
                ds = (p * (dot(v_ref[0, c], gj, 1, 1) - delta)).astype(BF)
                dv_scr[c] += dot(p.astype(BF), gj)
                dk_scr[c] += dot(ds, qm)
                ds_scr[pl.ds(pl.multiple_of(c * piece, piece), piece)] = ds
                return carry

            lax.fori_loop(0, pieces, one_piece, 0)
            dqt_scr[j * HD : (j + 1) * HD] = dot(kt_ref[0, j * HD : (j + 1) * HD], ds_scr[...])
        dq = dqt_scr[...].T.astype(BF)
        hsum_ref[0, 0:1] = column_sum(dq.astype(F32)) * HD**-0.5
        dq = (dq.astype(F32) * HD**-0.5).astype(BF)
        bias = jnp.zeros((1, hw), F32)
        wkv = w[:, : 2 * hw]
        grad_kv = jnp.zeros((width, 2 * hw), F32)
        for c in range(pieces):
            dv = dv_scr[c].astype(BF)
            bias += column_sum(dv.astype(F32))
            dkv = jnp.concatenate([dk_scr[c].astype(BF), dv], 1)
            genc_scr[c] += dot(dkv, wkv, 1, 1)
            grad_kv += dot(et_scr[:, c * piece : (c + 1) * piece], dkv)
        hsum_ref[0, 1:2] = bias
        grad_q = dot(n2t_scr[...], dq)
        grad_o = dot(b2t_scr[...], mix_ref[0])
        store_pack(grad_ref, own_out, jnp.concatenate([grad_kv, grad_q, grad_o], 1).astype(BF))
        acc_scr[...] += dot(dq, w[:, 2 * hw : 3 * hw], 1, 1)

        @pl.when(t == blocks - 1)
        def _():
            genc_ref[...] = genc_scr[...].astype(BF)
            grad = acc_scr[...]
            unit, inverse = layer_norm_parts(first_ref[...])
            sum_ref[0:1] = column_sum(grad * unit)
            sum_ref[1:2] = column_sum(grad)
            grad_first = g2_ref[...] + norm_back(grad, unit, inverse, prm_ref[1:2])
            g1_ref[...] = grad_first
            branch = grad_first.astype(BF)
            b1_ref[...] = branch
            sum_ref[2:3] = column_sum(branch.astype(F32))

    full = whole((seq, width))
    hb = per_block((blocks, seq, hw))
    once = lambda shape: pl.BlockSpec(shape, lambda t, *_: (0,) * len(shape), pipeline_mode=pl.Buffered(1))
    return call(
        body, "cross_backward", blocks,
        [(b2, full), (g2, full), (queries, hb), (keys, per_block(keys.shape)),
         (values, per_block(values.shape)), (keys_t, per_block(keys_t.shape)),
         (lse, per_block(lse.shape)), (ot, per_block(ot.shape)), (mixed, hb),
         (frames, once(frames.shape)), (n2, full), (first, full), (pack, packed(pack.shape)),
         (params, whole(params.shape))],
        [(sds(grad_shape, BF), packed(grad_shape)),
         (sds(frames.shape, BF), once(frames.shape)),
         (sds((seq, width), F32), full), (sds((seq, width), BF), full),
         (sds((8, width), F32), whole((8, width))),
         (sds((blocks, 8, hw), F32), per_block((blocks, 8, hw)))],
        [pltpu.VMEM((width, total_keys), BF), pltpu.VMEM((width, seq), BF),
         pltpu.VMEM((width, seq), BF), pltpu.VMEM((pieces, piece, hw), F32),
         pltpu.VMEM((pieces, piece, hw), F32), pltpu.VMEM((total_keys, seq), BF),
         pltpu.VMEM((hw, seq), F32), pltpu.VMEM(frames.shape, F32), pltpu.VMEM((seq, width), F32)],
        16 * seq * width * width + 8 * total_keys * width * width + 40 * seq * total_keys * width,
    )


def self_backward(length, b1, g1, queries, keys, values, lse, ot, mixed, n1, rows, pack, own, params,
                  grad_shape, dims):
    seq, width, blocks, hw = dims
    heads = hw // HD
    own_out = grad_shape[2]

    def body(len_ref, b1_ref, g1_ref, q_ref, k_ref, v_ref, lse_ref, ot_ref, mix_ref, n1_ref, x_ref,
             w_ref, prm_ref, grad_ref, gin_ref, sum_ref, hsum_ref, b1t_scr, n1t_scr, bias_scr,
             dqt_scr, acc_scr):
        t = pl.program_id(0)

        @pl.when(t == 0)
        def _():
            b1t_scr[...] = b1_ref[...].T
            n1t_scr[...] = n1_ref[...].T
            acc_scr[...] = jnp.zeros_like(acc_scr)
            key = lax.broadcasted_iota(jnp.int32, (seq, seq), 0)
            query = lax.broadcasted_iota(jnp.int32, (seq, seq), 1)
            bias_scr[...] = jnp.where((key <= query) & (key < len_ref[0]), 0.0, NEGATIVE)

        w = weight(w_ref, own)
        q = q_ref[0]
        k = k_ref[0]
        v = v_ref[0]
        kt = k.T
        gm = project_back(b1_ref[...], w, hw).astype(BF)
        weighted = gm.astype(F32).T * ot_ref[0]
        dk = jnp.zeros((seq, hw), F32)
        dv = jnp.zeros((seq, hw), F32)
        for j in range(heads):
            delta = jnp.sum(weighted[j * HD : (j + 1) * HD], 0, keepdims=True)
            qm = head_lanes(q, j, HD)
            gj = head_lanes(gm, j, HD)
            p = jnp.exp(dot(k, qm, 1, 1) + bias_scr[...] - lse_ref[0, j : j + 1])
            ds = (p * (dot(v, gj, 1, 1) - delta)).astype(BF)
            dv += dot(p.astype(BF), gj)
            dk += dot(ds, qm)
            dqt_scr[j * HD : (j + 1) * HD] = dot(kt[j * HD : (j + 1) * HD], ds)
        dq = dqt_scr[...].T.astype(BF).astype(F32) * HD**-0.5
        dv = dv.astype(BF)
        hsum_ref[0, 0:1] = column_sum(dq)
        hsum_ref[0, 1:2] = column_sum(dv.astype(F32))
        dqkv = jnp.concatenate([dq.astype(BF), dk.astype(BF), dv], 1)
        grad_qkv = dot(n1t_scr[...], dqkv)
        grad_o = dot(b1t_scr[...], mix_ref[0])
        store_pack(grad_ref, own_out, jnp.concatenate([grad_qkv, grad_o], 1).astype(BF))
        acc_scr[...] += dot(dqkv, w[:, : 3 * hw], 1, 1)

        @pl.when(t == blocks - 1)
        def _():
            grad = acc_scr[...]
            unit, inverse = layer_norm_parts(x_ref[...].astype(F32))
            sum_ref[0:1] = column_sum(grad * unit)
            sum_ref[1:2] = column_sum(grad)
            gin_ref[...] = g1_ref[...] + norm_back(grad, unit, inverse, prm_ref[0:1])

    full = whole((seq, width))
    hb = per_block((blocks, seq, hw))
    return call(
        body, "self_backward", blocks,
        [(b1, full), (g1, full), (queries, hb), (keys, hb), (values, hb),
         (lse, per_block(lse.shape)), (ot, per_block(ot.shape)), (mixed, hb), (n1, full),
         (rows, full), (pack, packed(pack.shape)), (params, whole(params.shape))],
        [(sds(grad_shape, BF), packed(grad_shape)),
         (sds((seq, width), F32), full),
         (sds((8, width), F32), whole((8, width))),
         (sds((blocks, 8, hw), F32), per_block((blocks, 8, hw)))],
        [pltpu.VMEM((width, seq), BF), pltpu.VMEM((width, seq), BF), pltpu.VMEM((seq, seq), F32),
         pltpu.VMEM((hw, seq), F32), pltpu.VMEM((seq, width), F32)],
        16 * seq * width * width + 40 * seq * seq * width,
        (length,),
    )


def pad_rows(rows, count):
    return jnp.pad(rows, ((0, count - rows.shape[0]),) + ((0, 0),) * (rows.ndim - 1))


def gather_pack(shard):
    whole_pack = lax.all_gather(shard, ("fsdp", "tp"), axis=0, tiled=False)
    return whole_pack.reshape((lax.axis_size("fsdp"), lax.axis_size("tp")) + shard.shape)


def kernel_form(pack, own):
    if own % 16 == 0:
        return pack, own
    outer, blocks, held, width = pack.shape
    flat = pack[:, :, :own].transpose(1, 0, 2, 3).reshape(1, blocks, outer * own, width)
    return flat, outer * own


def scatter_pack(grads, own):
    fsdp, tp = lax.axis_size("fsdp"), lax.axis_size("tp")
    if grads.shape[2] != own:
        blocks, width = grads.shape[1], grads.shape[3]
        grads = grads.reshape(blocks, fsdp, own, width).transpose(1, 0, 2, 3)
    place = lax.axis_index("fsdp")
    step = 1
    while step < fsdp:
        pairs = grads.reshape((grads.shape[0] // 2, 2) + grads.shape[1:])
        bit = (place // step) % 2
        kept = lax.dynamic_index_in_dim(pairs, bit, 1, keepdims=False)
        sent = lax.dynamic_index_in_dim(pairs, 1 - bit, 1, keepdims=False)
        come = lax.ppermute(sent, "fsdp", [(i, i ^ step) for i in range(fsdp)])
        grads = (kept.astype(F32) + come.astype(F32)).astype(BF)
        step *= 2
    grads = grads[0]
    here = lax.axis_index("tp")
    total = lax.dynamic_index_in_dim(grads, here, 0, keepdims=False).astype(F32)
    for hop in range(1, tp):
        sent = lax.dynamic_index_in_dim(grads, (here + hop) % tp, 0, keepdims=False)
        total += lax.ppermute(sent, "tp", [(i, (i + hop) % tp) for i in range(tp)]).astype(F32)
    return total


def local(
    inputs,
    encoder,
    lengths,
    self_qkv,
    self_out,
    cross_q,
    cross_kv,
    cross_out,
    fc_in,
    fc_out,
    norm_gain,
    norm_bias,
    proj_bias,
    fc_in_bias,
    cotangent,
):
    fsdp, tp = lax.axis_size("fsdp"), lax.axis_size("tp")
    devices = fsdp * tp
    tp_place = lax.axis_index("tp")
    seqs, seq, width = inputs.shape
    assert seqs == 1
    own, hw = cross_q.shape
    dims = (seq, width, tp, hw)
    frames_own = encoder.shape[1]
    small_own = norm_gain.shape[1]
    ff_own = fc_in_bias.shape[0]

    small = jnp.concatenate(
        [a.reshape(-1) for a in (norm_gain, norm_bias, proj_bias, fc_in_bias)]
    )
    small = jnp.pad(small, (0, width - small.size))
    high = small.astype(BF)
    low = (small - high.astype(F32)).astype(BF)
    extra = pad_rows(jnp.stack([high, low]), 16)

    pack_self = jnp.concatenate([self_qkv[0], self_qkv[1], self_qkv[2], self_out.T], 1)
    pack_self = jnp.concatenate([pack_self, extra], 0)
    pack_cross = jnp.concatenate([cross_kv[0], cross_kv[1], cross_q, cross_out.T], 1)
    w_self = gather_pack(pack_self)
    w_cross = gather_pack(pack_cross)
    w_in = gather_pack(fc_in)
    w_out = gather_pack(fc_out.T)

    table = w_self[:, :, own : own + 2].astype(F32).sum(2).reshape(devices, width)
    rows = (norm_gain.shape[0] + norm_bias.shape[0] + proj_bias.shape[0])
    params = table[:, : rows * small_own].reshape(devices, rows, small_own)
    params = params.transpose(1, 0, 2).reshape(rows, width)
    fc_bias = table[:, rows * small_own : rows * small_own + ff_own].reshape(tp, width)
    head_bias = jnp.stack([params[8], params[9], params[11], params[12]])
    head_bias = head_bias.reshape(4, tp, hw).transpose(1, 0, 2)
    head_bias = jnp.pad(head_bias, ((0, 0), (0, 4), (0, 0)))
    params = pad_rows(jnp.concatenate([params, fc_bias], 0), 24)

    w_self, own_rows = kernel_form(w_self, own)
    w_cross, _ = kernel_form(w_cross, own)
    w_in, _ = kernel_form(w_in, own)
    w_out, _ = kernel_form(w_out, own)
    grad_shape = (width // own_rows, tp, own_rows, width)

    piece = -(-frames_own // 128) * 128
    frames = lax.all_to_all(encoder, "tp", 0, 0, tiled=True)
    frames = jnp.pad(frames, ((0, 0), (0, piece - frames_own), (0, 0)))
    length = lax.dynamic_slice_in_dim(lengths, tp_place, 1)

    x = inputs[0]
    n1, q1, k1, v1, lse1, ot1, mixed1, first, n2 = self_forward(
        length, x, w_self, own_rows, params, head_bias, dims
    )
    k2, v2, k2t, v2t = frame_keys(frames, w_cross, own_rows, head_bias, dims)
    q2, lse2, ot2, mixed2, second, n3 = cross_forward(
        n2, first, w_cross, own_rows, params, head_bias, k2, v2t, frames_own, dims
    )
    hidden, slope, layer_out, g3, b3, sums3 = feed_forward(
        n3, second, w_in, w_out, own_rows, params, cotangent[0], dims
    )
    grad_out, grad_in, fcb, g2, b2, sums2 = feed_backward(
        b3, g3, hidden, slope, w_in, w_out, own_rows, n3, second, params, grad_shape, dims
    )
    grad_cross, grad_frames, g1, b1, sums1, hsum2 = cross_backward(
        b2, g2, q2, k2, v2, k2t, lse2, ot2, mixed2, frames, n2, first, w_cross, own_rows, params,
        frames_own, grad_shape, dims
    )
    grad_self, grad_inputs, sums0, hsum1 = self_backward(
        length, b1, g1, q1, k1, v1, lse1, ot1, mixed1, n1, x, w_self, own_rows, params, grad_shape,
        dims
    )

    grad_encoder = lax.all_to_all(grad_frames[:, :frames_own], "tp", 0, 0, tiled=True)

    def heads_row(block, row):
        return block[:, row].reshape(1, width)

    table = jnp.concatenate(
        [
            sums0[0:1], sums1[0:1], sums2[0:1], sums3[0:1],
            sums0[1:2], sums1[1:2], sums2[1:2], sums3[1:2],
            heads_row(hsum1, 0), heads_row(hsum1, 1), sums1[2:3],
            heads_row(hsum2, 0), heads_row(hsum2, 1), sums2[2:3], sums3[2:3],
        ],
        0,
    )
    table = table.reshape(rows, devices, small_own).transpose(1, 0, 2).reshape(devices, -1)
    table = jnp.concatenate([table, fcb[:, 0].reshape(devices, ff_own)], 1)
    mine = lax.psum_scatter(table, ("fsdp", "tp"), scatter_dimension=0, tiled=True)[0]
    rows4 = norm_gain.size
    own_gain = mine[:rows4].reshape(norm_gain.shape)
    own_shift = mine[rows4 : 2 * rows4].reshape(norm_bias.shape)
    own_bias = mine[2 * rows4 : rows * small_own].reshape(proj_bias.shape)
    own_fc_bias = mine[rows * small_own :]

    total_out = scatter_pack(grad_out, own)
    total_in = scatter_pack(grad_in, own)
    total_cross = scatter_pack(grad_cross, own)
    total_self = scatter_pack(grad_self, own)

    def part(total, index):
        return total[:, index * hw : (index + 1) * hw]

    return (
        layer_out[None],
        grad_inputs[None],
        grad_encoder.astype(F32),
        jnp.stack([part(total_self, 0), part(total_self, 1), part(total_self, 2)]),
        part(total_self, 3).T,
        part(total_cross, 2),
        jnp.stack([part(total_cross, 0), part(total_cross, 1)]),
        part(total_cross, 3).T,
        total_in,
        total_out.T,
        own_gain,
        own_shift,
        own_bias,
        own_fc_bias,
    )


def solution(mesh):
    return jax.shard_map(
        local,
        mesh=mesh,
        in_specs=(
            P(("fsdp", "tp"), None, None),
            P("fsdp", "tp", None),
            P("fsdp"),
            P(None, "fsdp", "tp"),
            P("tp", "fsdp"),
            P("fsdp", "tp"),
            P(None, "fsdp", "tp"),
            P("tp", "fsdp"),
            P("fsdp", "tp"),
            P("tp", "fsdp"),
            P(None, ("fsdp", "tp")),
            P(None, ("fsdp", "tp")),
            P(None, ("fsdp", "tp")),
            P(("fsdp", "tp")),
            P(("fsdp", "tp"), None, None),
        ),
        out_specs=(
            P(("fsdp", "tp"), None, None),
            P(("fsdp", "tp"), None, None),
            P("fsdp", "tp", None),
            P(None, "fsdp", "tp"),
            P("tp", "fsdp"),
            P("fsdp", "tp"),
            P(None, "fsdp", "tp"),
            P("tp", "fsdp"),
            P("fsdp", "tp"),
            P("tp", "fsdp"),
            P(None, ("fsdp", "tp")),
            P(None, ("fsdp", "tp")),
            P(None, ("fsdp", "tp")),
            P(("fsdp", "tp")),
        ),
        check_vma=False,
    )
```

```python
import functools

import jax
import jax.numpy as jnp
from jax import lax
from jax.experimental import pallas as pl
from jax.experimental.pallas import tpu as pltpu
from jax.sharding import PartitionSpec as P

HD = 64
EPSILON = 1e-05
NEGATIVE = -1e30
VMEM_LIMIT = 60 * 2**20
BF = jnp.bfloat16
F32 = jnp.float32


def dot(left, right, left_dim=1, right_dim=0):
    return lax.dot_general(
        left, right, (((left_dim,), (right_dim,)), ((), ())), preferred_element_type=F32
    )


def layer_norm_parts(rows):
    center = rows - jnp.mean(rows, -1, keepdims=True)
    inverse = lax.rsqrt(jnp.mean(center * center, -1, keepdims=True) + EPSILON)
    return center * inverse, inverse


def norm_back(grad_rows, unit, inverse, gain):
    scaled = grad_rows * gain
    return inverse * (
        scaled
        - jnp.mean(scaled, -1, keepdims=True)
        - unit * jnp.mean(scaled * unit, -1, keepdims=True)
    )


def put_heads(sum_ref, row, block, count, value):
    size = value.shape[1]
    for t in range(count):

        @pl.when(block == t)
        def _():
            sum_ref[row : row + 1, t * size : (t + 1) * size] = value


def column_sum(rows):
    return jnp.sum(rows, 0, keepdims=True)


def whole(shape):
    zeros = (0,) * len(shape)
    return pl.BlockSpec(shape, lambda t, *_: zeros)


def per_block(shape):
    rest = (0,) * (len(shape) - 1)
    return pl.BlockSpec((1,) + tuple(shape[1:]), lambda t, *_: (t,) + rest)


def packed(shape):
    return pl.BlockSpec((shape[0], 1) + tuple(shape[2:]), lambda t, *_: (0, t, 0, 0))


def sds(shape, dtype):
    return jax.ShapeDtypeStruct(tuple(shape), dtype)


def call(body, name, grid, ins, outs, scratch, flops, scalars=(), deps=(), carried=()):
    moved = sum(a.size * a.dtype.itemsize for a, _ in ins)
    moved += sum(o.size * o.dtype.itemsize for o, _ in outs)
    first = len(scalars) + len(ins)
    extra = list(carried) + list(deps)

    def inner(*refs):
        return body(*refs[:first], *refs[first + len(extra) :])

    return pl.pallas_call(
        inner,
        out_shape=[o for o, _ in outs],
        grid_spec=pltpu.PrefetchScalarGridSpec(
            num_scalar_prefetch=len(scalars),
            grid=(grid,),
            in_specs=[s for _, s in ins] + [pl.BlockSpec(memory_space=pl.ANY)] * len(extra),
            out_specs=[s for _, s in outs],
            scratch_shapes=scratch,
        ),
        compiler_params=pltpu.CompilerParams(
            dimension_semantics=("arbitrary",), vmem_limit_bytes=VMEM_LIMIT
        ),
        input_output_aliases={first + i: i for i in range(len(carried))},
        cost_estimate=pl.CostEstimate(flops=flops, bytes_accessed=moved, transcendentals=0),
        name=name,
    )(*scalars, *[a for a, _ in ins], *extra)


def head_lanes(rows, head, block):
    lane = lax.broadcasted_iota(jnp.int32, rows.shape, 1)
    return jnp.where((lane >= head * block) & (lane < (head + 1) * block), rows, jnp.zeros_like(rows))


def pack_in(pack):
    return [(array, packed(array.shape)) for array in pack]


def at_block(shape, start):
    rest = (0,) * (len(shape) - 1)
    return pl.BlockSpec((1,) + tuple(shape[1:]), lambda t, *_: (start + t,) + rest)


def pack_at(pack, start):
    return [
        (a, pl.BlockSpec((a.shape[0], 1) + a.shape[2:], lambda t, *_: (0, start + t, 0, 0))) for a in pack
    ]


def pack_scratch(width):
    return pltpu.VMEM((width, width), BF)


def assemble(refs, rows, place_ref, scr):
    if len(refs) == 1:
        parts = refs[0][:, 0, :rows, :]
        scr[...] = parts.reshape(parts.shape[0] * rows, parts.shape[2])
        return
    count = 2 * refs[0].shape[0]
    for f in range(count):
        distance = f ^ place_ref[0]
        source = distance >> 1
        for bit in range(2):

            @pl.when((distance & 1) == bit)
            def _():
                scr[f * rows : (f + 1) * rows] = refs[bit][source, 0, :rows, :]


def grad_outs(shape):
    return [(sds(shape, BF), packed(shape))] * (1 if shape[0] == 1 else 2)


def store_pack(refs, value, place_ref):
    rows = refs[0].shape[2]
    if len(refs) == 1:
        refs[0][0, 0] = value
        return
    for f in range(2 * refs[0].shape[0]):
        distance = f ^ place_ref[0]
        target = distance >> 1
        for bit in range(2):

            @pl.when((distance & 1) == bit)
            def _():
                refs[bit][target, 0] = value[f * rows : (f + 1) * rows]


def tail_start(hw):
    return (3 * hw) // 128 * 128


def project_out(mixed, w_scr, hw):
    start = tail_start(hw)
    extra = 3 * hw - start
    if extra:
        mixed = jnp.concatenate([jnp.zeros((mixed.shape[0], extra), mixed.dtype), mixed], 1)
    return dot(mixed, w_scr[:, start:], 1, 1)


def project_back(branch, w_scr, hw):
    start = tail_start(hw)
    return dot(branch, w_scr[:, start:])[:, 3 * hw - start :]


def self_forward(length, place, start, count, rows, part, pack, own, params, head_bias, dims, deps=(), carried=()):
    seq, width, blocks, hw = dims
    heads = hw // HD

    def body(len_ref, place_ref, x_ref, part_ref, *refs):
        w_refs, refs = refs[: len(pack)], refs[len(pack) :]
        (prm_ref, hb_ref, q_ref, k_ref, v_ref, lse_ref, ot_ref, mix_ref, n1_ref, first_ref, n2_ref,
         bias_scr, acc_scr, w_scr) = refs
        t = pl.program_id(0)
        assemble(w_refs, own, place_ref, w_scr)

        @pl.when(t == 0)
        def _():
            unit, _ = layer_norm_parts(x_ref[...].astype(F32))
            n1_ref[...] = (unit * prm_ref[0:1] + prm_ref[4:5]).astype(BF)
            key = lax.broadcasted_iota(jnp.int32, (seq, seq), 0)
            query = lax.broadcasted_iota(jnp.int32, (seq, seq), 1)
            bias_scr[...] = jnp.where((key <= query) & (key < len_ref[0]), 0.0, NEGATIVE)
            acc_scr[...] = part_ref[...].astype(F32) + prm_ref[10:11] if start == 0 else part_ref[...]

        qkv = dot(n1_ref[...], w_scr[:, : 3 * hw])
        q = ((qkv[:, :hw] + hb_ref[0, 0:1]) * HD**-0.5).astype(BF)
        k = qkv[:, hw : 2 * hw].astype(BF)
        v = (qkv[:, 2 * hw :] + hb_ref[0, 1:2]).astype(BF)
        q_ref[0] = q
        k_ref[0] = k
        v_ref[0] = v
        vt = v.T
        for j in range(heads):
            s = dot(k, head_lanes(q, j, HD), 1, 1) + bias_scr[...]
            m = jnp.max(s, 0, keepdims=True)
            p = jnp.exp(s - m)
            total = jnp.sum(p, 0, keepdims=True)
            lse_ref[0, j : j + 1] = m + jnp.log(total)
            ot_ref[0, j * HD : (j + 1) * HD] = dot(vt[j * HD : (j + 1) * HD], p.astype(BF)) / total
        mixed = ot_ref[0].T.astype(BF)
        mix_ref[0] = mixed
        acc_scr[...] += project_out(mixed, w_scr, hw)

        @pl.when(t == count - 1)
        def _():
            first = acc_scr[...]
            first_ref[...] = first
            unit, _ = layer_norm_parts(first)
            n2_ref[...] = (unit * prm_ref[1:2] + prm_ref[5:6]).astype(BF)

    full = whole((seq, width))
    hb = sds((blocks, seq, hw), BF)

    def block(shape):
        return at_block(shape, start)

    return call(
        body, "self_forward", count,
        [(rows, full), (part, full), *pack_at(pack, start), (params, whole(params.shape)),
         (head_bias, block(head_bias.shape))],
        [(hb, block(hb.shape))] * 3
        + [(sds((blocks, 8, seq), F32), block((blocks, 8, seq))),
           (sds((blocks, hw, seq), F32), block((blocks, hw, seq))),
           (hb, block(hb.shape)),
           (sds((seq, width), BF), full),
           (sds((seq, width), F32), full),
           (sds((seq, width), BF), full)],
        [pltpu.VMEM((seq, seq), F32), pltpu.VMEM((seq, width), F32), pack_scratch(width)],
        count * (8 * seq * width * hw + 16 * seq * seq * hw),
        (length, place),
        deps,
        carried,
    )


def frame_keys(place, frames, pack, own, head_bias, dims, deps=()):
    seq, width, blocks, hw = dims
    pieces, piece, _ = frames.shape
    total = pieces * piece

    def body(place_ref, e_ref, *refs):
        w_refs, refs = refs[: len(pack)], refs[len(pack) :]
        hb_ref, k_ref, v_ref, kt_ref, vt_ref, w_scr = refs
        assemble(w_refs, own, place_ref, w_scr)
        w = w_scr[:, : 2 * hw]
        for c in range(pieces):
            kv = dot(e_ref[c], w)
            k = kv[:, :hw].astype(BF)
            v = (kv[:, hw:] + hb_ref[0, 3:4]).astype(BF)
            k_ref[0, c] = k
            v_ref[0, c] = v
            kt_ref[0, :, c * piece : (c + 1) * piece] = k.T
            vt_ref[0, :, c * piece : (c + 1) * piece] = v.T

    kv = sds((blocks, pieces, piece, hw), BF)
    kvt = sds((blocks, hw, total), BF)
    return call(
        body, "frame_keys", blocks,
        [(frames, whole(frames.shape)), *pack_in(pack), (head_bias, per_block(head_bias.shape))],
        [(kv, per_block(kv.shape))] * 2 + [(kvt, per_block(kvt.shape))] * 2,
        [pack_scratch(width)],
        4 * total * width * width,
        (place,),
        deps,
    )


def cross_forward(place, start, count, n2, first, pack, own, params, head_bias, keys, values_t, valid, dims, deps=(),
                  carried=()):
    seq, width, blocks, hw = dims
    heads = hw // HD
    _, pieces, piece, _ = keys.shape
    total_keys = pieces * piece

    def body(place_ref, n2_ref, first_ref, *refs):
        w_refs, refs = refs[: len(pack)], refs[len(pack) :]
        (prm_ref, hb_ref, k_ref, vt_ref, q_ref, lse_ref, ot_ref, mix_ref, second_ref, n3_ref, s_scr,
         p_scr, acc_scr, w_scr) = refs
        t = pl.program_id(0)
        assemble(w_refs, own, place_ref, w_scr)

        @pl.when(t == 0)
        def _():
            acc_scr[...] = first_ref[...] + prm_ref[13:14] if start == 0 else first_ref[...]

        q = ((dot(n2_ref[...], w_scr[:, 2 * hw : 3 * hw]) + hb_ref[0, 2:3]) * HD**-0.5).astype(BF)
        q_ref[0] = q
        row = lax.broadcasted_iota(jnp.int32, (piece, 1), 0)
        pad = jnp.where(row < valid, 0.0, NEGATIVE)

        for j in range(heads):
            qm = head_lanes(q, j, HD)

            def score(c, m):
                s = dot(k_ref[0, c], qm, 1, 1) + pad
                s_scr[c] = s
                return jnp.maximum(m, jnp.max(s, 0, keepdims=True))

            m = lax.fori_loop(0, pieces, score, jnp.full((1, seq), NEGATIVE, F32))

            def weigh(c, total):
                p = jnp.exp(s_scr[c] - m)
                p_scr[pl.ds(pl.multiple_of(c * piece, piece), piece)] = p.astype(BF)
                return total + jnp.sum(p, 0, keepdims=True)

            total = lax.fori_loop(0, pieces, weigh, jnp.zeros((1, seq), F32))
            lse_ref[0, j : j + 1] = m + jnp.log(total)
            at = j * HD
            ot_ref[0, at : at + HD] = dot(vt_ref[0, at : at + HD], p_scr[...]) / total

        mixed = ot_ref[0].T.astype(BF)
        mix_ref[0] = mixed
        acc_scr[...] += project_out(mixed, w_scr, hw)

        @pl.when(t == count - 1)
        def _():
            second = acc_scr[...]
            second_ref[...] = second
            unit, _ = layer_norm_parts(second)
            n3_ref[...] = (unit * prm_ref[2:3] + prm_ref[6:7]).astype(BF)

    full = whole((seq, width))
    hb = sds((blocks, seq, hw), BF)

    def block(shape):
        return at_block(shape, start)

    packs = pack_at(pack, start)
    return call(
        body, "cross_forward", count,
        [(n2, full), (first, full), *packs, (params, whole(params.shape)), (head_bias, block(head_bias.shape)),
         (keys, block(keys.shape)), (values_t, block(values_t.shape))],
        [(hb, block(hb.shape)), (sds((blocks, 8, seq), F32), block((blocks, 8, seq))),
         (sds((blocks, hw, seq), F32), block((blocks, hw, seq))), (hb, block(hb.shape)),
         (sds((seq, width), F32), full), (sds((seq, width), BF), full)],
        [pltpu.VMEM((pieces, piece, seq), F32), pltpu.VMEM((total_keys, seq), BF),
         pltpu.VMEM((seq, width), F32), pack_scratch(width)],
        count * (4 * seq * width * hw + 4 * seq * total_keys * 256 * heads),
        (place,),
        deps,
        carried,
    )


def feed_forward(place, n3, second, w_in, w_out, own, params, cotangent, dims, deps=()):
    seq, width, blocks, hw = dims

    def body(place_ref, n3_ref, second_ref, *refs):
        wi_refs, wo_refs, refs = refs[: len(w_in)], refs[len(w_in) : 2 * len(w_in)], refs[2 * len(w_in) :]
        (prm_ref, cot_ref, hid_ref, slope_ref, out_ref, g3_ref, b3_ref, sum_ref, wi_scr, wo_scr,
         acc_scr) = refs
        t = pl.program_id(0)
        assemble(wi_refs, own, place_ref, wi_scr)
        assemble(wo_refs, own, place_ref, wo_scr)

        @pl.when(t == 0)
        def _():
            acc_scr[...] = second_ref[...] + prm_ref[14:15]

        before = dot(n3_ref[...], wi_scr[...]) + prm_ref[pl.ds(15 + t, 1)]
        phi = 0.5 + 0.5 * lax.erf(before * 2**-0.5)
        hidden = (before * phi).astype(BF)
        hid_ref[0] = hidden
        slope_ref[0] = phi + before * (jnp.exp(-0.5 * before * before) * 0.3989422804014327)
        acc_scr[...] += dot(hidden, wo_scr[...], 1, 1)

        @pl.when(t == blocks - 1)
        def _():
            unit, inverse = layer_norm_parts(acc_scr[...])
            out_ref[...] = (unit * prm_ref[3:4] + prm_ref[7:8]).astype(BF)
            cot = cot_ref[...].astype(F32)
            grad = norm_back(cot, unit, inverse, prm_ref[3:4])
            g3_ref[...] = grad
            branch = grad.astype(BF)
            b3_ref[...] = branch
            sum_ref[...] = jnp.zeros_like(sum_ref)
            sum_ref[3:4] = column_sum(cot * unit)
            sum_ref[7:8] = column_sum(cot)
            sum_ref[14:15] = column_sum(branch.astype(F32))

    full = whole((seq, width))
    wide = (blocks, seq, width)
    return call(
        body, "feed_forward", blocks,
        [(n3, full), (second, full), *pack_in(w_in), *pack_in(w_out),
         (params, whole(params.shape)), (cotangent, full)],
        [(sds(wide, BF), per_block(wide)), (sds(wide, F32), per_block(wide)),
         (sds((seq, width), BF), full), (sds((seq, width), F32), full),
         (sds((seq, width), BF), full), (sds(params.shape, F32), whole(params.shape))],
        [pack_scratch(width), pack_scratch(width), pltpu.VMEM((seq, width), F32)],
        16 * seq * width * width,
        (place,),
        deps,
    )


def feed_out_grads(place, b3, hidden, grad_shape, dims, deps=()):
    seq, width, blocks, hw = dims

    def body(place_ref, b3_ref, hid_ref, *refs):
        grad_refs, (b3t_scr,) = refs[:-1], refs[-1:]

        @pl.when(pl.program_id(0) == 0)
        def _():
            b3t_scr[...] = b3_ref[...].T

        store_pack(grad_refs, dot(b3t_scr[...], hid_ref[0]).astype(BF), place_ref)

    wide = (blocks, seq, width)
    return call(
        body, "feed_out_grads", blocks,
        [(b3, whole((seq, width))), (hidden, per_block(wide))],
        grad_outs(grad_shape),
        [pltpu.VMEM((width, seq), BF)],
        8 * seq * width * width,
        (place,),
        deps,
    )


def feed_backward(place, b3, g3, slope, w_in, w_out, own, n3, second, params, sums, grad_shape, dims, deps=()):
    seq, width, blocks, hw = dims
    grads = grad_outs(grad_shape)

    def body(place_ref, b3_ref, g3_ref, slope_ref, *refs):
        wi_refs, wo_refs, refs = refs[: len(w_in)], refs[len(w_in) : 2 * len(w_in)], refs[2 * len(w_in) :]
        (n3_ref, second_ref, prm_ref, old_ref), refs = refs[:4], refs[4:]
        grad_refs, refs = refs[: len(grads)], refs[len(grads) :]
        g2_ref, b2_ref, sum_ref, wi_scr, wo_scr, n3t_scr, acc_scr = refs
        t = pl.program_id(0)
        assemble(wi_refs, own, place_ref, wi_scr)
        assemble(wo_refs, own, place_ref, wo_scr)

        @pl.when(t == 0)
        def _():
            sum_ref[...] = old_ref[...]
            n3t_scr[...] = n3_ref[...].T
            acc_scr[...] = jnp.zeros_like(acc_scr)

        grad_before = (dot(b3_ref[...], wo_scr[...]) * slope_ref[0]).astype(BF)
        sum_ref[pl.ds(15 + t, 1)] = column_sum(grad_before.astype(F32))
        store_pack(grad_refs, dot(n3t_scr[...], grad_before).astype(BF), place_ref)
        acc_scr[...] += dot(grad_before, wi_scr[...], 1, 1)

        @pl.when(t == blocks - 1)
        def _():
            grad = acc_scr[...]
            unit, inverse = layer_norm_parts(second_ref[...])
            sum_ref[2:3] = column_sum(grad * unit)
            sum_ref[6:7] = column_sum(grad)
            grad_second = g3_ref[...] + norm_back(grad, unit, inverse, prm_ref[2:3])
            g2_ref[...] = grad_second
            branch = grad_second.astype(BF)
            b2_ref[...] = branch
            sum_ref[13:14] = column_sum(branch.astype(F32))

    full = whole((seq, width))
    wide = (blocks, seq, width)
    return call(
        body, "feed_backward", blocks,
        [(b3, full), (g3, full), (slope, per_block(wide)), *pack_in(w_in), *pack_in(w_out), (n3, full),
         (second, full), (params, whole(params.shape)), (sums, whole(sums.shape))],
        grads
        + [(sds((seq, width), F32), full), (sds((seq, width), BF), full),
           (sds(sums.shape, F32), whole(sums.shape))],
        [pack_scratch(width), pack_scratch(width), pltpu.VMEM((width, seq), BF), pltpu.VMEM((seq, width), F32)],
        24 * seq * width * width,
        (place,),
        deps,
    )


def cross_attend_back(place, start, count, sums, b2, queries, keys, values, keys_t, lse, ot, pack, own, valid,
                      dims, deps=(), carried=()):
    seq, width, blocks, hw = dims
    heads = hw // HD
    _, pieces, piece, _ = keys.shape
    total_keys = pieces * piece

    def body(place_ref, old_ref, b2_ref, q_ref, k_ref, v_ref, kt_ref, lse_ref, ot_ref, *refs):
        w_refs, refs = refs[: len(pack)], refs[len(pack) :]
        dq_ref, dkv_ref, sum_ref, w_scr, dk_scr, dv_scr, ds_scr, dqt_scr = refs
        t = pl.program_id(0)
        assemble(w_refs, own, place_ref, w_scr)

        @pl.when(t == 0)
        def _():
            sum_ref[...] = old_ref[...]

        q = q_ref[0]
        gm = project_back(b2_ref[...], w_scr, hw).astype(BF)
        weighted = gm.astype(F32).T * ot_ref[0]
        row = lax.broadcasted_iota(jnp.int32, (piece, 1), 0)
        pad = jnp.where(row < valid, 0.0, NEGATIVE)
        dk_scr[...] = jnp.zeros_like(dk_scr)
        dv_scr[...] = jnp.zeros_like(dv_scr)
        for j in range(heads):
            delta = jnp.sum(weighted[j * HD : (j + 1) * HD], 0, keepdims=True)
            shift = lse_ref[0, j : j + 1]
            qm = head_lanes(q, j, HD)
            gj = head_lanes(gm, j, HD)

            def one_piece(c, carry):
                s = dot(k_ref[0, c], qm, 1, 1) + pad
                p = jnp.exp(s - shift)
                ds = (p * (dot(v_ref[0, c], gj, 1, 1) - delta)).astype(BF)
                dv_scr[c] += dot(p.astype(BF), gj)
                dk_scr[c] += dot(ds, qm)
                ds_scr[pl.ds(pl.multiple_of(c * piece, piece), piece)] = ds
                return carry

            lax.fori_loop(0, pieces, one_piece, 0)
            dqt_scr[j * HD : (j + 1) * HD] = dot(kt_ref[0, j * HD : (j + 1) * HD], ds_scr[...])
        dq = dqt_scr[...].T.astype(BF).astype(F32) * HD**-0.5
        put_heads(sum_ref, 11, start + t, blocks, column_sum(dq))
        dq_ref[0] = dq.astype(BF)
        bias = jnp.zeros((1, hw), F32)
        for c in range(pieces):
            dv = dv_scr[c].astype(BF)
            bias += column_sum(dv.astype(F32))
            dkv_ref[0, c] = jnp.concatenate([dk_scr[c].astype(BF), dv], 1)
        put_heads(sum_ref, 12, start + t, blocks, bias)

    def block(shape):
        return at_block(shape, start)

    packs = pack_at(pack, start)
    dkv = (blocks, pieces, piece, 2 * hw)
    return call(
        body, "cross_attend_back", count,
        [(sums, whole(sums.shape)), (b2, whole((seq, width))), (queries, block(queries.shape)), (keys, block(keys.shape)),
         (values, block(values.shape)), (keys_t, block(keys_t.shape)), (lse, block(lse.shape)),
         (ot, block(ot.shape)), *packs],
        [(sds(queries.shape, BF), block(queries.shape)), (sds(dkv, BF), block(dkv)),
         (sds(sums.shape, F32), whole(sums.shape))],
        [pack_scratch(width), pltpu.VMEM((pieces, piece, hw), F32), pltpu.VMEM((pieces, piece, hw), F32),
         pltpu.VMEM((total_keys, seq), BF), pltpu.VMEM((hw, seq), F32)],
        count * (2 * seq * width * hw + 10 * seq * total_keys * 256 * heads // 2),
        (place,),
        deps,
        carried,
    )


def cross_rows_back(place, sums, dq, dkv, g2, first, pack, own, params, valid, dims, deps=()):
    seq, width, blocks, hw = dims
    _, pieces, piece, _ = dkv.shape
    frames = (pieces, piece, width)
    kept = (pieces, valid, width)

    def body(place_ref, old_ref, dq_ref, dkv_ref, g2_ref, first_ref, *refs):
        w_refs, refs = refs[: len(pack)], refs[len(pack) :]
        prm_ref, genc_ref, g1_ref, b1_ref, sum_ref, w_scr, genc_scr, acc_scr = refs
        t = pl.program_id(0)
        assemble(w_refs, own, place_ref, w_scr)

        @pl.when(t == 0)
        def _():
            acc_scr[...] = jnp.zeros_like(acc_scr)
            genc_scr[...] = jnp.zeros_like(genc_scr)
            sum_ref[...] = old_ref[...]

        wkv = w_scr[:, : 2 * hw]
        for c in range(pieces):
            genc_scr[c] += dot(dkv_ref[0, c], wkv, 1, 1)
        acc_scr[...] += dot(dq_ref[0], w_scr[:, 2 * hw : 3 * hw], 1, 1)

        @pl.when(t == blocks - 1)
        def _():
            genc_ref[...] = genc_scr[:, :valid].astype(BF)
            grad = acc_scr[...]
            unit, inverse = layer_norm_parts(first_ref[...])
            sum_ref[1:2] = column_sum(grad * unit)
            sum_ref[5:6] = column_sum(grad)
            grad_first = g2_ref[...] + norm_back(grad, unit, inverse, prm_ref[1:2])
            g1_ref[...] = grad_first
            branch = grad_first.astype(BF)
            b1_ref[...] = branch
            sum_ref[10:11] = column_sum(branch.astype(F32))

    full = whole((seq, width))
    return call(
        body, "cross_rows_back", blocks,
        [(sums, whole(sums.shape)), (dq, per_block(dq.shape)), (dkv, per_block(dkv.shape)), (g2, full), (first, full), *pack_in(pack),
         (params, whole(params.shape))],
        [(sds(kept, BF), whole(kept)), (sds((seq, width), F32), full), (sds((seq, width), BF), full),
         (sds(sums.shape, F32), whole(sums.shape))],
        [pack_scratch(width), pltpu.VMEM(frames, F32), pltpu.VMEM((seq, width), F32)],
        2 * seq * width * width + 4 * pieces * piece * width * width,
        (place,),
        deps,
    )


def cross_grads(place, dq, dkv, mixed, b2, n2, frames, grad_shape, dims, deps=()):
    seq, width, blocks, hw = dims
    _, pieces, piece, _ = dkv.shape
    total_keys = pieces * piece

    def body(place_ref, dq_ref, dkv_ref, mix_ref, b2_ref, n2_ref, e_ref, *refs):
        grad_refs, (et_scr, b2t_scr, n2t_scr) = refs[:-3], refs[-3:]

        @pl.when(pl.program_id(0) == 0)
        def _():
            for c in range(pieces):
                et_scr[:, c * piece : (c + 1) * piece] = e_ref[c].T
            b2t_scr[...] = b2_ref[...].T
            n2t_scr[...] = n2_ref[...].T

        grad_kv = dot(et_scr[...], dkv_ref[0].reshape(total_keys, 2 * hw))
        grad_q = dot(n2t_scr[...], dq_ref[0])
        grad_o = dot(b2t_scr[...], mix_ref[0])
        store_pack(grad_refs, jnp.concatenate([grad_kv, grad_q, grad_o], 1).astype(BF), place_ref)

    full = whole((seq, width))
    return call(
        body, "cross_grads", blocks,
        [(dq, per_block(dq.shape)), (dkv, per_block(dkv.shape)), (mixed, per_block(mixed.shape)), (b2, full),
         (n2, full), (frames, whole(frames.shape))],
        grad_outs(grad_shape),
        [pltpu.VMEM((width, total_keys), BF), pltpu.VMEM((width, seq), BF), pltpu.VMEM((width, seq), BF)],
        4 * seq * width * width + 4 * total_keys * width * width,
        (place,),
        deps,
    )


def self_attend_back(length, place, sums, b1, queries, keys, values, lse, ot, pack, own, dims, deps=()):
    seq, width, blocks, hw = dims
    heads = hw // HD

    def body(len_ref, place_ref, old_ref, b1_ref, q_ref, k_ref, v_ref, lse_ref, ot_ref, *refs):
        w_refs, refs = refs[: len(pack)], refs[len(pack) :]
        dqkv_ref, sum_ref, w_scr, bias_scr, dqt_scr = refs
        t = pl.program_id(0)
        assemble(w_refs, own, place_ref, w_scr)

        @pl.when(t == 0)
        def _():
            sum_ref[...] = old_ref[...]
            key = lax.broadcasted_iota(jnp.int32, (seq, seq), 0)
            query = lax.broadcasted_iota(jnp.int32, (seq, seq), 1)
            bias_scr[...] = jnp.where((key <= query) & (key < len_ref[0]), 0.0, NEGATIVE)

        q = q_ref[0]
        k = k_ref[0]
        v = v_ref[0]
        kt = k.T
        gm = project_back(b1_ref[...], w_scr, hw).astype(BF)
        weighted = gm.astype(F32).T * ot_ref[0]
        dk = jnp.zeros((seq, hw), F32)
        dv = jnp.zeros((seq, hw), F32)
        for j in range(heads):
            delta = jnp.sum(weighted[j * HD : (j + 1) * HD], 0, keepdims=True)
            qm = head_lanes(q, j, HD)
            gj = head_lanes(gm, j, HD)
            p = jnp.exp(dot(k, qm, 1, 1) + bias_scr[...] - lse_ref[0, j : j + 1])
            ds = (p * (dot(v, gj, 1, 1) - delta)).astype(BF)
            dv += dot(p.astype(BF), gj)
            dk += dot(ds, qm)
            dqt_scr[j * HD : (j + 1) * HD] = dot(kt[j * HD : (j + 1) * HD], ds)
        dq = dqt_scr[...].T.astype(BF).astype(F32) * HD**-0.5
        dv = dv.astype(BF)
        put_heads(sum_ref, 8, t, blocks, column_sum(dq))
        put_heads(sum_ref, 9, t, blocks, column_sum(dv.astype(F32)))
        dqkv_ref[0] = jnp.concatenate([dq.astype(BF), dk.astype(BF), dv], 1)

    hb = per_block((blocks, seq, hw))
    dqkv = (blocks, seq, 3 * hw)
    return call(
        body, "self_attend_back", blocks,
        [(sums, whole(sums.shape)), (b1, whole((seq, width))), (queries, hb), (keys, hb), (values, hb), (lse, per_block(lse.shape)),
         (ot, per_block(ot.shape)), *pack_in(pack)],
        [(sds(dqkv, BF), per_block(dqkv)), (sds(sums.shape, F32), whole(sums.shape))],
        [pack_scratch(width), pltpu.VMEM((seq, seq), F32), pltpu.VMEM((hw, seq), F32)],
        2 * seq * width * width + 40 * seq * seq * width,
        (length, place),
        deps,
    )


def self_grads(place, dqkv, mixed, b1, n1, grad_shape, dims, deps=()):
    seq, width, blocks, hw = dims

    def body(place_ref, dqkv_ref, mix_ref, b1_ref, n1_ref, *refs):
        grad_refs, (b1t_scr, n1t_scr) = refs[:-2], refs[-2:]

        @pl.when(pl.program_id(0) == 0)
        def _():
            b1t_scr[...] = b1_ref[...].T
            n1t_scr[...] = n1_ref[...].T

        grad_qkv = dot(n1t_scr[...], dqkv_ref[0])
        grad_o = dot(b1t_scr[...], mix_ref[0])
        store_pack(grad_refs, jnp.concatenate([grad_qkv, grad_o], 1).astype(BF), place_ref)

    full = whole((seq, width))
    return call(
        body, "self_grads", blocks,
        [(dqkv, per_block(dqkv.shape)), (mixed, per_block(mixed.shape)), (b1, full), (n1, full)],
        grad_outs(grad_shape),
        [pltpu.VMEM((width, seq), BF), pltpu.VMEM((width, seq), BF)],
        8 * seq * width * width,
        (place,),
        deps,
    )


def self_rows_back(place, sums, dqkv, g1, rows, pack, own, params, dims, deps=()):
    seq, width, blocks, hw = dims

    def body(place_ref, old_ref, dqkv_ref, g1_ref, x_ref, *refs):
        w_refs, refs = refs[: len(pack)], refs[len(pack) :]
        prm_ref, gin_ref, sum_ref, w_scr, acc_scr = refs
        t = pl.program_id(0)
        assemble(w_refs, own, place_ref, w_scr)

        @pl.when(t == 0)
        def _():
            acc_scr[...] = jnp.zeros_like(acc_scr)
            sum_ref[...] = old_ref[...]

        acc_scr[...] += dot(dqkv_ref[0], w_scr[:, : 3 * hw], 1, 1)

        @pl.when(t == blocks - 1)
        def _():
            grad = acc_scr[...]
            unit, inverse = layer_norm_parts(x_ref[...].astype(F32))
            sum_ref[0:1] = column_sum(grad * unit)
            sum_ref[4:5] = column_sum(grad)
            gin_ref[...] = g1_ref[...] + norm_back(grad, unit, inverse, prm_ref[0:1])

    full = whole((seq, width))
    return call(
        body, "self_rows_back", blocks,
        [(sums, whole(sums.shape)), (dqkv, per_block(dqkv.shape)), (g1, full), (rows, full), *pack_in(pack), (params, whole(params.shape))],
        [(sds((seq, width), F32), full), (sds(sums.shape, F32), whole(sums.shape))],
        [pack_scratch(width), pltpu.VMEM((seq, width), F32)],
        6 * seq * width * width,
        (place,),
        deps,
    )


def pad_rows(rows, count):
    return jnp.pad(rows, ((0, count - rows.shape[0]),) + ((0, 0),) * (rows.ndim - 1))


def swap(array, step):
    count = lax.axis_size("fsdp")
    return lax.ppermute(array, "fsdp", [(i, i ^ step) for i in range(count)])


def around(array, hop):
    count = lax.axis_size("tp")
    return lax.ppermute(array, "tp", [(i, (i + hop) % count) for i in range(count)])


def native_gather(shard):
    whole_pack = lax.all_gather(shard, ("fsdp", "tp"), axis=0, tiled=False)
    return whole_pack.reshape((lax.axis_size("fsdp"), lax.axis_size("tp")) + shard.shape)


def in_order(pieces, here):
    count = len(pieces)
    stacked = jnp.stack(pieces)
    return jnp.stack(
        [lax.dynamic_index_in_dim(stacked, (here - t) % count, 0, keepdims=False) for t in range(count)]
    )


def gate(array, things):
    return lax.optimization_barrier((array,) + tuple(things))[0] if things else array


class Gather:
    def __init__(self, shard):
        self.shard = shard
        self.here = lax.axis_index("tp")

    def after(self, names, things):
        for name in names.split():
            setattr(self, name, gate(getattr(self, name), things))

    def direct(self):
        self.line = in_order([self.shard] + [around(self.shard, hop) for hop in range(1, 4)], self.here)
        return (self.line,)

    def pair(self):
        self.come = lax.ppermute(self.shard, "tp", [(i, i ^ 1) for i in range(4)])
        return (self.come,)

    def middle(self):
        odd = self.here % 2 == 1
        first, last = jnp.where(odd, self.come, self.shard), jnp.where(odd, self.shard, self.come)
        self.near = jnp.stack([first, last])
        self.inner = lax.ppermute(self.near, "tp", [(1, 2), (2, 1)])
        return (self.inner,)

    def ends(self):
        outer = lax.ppermute(self.inner, "tp", [(1, 0), (2, 3)])
        far = jnp.where((self.here == 1) | (self.here == 2), self.inner, outer)
        upper = self.here >= 2
        self.line = jnp.concatenate([jnp.where(upper, far, self.near), jnp.where(upper, self.near, far)])
        return (outer,)

    def first(self):
        self.low, self.high = self.line[None, :2], self.line[None, 2:]
        self.low_x, self.high_y = swap(self.low, 2), swap(self.high, 4)
        return self.low_x, self.high_y

    def second(self):
        low = jnp.concatenate([self.low, self.low_x])
        high = jnp.concatenate([self.high, self.high_y])
        low_y, high_x = swap(low, 4), swap(high, 2)
        low = jnp.concatenate([low, low_y])
        high = jnp.stack([high[0], high_x[0], high[1], high_x[1]])
        self.mine = jnp.concatenate([low, high], 1)
        return low_y, high_x

    def core(self):
        self.pack = (self.mine, swap(self.mine, 1))
        return self.pack


def wide(array):
    return array.astype(F32)


class Scatter:
    def __init__(self, halves):
        self.kept, self.sent = halves
        self.tp = self.kept.shape[1]
        self.half = self.tp // 2

    def core(self):
        self.come = swap(self.sent, 1)
        return self.come

    def first(self):
        def both(q, t):
            return (wide(self.kept[q, t]) + wide(self.come[q, t])).astype(BF)

        low, high = slice(0, self.half), slice(self.half, self.tp)
        self.low_y = swap(both(slice(2, 4), low), 4)
        self.high_x = swap(both(slice(1, 4, 2), high), 2)
        return self.low_y, self.high_x

    def second(self):
        low, high = slice(0, self.half), slice(self.half, self.tp)

        def three(q, t, more):
            return wide(self.kept[q, t]) + wide(self.come[q, t]) + wide(more)

        self.low_x = swap(three(1, low, self.low_y[1]).astype(BF), 2)
        self.high_y = swap(three(2, high, self.high_x[1]).astype(BF), 4)
        return self.low_x, self.high_y

    def line(self):
        def total(t, more, last):
            return wide(self.kept[0, t]) + wide(self.come[0, t]) + wide(more) + wide(last)

        low, high = slice(0, self.half), slice(self.half, self.tp)
        sums = jnp.concatenate(
            [total(low, self.low_y[0], self.low_x), total(high, self.high_x[0], self.high_y)]
        ).astype(BF)
        here = lax.axis_index("tp")
        self.own = lax.dynamic_index_in_dim(sums, here, 0, keepdims=False)
        self.parts = [
            around(lax.dynamic_index_in_dim(sums, (here + hop) % self.tp, 0, keepdims=False), hop)
            for hop in range(1, self.tp)
        ]
        return tuple(self.parts)

    def total(self):
        result = wide(self.own)
        for part in self.parts:
            result += wide(part)
        return result


def butterfly_scatter(grads, own, narrow=BF):
    fsdp, tp = lax.axis_size("fsdp"), lax.axis_size("tp")
    if grads.shape[0] != fsdp:
        blocks, width = grads.shape[1], grads.shape[3]
        grads = grads.reshape(blocks, fsdp, own, width).transpose(1, 0, 2, 3)
    place = lax.axis_index("fsdp")
    step = 1
    while step < fsdp:
        pairs = grads.reshape((grads.shape[0] // 2, 2) + grads.shape[1:])
        bit = (place // step) % 2
        kept = lax.dynamic_index_in_dim(pairs, bit, 1, keepdims=False)
        sent = lax.dynamic_index_in_dim(pairs, 1 - bit, 1, keepdims=False)
        grads = (wide(kept) + wide(swap(sent, step))).astype(narrow)
        step *= 2
    grads = grads[0]
    here = lax.axis_index("tp")
    total = wide(lax.dynamic_index_in_dim(grads, here, 0, keepdims=False))
    for hop in range(1, tp):
        sent = lax.dynamic_index_in_dim(grads, (here + hop) % tp, 0, keepdims=False)
        total += wide(around(sent, hop))
    return total


def local(
    inputs,
    encoder,
    lengths,
    self_qkv,
    self_out,
    cross_q,
    cross_kv,
    cross_out,
    fc_in,
    fc_out,
    norm_gain,
    norm_bias,
    proj_bias,
    fc_in_bias,
    cotangent,
):
    fsdp, tp = lax.axis_size("fsdp"), lax.axis_size("tp")
    devices = fsdp * tp
    tp_place = lax.axis_index("tp")
    place = lax.axis_index("fsdp").reshape(1)
    seqs, seq, width = inputs.shape
    assert seqs == 1
    own, hw = cross_q.shape
    dims = (seq, width, tp, hw)
    frames_own = encoder.shape[1]
    small_own = norm_gain.shape[1]
    ff_own = fc_in_bias.shape[0]
    chained = fsdp == 8 and tp == 4 and own % 16 == 0

    small = jnp.concatenate(
        [a.reshape(-1) for a in (norm_gain, norm_bias, proj_bias, fc_in_bias)]
    )
    small = jnp.pad(small, (0, width - small.size))
    high = small.astype(BF)
    low = (small - high.astype(F32)).astype(BF)
    extra = pad_rows(jnp.stack([high, low]), 16)

    pack_self = jnp.concatenate([self_qkv[0], self_qkv[1], self_qkv[2], self_out.T], 1)
    pack_self = jnp.concatenate([pack_self, extra], 0)
    pack_cross = jnp.concatenate([cross_kv[0], cross_kv[1], cross_q, cross_out.T], 1)
    x = inputs[0]
    length = lax.dynamic_slice_in_dim(lengths, tp_place, 1)
    chains = {}
    sends = {"direct": "shard", "pair": "shard", "middle": "come", "ends": "inner", "first": "line",
             "second": "low_x high_y", "core": "mine"}

    def move(after, *steps):
        if not chained:
            return ()
        out = ()
        for text in steps:
            name, step = text.split(".")
            if step != "core":
                chains[name].after(sends[step], after)
            else:
                chains[name].mine = gate(chains[name].mine, after)
            out += tuple(getattr(chains[name], step)())
        return out

    frames = encoder
    if chained:
        for name, shard in (("self", pack_self), ("cross", pack_cross), ("in", fc_in), ("out", fc_out.T)):
            chains[name] = Gather(shard)
        moved = move((), "self.direct")
        side = move((), "cross.pair")
        frames = gate(frames, moved)
        more = move(moved, "self.first")
        side = move(moved + side, "cross.middle")
        moved = move(more, "self.second")
        side = move(more + side, "cross.ends", "in.pair")
        more = move(moved, "self.core")
        moved = move(moved + side, "cross.first", "in.middle", "out.pair") + more[1:]
        w_self = chains["self"].pack
        own_rows = own
        grad_shape = (fsdp // 2, tp, own, width)
        blocks = jnp.stack([part[:, :, own : own + 2] for part in w_self], 1)
        blocks = blocks.reshape(fsdp, tp, 2, width)
        table = jnp.stack(
            [lax.dynamic_index_in_dim(blocks, f ^ place[0], 0, keepdims=False) for f in range(fsdp)]
        )
        table = wide(table).sum(2).reshape(devices, width)
    else:
        moved = ()
        more = ()
        w_self = native_gather(pack_self)
        table = wide(w_self[:, :, own : own + 2]).sum(2).reshape(devices, width)
        own_rows = own * fsdp
        grad_shape = (1, tp, own_rows, width)

        def end_to_end(pack):
            return pack[:, :, :own].transpose(1, 0, 2, 3).reshape(1, tp, own_rows, width)

        w_self = (end_to_end(w_self),)
        w_cross = (end_to_end(native_gather(pack_cross)),)
        w_in = (end_to_end(native_gather(fc_in)),)
        w_out = (end_to_end(native_gather(fc_out.T)),)

    rows = norm_gain.shape[0] + norm_bias.shape[0] + proj_bias.shape[0]
    params = table[:, : rows * small_own].reshape(devices, rows, small_own)
    params = params.transpose(1, 0, 2).reshape(rows, width)
    fc_bias = table[:, rows * small_own : rows * small_own + ff_own].reshape(tp, width)
    head_bias = jnp.stack([params[8], params[9], params[11], params[12]])
    head_bias = head_bias.reshape(4, tp, hw).transpose(1, 0, 2)
    head_bias = jnp.pad(head_bias, ((0, 0), (0, 4), (0, 0)))
    params = pad_rows(jnp.concatenate([params, fc_bias], 0), 24)

    piece = -(-frames_own // 128) * 128
    frames = lax.all_to_all(frames, "tp", 0, 0, tiled=True)
    frames = jnp.pad(frames, ((0, 0), (0, piece - frames_own), (0, 0)))
    half = tp // 2

    later = move(moved, "cross.second", "in.ends", "out.middle")
    shared = (w_self, own_rows, params, head_bias, dims)
    *kept, part, _ = self_forward(length, place, 0, half, x, x, *shared, moved)
    moved = move(later + (part,), "cross.core", "in.first", "out.ends")
    q1, k1, v1, lse1, ot1, mixed1, n1, first, n2 = self_forward(
        length, place, half, tp - half, x, part, *shared, later, kept[:-1]
    )
    if chained:
        w_cross = chains["cross"].pack
    later = move(moved + (n2,), "in.second", "out.first")
    k2, v2, k2t, v2t = frame_keys(place, frames, w_cross, own_rows, head_bias, dims, (n2,) + moved)
    moved = move(later + (k2,), "in.core", "out.second")
    shared = (w_cross, own_rows, params, head_bias, k2, v2t, frames_own, dims)
    *kept, part, _ = cross_forward(place, 0, half, n2, first, *shared, later)
    later = move(moved + (part,), "out.core")
    q2, lse2, ot2, mixed2, second, n3 = cross_forward(
        place, half, tp - half, n2, part, *shared, moved, kept
    )
    if chained:
        w_in, w_out = chains["in"].pack, chains["out"].pack
    hidden, slope, layer_out, g3, b3, sums = feed_forward(
        place, n3, second, w_in, w_out, own_rows, params, cotangent[0], dims
    )
    scatters = {}

    def begin(name, halves):
        if chained:
            scatters[name] = Scatter(halves)

    def go(name, step):
        if not chained:
            return ()
        out = getattr(scatters[name], step)()
        return out if isinstance(out, tuple) else (out,)

    grad_out = feed_out_grads(place, b3, hidden, grad_shape, dims)
    begin("out", grad_out)
    step1 = go("out", "core")
    *grad_in, g2, b2, sums = feed_backward(
        place, b3, g3, slope, w_in, w_out, own_rows, n3, second, params, sums, grad_shape, dims, (grad_out[0],)
    )
    begin("in", grad_in)
    step2 = go("out", "first") + go("in", "core")
    shared = (b2, q2, k2, v2, k2t, lse2, ot2, w_cross, own_rows, frames_own, dims)
    *kept, sums = cross_attend_back(place, 0, half, sums, *shared, step1)
    step3 = go("out", "second") + go("in", "first")
    dq2, dkv2, sums = cross_attend_back(place, half, tp - half, sums, *shared, step2, kept)
    step4 = go("out", "line") + go("in", "second")
    grad_frames, g1, b1, sums = cross_rows_back(
        place, sums, dq2, dkv2, g2, first, w_cross, own_rows, params, frames_own, dims, step3
    )
    step5 = go("in", "line")
    grad_cross = cross_grads(place, dq2, dkv2, mixed2, b2, n2, frames, grad_shape, dims, step4 + (b1,))
    begin("cross", grad_cross)
    frames_back = lax.all_to_all(gate(grad_frames, (grad_cross[0],)), "tp", 0, 0, tiled=True)
    step6 = go("cross", "core")
    dqkv1, sums = self_attend_back(
        length, place, sums, b1, q1, k1, v1, lse1, ot1, w_self, own_rows, dims, step5 + (grad_cross[0],)
    )
    step7 = go("cross", "first")
    grad_self = self_grads(place, dqkv1, mixed1, b1, n1, grad_shape, dims, step6)
    begin("self", grad_self)
    go("self", "core")
    grad_inputs, sums = self_rows_back(
        place, sums, dqkv1, g1, x, w_self, own_rows, params, dims, step7 + (grad_self[0],)
    )
    go("cross", "second")

    for step in range(max(fsdp, tp)):
        if 2**step < fsdp:
            sums = sums + swap(sums, 2**step)
        if 2**step < tp:
            sums = sums + lax.ppermute(sums, "tp", [(i, i ^ 2**step) for i in range(tp)])
    device = lax.axis_index("fsdp") * tp + tp_place
    mine = lax.dynamic_slice_in_dim(sums[:rows], device * small_own, small_own, 1)
    gains = norm_gain.shape[0]
    own_gain, own_shift, own_bias = mine[:gains], mine[gains : 2 * gains], mine[2 * gains :]
    per_row = width // ff_own
    own_fc_bias = lax.dynamic_slice(
        sums, (rows + device // per_row, (device % per_row) * ff_own), (1, ff_own)
    )[0]

    if chained:
        go("self", "first")
        go("cross", "line")
        go("self", "second")
        go("self", "line")
        total_out, total_in, total_cross, total_self = (
            scatters[name].total() for name in ("out", "in", "cross", "self")
        )
    else:
        total_out, total_in, total_cross, total_self = (
            butterfly_scatter(grads[0], own) for grads in (grad_out, grad_in, grad_cross, grad_self)
        )

    def part(total, index):
        return total[:, index * hw : (index + 1) * hw]

    return (
        layer_out[None],
        grad_inputs[None],
        frames_back.astype(F32),
        jnp.stack([part(total_self, 0), part(total_self, 1), part(total_self, 2)]),
        part(total_self, 3).T,
        part(total_cross, 2),
        jnp.stack([part(total_cross, 0), part(total_cross, 1)]),
        part(total_cross, 3).T,
        total_in,
        total_out.T,
        own_gain,
        own_shift,
        own_bias,
        own_fc_bias,
    )


def solution(mesh):
    return jax.shard_map(
        local,
        mesh=mesh,
        in_specs=(
            P(("fsdp", "tp"), None, None),
            P("fsdp", "tp", None),
            P("fsdp"),
            P(None, "fsdp", "tp"),
            P("tp", "fsdp"),
            P("fsdp", "tp"),
            P(None, "fsdp", "tp"),
            P("tp", "fsdp"),
            P("fsdp", "tp"),
            P("tp", "fsdp"),
            P(None, ("fsdp", "tp")),
            P(None, ("fsdp", "tp")),
            P(None, ("fsdp", "tp")),
            P(("fsdp", "tp")),
            P(("fsdp", "tp"), None, None),
        ),
        out_specs=(
            P(("fsdp", "tp"), None, None),
            P(("fsdp", "tp"), None, None),
            P("fsdp", "tp", None),
            P(None, "fsdp", "tp"),
            P("tp", "fsdp"),
            P("fsdp", "tp"),
            P(None, "fsdp", "tp"),
            P("tp", "fsdp"),
            P("fsdp", "tp"),
            P("tp", "fsdp"),
            P(None, ("fsdp", "tp")),
            P(None, ("fsdp", "tp")),
            P(None, ("fsdp", "tp")),
            P(("fsdp", "tp")),
        ),
        check_vma=False,
    )
```

```python
import functools

import jax
import jax.numpy as jnp
from jax import lax
from jax.experimental import pallas as pl
from jax.experimental.pallas import tpu as pltpu
from jax.sharding import PartitionSpec as P

HD = 64
EPSILON = 1e-05
NEGATIVE = -1e30
VMEM_LIMIT = 60 * 2**20
HINT = 20
BF = jnp.bfloat16
F32 = jnp.float32


def dot(left, right, left_dim=1, right_dim=0):
    return lax.dot_general(
        left, right, (((left_dim,), (right_dim,)), ((), ())), preferred_element_type=F32
    )


def layer_norm_parts(rows):
    center = rows - jnp.mean(rows, -1, keepdims=True)
    inverse = lax.rsqrt(jnp.mean(center * center, -1, keepdims=True) + EPSILON)
    return center * inverse, inverse


def norm_back(grad_rows, unit, inverse, gain):
    scaled = grad_rows * gain
    return inverse * (
        scaled
        - jnp.mean(scaled, -1, keepdims=True)
        - unit * jnp.mean(scaled * unit, -1, keepdims=True)
    )


def put_heads(sum_ref, row, block, count, value):
    size = value.shape[1]
    for t in range(count):

        @pl.when(block == t)
        def _():
            sum_ref[row : row + 1, t * size : (t + 1) * size] = value


def column_sum(rows):
    return jnp.sum(rows, 0, keepdims=True)


def whole(shape):
    zeros = (0,) * len(shape)
    return pl.BlockSpec(shape, lambda t, *_: zeros)


def per_block(shape):
    rest = (0,) * (len(shape) - 1)
    return pl.BlockSpec((1,) + tuple(shape[1:]), lambda t, *_: (t,) + rest)


def packed(shape):
    return pl.BlockSpec((shape[0], 1) + tuple(shape[2:]), lambda t, *_: (0, t, 0, 0))


def sds(shape, dtype):
    return jax.ShapeDtypeStruct(tuple(shape), dtype)


def call(body, name, grid, ins, outs, scratch, flops, scalars=(), deps=(), carried=()):
    moved = sum(a.size * a.dtype.itemsize for a, _ in ins)
    moved += sum(o.size * o.dtype.itemsize for o, _ in outs)
    first = len(scalars) + len(ins)
    extra = list(carried) + list(deps)

    def inner(*refs):
        return body(*refs[:first], *refs[first + len(extra) :])

    return pl.pallas_call(
        inner,
        out_shape=[o for o, _ in outs],
        grid_spec=pltpu.PrefetchScalarGridSpec(
            num_scalar_prefetch=len(scalars),
            grid=(grid,),
            in_specs=[s for _, s in ins] + [pl.BlockSpec(memory_space=pl.ANY)] * len(extra),
            out_specs=[s for _, s in outs],
            scratch_shapes=scratch,
        ),
        compiler_params=pltpu.CompilerParams(
            dimension_semantics=("arbitrary",), vmem_limit_bytes=VMEM_LIMIT
        ),
        input_output_aliases={first + i: i for i in range(len(carried))},
        cost_estimate=pl.CostEstimate(flops=HINT * flops, bytes_accessed=moved, transcendentals=0),
        name=name,
    )(*scalars, *[a for a, _ in ins], *extra)


def head_lanes(rows, head, block):
    lane = lax.broadcasted_iota(jnp.int32, rows.shape, 1)
    return jnp.where((lane >= head * block) & (lane < (head + 1) * block), rows, jnp.zeros_like(rows))


def pack_in(pack):
    return pack_at(pack, 0)


def at_block(shape, start):
    rest = (0,) * (len(shape) - 1)
    return pl.BlockSpec((1,) + tuple(shape[1:]), lambda t, *_: (start + t,) + rest)


def pack_at(pack, start):
    return [
        (a, pl.BlockSpec((a.shape[0], 1) + a.shape[2:], lambda t, *_: (0, start + t, 0, 0))) for a in pack
    ]


def pack_scratch(width):
    return pltpu.VMEM((width, width), BF)


def assemble(refs, rows, place_ref, scr):
    if len(refs) == 1:
        parts = refs[0][:, 0, :rows, :]
        scr[...] = parts.reshape(parts.shape[0] * rows, parts.shape[2])
        return
    count = 2 * refs[0].shape[0]
    for f in range(count):
        distance = f ^ place_ref[0]
        source = distance >> 1
        for bit in range(2):

            @pl.when((distance & 1) == bit)
            def _():
                scr[f * rows : (f + 1) * rows] = refs[bit][source, 0, :rows, :]


def grad_outs(shape):
    return [(sds(shape, BF), packed(shape))] * (1 if shape[0] == 1 else 2)


def store_pack(refs, value, place_ref):
    rows = refs[0].shape[2]
    if len(refs) == 1:
        refs[0][0, 0] = value
        return
    for f in range(2 * refs[0].shape[0]):
        distance = f ^ place_ref[0]
        target = distance >> 1
        for bit in range(2):

            @pl.when((distance & 1) == bit)
            def _():
                refs[bit][target, 0] = value[f * rows : (f + 1) * rows]


def tail_start(hw):
    return (3 * hw) // 128 * 128


def project_out(mixed, w_scr, hw):
    start = tail_start(hw)
    extra = 3 * hw - start
    if extra:
        mixed = jnp.concatenate([jnp.zeros((mixed.shape[0], extra), mixed.dtype), mixed], 1)
    return dot(mixed, w_scr[:, start:], 1, 1)


def project_back(branch, w_scr, hw):
    start = tail_start(hw)
    return dot(branch, w_scr[:, start:])[:, 3 * hw - start :]


def self_forward(length, place, start, count, rows, part, pack, own, params, head_bias, dims, deps=(), carried=()):
    seq, width, blocks, hw = dims
    heads = hw // HD

    def body(len_ref, place_ref, x_ref, part_ref, *refs):
        w_refs, refs = refs[: len(pack)], refs[len(pack) :]
        (prm_ref, hb_ref, q_ref, k_ref, v_ref, lse_ref, ot_ref, mix_ref, n1_ref, first_ref, n2_ref,
         bias_scr, acc_scr, w_scr) = refs
        t = pl.program_id(0)
        assemble(w_refs, own, place_ref, w_scr)

        @pl.when(t == 0)
        def _():
            unit, _ = layer_norm_parts(x_ref[...].astype(F32))
            n1_ref[...] = (unit * prm_ref[0:1] + prm_ref[4:5]).astype(BF)
            key = lax.broadcasted_iota(jnp.int32, (seq, seq), 0)
            query = lax.broadcasted_iota(jnp.int32, (seq, seq), 1)
            bias_scr[...] = jnp.where((key <= query) & (key < len_ref[0]), 0.0, NEGATIVE)
            acc_scr[...] = part_ref[...].astype(F32) + prm_ref[10:11] if start == 0 else part_ref[...]

        qkv = dot(n1_ref[...], w_scr[:, : 3 * hw])
        q = ((qkv[:, :hw] + hb_ref[0, 0:1]) * HD**-0.5).astype(BF)
        k = qkv[:, hw : 2 * hw].astype(BF)
        v = (qkv[:, 2 * hw :] + hb_ref[0, 1:2]).astype(BF)
        q_ref[0] = q
        k_ref[0] = k
        v_ref[0] = v
        vt = v.T
        for j in range(heads):
            s = dot(k, head_lanes(q, j, HD), 1, 1) + bias_scr[...]
            m = jnp.max(s, 0, keepdims=True)
            p = jnp.exp(s - m)
            total = jnp.sum(p, 0, keepdims=True)
            lse_ref[0, j : j + 1] = m + jnp.log(total)
            ot_ref[0, j * HD : (j + 1) * HD] = dot(vt[j * HD : (j + 1) * HD], p.astype(BF)) / total
        mixed = ot_ref[0].T.astype(BF)
        mix_ref[0] = mixed
        acc_scr[...] += project_out(mixed, w_scr, hw)

        @pl.when(t == count - 1)
        def _():
            first = acc_scr[...]
            first_ref[...] = first
            unit, _ = layer_norm_parts(first)
            n2_ref[...] = (unit * prm_ref[1:2] + prm_ref[5:6]).astype(BF)

    full = whole((seq, width))
    hb = sds((blocks, seq, hw), BF)

    def block(shape):
        return at_block(shape, start)

    return call(
        body, "self_forward", count,
        [(rows, full), (part, full), *pack_at(pack, start), (params, whole(params.shape)),
         (head_bias, block(head_bias.shape))],
        [(hb, block(hb.shape))] * 3
        + [(sds((blocks, 8, seq), F32), block((blocks, 8, seq))),
           (sds((blocks, hw, seq), F32), block((blocks, hw, seq))),
           (hb, block(hb.shape)),
           (sds((seq, width), BF), full),
           (sds((seq, width), F32), full),
           (sds((seq, width), BF), full)],
        [pltpu.VMEM((seq, seq), F32), pltpu.VMEM((seq, width), F32), pack_scratch(width)],
        count * (8 * seq * width * hw + 16 * seq * seq * hw),
        (length, place),
        deps,
        carried,
    )


def frame_keys(place, frames, pack, own, head_bias, piece, dims, deps=()):
    seq, width, blocks, hw = dims
    pieces = len(frames)
    valid = sum(part.shape[0] for part in frames[0])
    parts = [part for group in frames for part in group]
    total = pieces * piece
    edge = valid // 16 * 16

    def body(place_ref, *refs):
        f_refs, refs = list(refs[: len(parts)]), refs[len(parts) :]
        w_refs, refs = refs[: len(pack)], refs[len(pack) :]
        hb_ref, k_ref, v_ref, kt_ref, vt_ref, e_ref, w_scr = refs
        assemble(w_refs, own, place_ref, w_scr)

        @pl.when(pl.program_id(0) == 0)
        def _():
            for c in range(pieces):
                e_ref[c, edge:] = jnp.zeros((piece - edge, width), BF)
                at = 0
                for part in frames[c]:
                    e_ref[c, at : at + part.shape[0]] = f_refs.pop(0)[...]
                    at += part.shape[0]

        w = w_scr[:, : 2 * hw]
        for c in range(pieces):
            kv = dot(e_ref[c], w)
            k = kv[:, :hw].astype(BF)
            v = (kv[:, hw:] + hb_ref[0, 3:4]).astype(BF)
            k_ref[0, c] = k
            v_ref[0, c] = v
            kt_ref[0, :, c * piece : (c + 1) * piece] = k.T
            vt_ref[0, :, c * piece : (c + 1) * piece] = v.T

    kv = sds((blocks, pieces, piece, hw), BF)
    kvt = sds((blocks, hw, total), BF)
    padded = sds((pieces, piece, width), BF)
    return call(
        body, "frame_keys", blocks,
        [(part, whole(part.shape)) for part in parts] + [*pack_in(pack), (head_bias, per_block(head_bias.shape))],
        [(kv, per_block(kv.shape))] * 2 + [(kvt, per_block(kvt.shape))] * 2 + [(padded, whole(padded.shape))],
        [pack_scratch(width)],
        4 * total * width * width,
        (place,),
        deps,
    )


def cross_forward(place, start, count, n2, first, pack, own, params, head_bias, keys, values_t, valid, dims, deps=(),
                  carried=()):
    seq, width, blocks, hw = dims
    heads = hw // HD
    _, pieces, piece, _ = keys.shape
    total_keys = pieces * piece

    def body(place_ref, n2_ref, first_ref, *refs):
        w_refs, refs = refs[: len(pack)], refs[len(pack) :]
        (prm_ref, hb_ref, k_ref, vt_ref, q_ref, lse_ref, ot_ref, mix_ref, second_ref, n3_ref, s_scr,
         p_scr, acc_scr, w_scr) = refs
        t = pl.program_id(0)
        assemble(w_refs, own, place_ref, w_scr)

        @pl.when(t == 0)
        def _():
            acc_scr[...] = first_ref[...] + prm_ref[13:14] if start == 0 else first_ref[...]

        q = ((dot(n2_ref[...], w_scr[:, 2 * hw : 3 * hw]) + hb_ref[0, 2:3]) * HD**-0.5).astype(BF)
        q_ref[0] = q
        row = lax.broadcasted_iota(jnp.int32, (piece, 1), 0)
        pad = jnp.where(row < valid, 0.0, NEGATIVE)

        for j in range(heads):
            qm = head_lanes(q, j, HD)

            def score(c, m):
                s = dot(k_ref[0, c], qm, 1, 1) + pad
                s_scr[c] = s
                return jnp.maximum(m, jnp.max(s, 0, keepdims=True))

            m = lax.fori_loop(0, pieces, score, jnp.full((1, seq), NEGATIVE, F32))

            def weigh(c, total):
                p = jnp.exp(s_scr[c] - m)
                p_scr[pl.ds(pl.multiple_of(c * piece, piece), piece)] = p.astype(BF)
                return total + jnp.sum(p, 0, keepdims=True)

            total = lax.fori_loop(0, pieces, weigh, jnp.zeros((1, seq), F32))
            lse_ref[0, j : j + 1] = m + jnp.log(total)
            at = j * HD
            ot_ref[0, at : at + HD] = dot(vt_ref[0, at : at + HD], p_scr[...]) / total

        mixed = ot_ref[0].T.astype(BF)
        mix_ref[0] = mixed
        acc_scr[...] += project_out(mixed, w_scr, hw)

        @pl.when(t == count - 1)
        def _():
            second = acc_scr[...]
            second_ref[...] = second
            unit, _ = layer_norm_parts(second)
            n3_ref[...] = (unit * prm_ref[2:3] + prm_ref[6:7]).astype(BF)

    full = whole((seq, width))
    hb = sds((blocks, seq, hw), BF)

    def block(shape):
        return at_block(shape, start)

    packs = pack_at(pack, start)
    return call(
        body, "cross_forward", count,
        [(n2, full), (first, full), *packs, (params, whole(params.shape)), (head_bias, block(head_bias.shape)),
         (keys, block(keys.shape)), (values_t, block(values_t.shape))],
        [(hb, block(hb.shape)), (sds((blocks, 8, seq), F32), block((blocks, 8, seq))),
         (sds((blocks, hw, seq), F32), block((blocks, hw, seq))), (hb, block(hb.shape)),
         (sds((seq, width), F32), full), (sds((seq, width), BF), full)],
        [pltpu.VMEM((pieces, piece, seq), F32), pltpu.VMEM((total_keys, seq), BF),
         pltpu.VMEM((seq, width), F32), pack_scratch(width)],
        count * (4 * seq * width * hw + 4 * seq * total_keys * 256 * heads),
        (place,),
        deps,
        carried,
    )


def feed_forward(place, n3, second, w_in, w_out, own, params, cotangent, dims, deps=()):
    seq, width, blocks, hw = dims

    def body(place_ref, n3_ref, second_ref, *refs):
        wi_refs, wo_refs, refs = refs[: len(w_in)], refs[len(w_in) : 2 * len(w_in)], refs[2 * len(w_in) :]
        (prm_ref, cot_ref, hid_ref, slope_ref, out_ref, g3_ref, b3_ref, sum_ref, wi_scr, wo_scr,
         acc_scr) = refs
        t = pl.program_id(0)
        assemble(wi_refs, own, place_ref, wi_scr)
        assemble(wo_refs, own, place_ref, wo_scr)

        @pl.when(t == 0)
        def _():
            acc_scr[...] = second_ref[...] + prm_ref[14:15]

        before = dot(n3_ref[...], wi_scr[...]) + prm_ref[pl.ds(15 + t, 1)]
        phi = 0.5 + 0.5 * lax.erf(before * 2**-0.5)
        hidden = (before * phi).astype(BF)
        hid_ref[0] = hidden
        slope_ref[0] = phi + before * (jnp.exp(-0.5 * before * before) * 0.3989422804014327)
        acc_scr[...] += dot(hidden, wo_scr[...], 1, 1)

        @pl.when(t == blocks - 1)
        def _():
            unit, inverse = layer_norm_parts(acc_scr[...])
            out_ref[...] = (unit * prm_ref[3:4] + prm_ref[7:8]).astype(BF)
            cot = cot_ref[...].astype(F32)
            grad = norm_back(cot, unit, inverse, prm_ref[3:4])
            g3_ref[...] = grad
            branch = grad.astype(BF)
            b3_ref[...] = branch
            sum_ref[...] = jnp.zeros_like(sum_ref)
            sum_ref[3:4] = column_sum(cot * unit)
            sum_ref[7:8] = column_sum(cot)
            sum_ref[14:15] = column_sum(branch.astype(F32))

    full = whole((seq, width))
    wide = (blocks, seq, width)
    return call(
        body, "feed_forward", blocks,
        [(n3, full), (second, full), *pack_in(w_in), *pack_in(w_out),
         (params, whole(params.shape)), (cotangent, full)],
        [(sds(wide, BF), per_block(wide)), (sds(wide, F32), per_block(wide)),
         (sds((seq, width), BF), full), (sds((seq, width), F32), full),
         (sds((seq, width), BF), full), (sds(params.shape, F32), whole(params.shape))],
        [pack_scratch(width), pack_scratch(width), pltpu.VMEM((seq, width), F32)],
        16 * seq * width * width,
        (place,),
        deps,
    )


def feed_out_grads(place, b3, hidden, grad_shape, dims, deps=()):
    seq, width, blocks, hw = dims

    def body(place_ref, b3_ref, hid_ref, *refs):
        grad_refs, (b3t_scr,) = refs[:-1], refs[-1:]

        @pl.when(pl.program_id(0) == 0)
        def _():
            b3t_scr[...] = b3_ref[...].T

        store_pack(grad_refs, dot(b3t_scr[...], hid_ref[0]).astype(BF), place_ref)

    wide = (blocks, seq, width)
    return call(
        body, "feed_out_grads", blocks,
        [(b3, whole((seq, width))), (hidden, per_block(wide))],
        grad_outs(grad_shape),
        [pltpu.VMEM((width, seq), BF)],
        8 * seq * width * width,
        (place,),
        deps,
    )


def feed_backward(place, b3, g3, slope, w_in, w_out, own, n3, second, params, sums, grad_shape, dims, deps=()):
    seq, width, blocks, hw = dims
    grads = grad_outs(grad_shape)

    def body(place_ref, b3_ref, g3_ref, slope_ref, *refs):
        wi_refs, wo_refs, refs = refs[: len(w_in)], refs[len(w_in) : 2 * len(w_in)], refs[2 * len(w_in) :]
        (n3_ref, second_ref, prm_ref, old_ref), refs = refs[:4], refs[4:]
        grad_refs, refs = refs[: len(grads)], refs[len(grads) :]
        g2_ref, b2_ref, sum_ref, wi_scr, wo_scr, n3t_scr, acc_scr = refs
        t = pl.program_id(0)
        assemble(wi_refs, own, place_ref, wi_scr)
        assemble(wo_refs, own, place_ref, wo_scr)

        @pl.when(t == 0)
        def _():
            sum_ref[...] = old_ref[...]
            n3t_scr[...] = n3_ref[...].T
            acc_scr[...] = jnp.zeros_like(acc_scr)

        grad_before = (dot(b3_ref[...], wo_scr[...]) * slope_ref[0]).astype(BF)
        sum_ref[pl.ds(15 + t, 1)] = column_sum(grad_before.astype(F32))
        store_pack(grad_refs, dot(n3t_scr[...], grad_before).astype(BF), place_ref)
        acc_scr[...] += dot(grad_before, wi_scr[...], 1, 1)

        @pl.when(t == blocks - 1)
        def _():
            grad = acc_scr[...]
            unit, inverse = layer_norm_parts(second_ref[...])
            sum_ref[2:3] = column_sum(grad * unit)
            sum_ref[6:7] = column_sum(grad)
            grad_second = g3_ref[...] + norm_back(grad, unit, inverse, prm_ref[2:3])
            g2_ref[...] = grad_second
            branch = grad_second.astype(BF)
            b2_ref[...] = branch
            sum_ref[13:14] = column_sum(branch.astype(F32))

    full = whole((seq, width))
    wide = (blocks, seq, width)
    return call(
        body, "feed_backward", blocks,
        [(b3, full), (g3, full), (slope, per_block(wide)), *pack_in(w_in), *pack_in(w_out), (n3, full),
         (second, full), (params, whole(params.shape)), (sums, whole(sums.shape))],
        grads
        + [(sds((seq, width), F32), full), (sds((seq, width), BF), full),
           (sds(sums.shape, F32), whole(sums.shape))],
        [pack_scratch(width), pack_scratch(width), pltpu.VMEM((width, seq), BF), pltpu.VMEM((seq, width), F32)],
        24 * seq * width * width,
        (place,),
        deps,
    )


def cross_attend_back(place, start, count, sums, b2, queries, keys, values, keys_t, lse, ot, pack, own, valid,
                      dims, deps=(), carried=()):
    seq, width, blocks, hw = dims
    heads = hw // HD
    _, pieces, piece, _ = keys.shape
    total_keys = pieces * piece

    def body(place_ref, old_ref, b2_ref, q_ref, k_ref, v_ref, kt_ref, lse_ref, ot_ref, *refs):
        w_refs, refs = refs[: len(pack)], refs[len(pack) :]
        dq_ref, dkv_ref, sum_ref, w_scr, dk_scr, dv_scr, ds_scr, dqt_scr = refs
        t = pl.program_id(0)
        assemble(w_refs, own, place_ref, w_scr)

        @pl.when(t == 0)
        def _():
            sum_ref[...] = old_ref[...]

        q = q_ref[0]
        gm = project_back(b2_ref[...], w_scr, hw).astype(BF)
        weighted = gm.astype(F32).T * ot_ref[0]
        row = lax.broadcasted_iota(jnp.int32, (piece, 1), 0)
        pad = jnp.where(row < valid, 0.0, NEGATIVE)
        dk_scr[...] = jnp.zeros_like(dk_scr)
        dv_scr[...] = jnp.zeros_like(dv_scr)
        for j in range(heads):
            delta = jnp.sum(weighted[j * HD : (j + 1) * HD], 0, keepdims=True)
            shift = lse_ref[0, j : j + 1]
            qm = head_lanes(q, j, HD)
            gj = head_lanes(gm, j, HD)

            def one_piece(c, carry):
                s = dot(k_ref[0, c], qm, 1, 1) + pad
                p = jnp.exp(s - shift)
                ds = (p * (dot(v_ref[0, c], gj, 1, 1) - delta)).astype(BF)
                dv_scr[c] += dot(p.astype(BF), gj)
                dk_scr[c] += dot(ds, qm)
                ds_scr[pl.ds(pl.multiple_of(c * piece, piece), piece)] = ds
                return carry

            lax.fori_loop(0, pieces, one_piece, 0)
            dqt_scr[j * HD : (j + 1) * HD] = dot(kt_ref[0, j * HD : (j + 1) * HD], ds_scr[...])
        dq = dqt_scr[...].T.astype(BF).astype(F32) * HD**-0.5
        put_heads(sum_ref, 11, start + t, blocks, column_sum(dq))
        dq_ref[0] = dq.astype(BF)
        bias = jnp.zeros((1, hw), F32)
        for c in range(pieces):
            dv = dv_scr[c].astype(BF)
            bias += column_sum(dv.astype(F32))
            dkv_ref[0, c] = jnp.concatenate([dk_scr[c].astype(BF), dv], 1)
        put_heads(sum_ref, 12, start + t, blocks, bias)

    def block(shape):
        return at_block(shape, start)

    packs = pack_at(pack, start)
    dkv = (blocks, pieces, piece, 2 * hw)
    return call(
        body, "cross_attend_back", count,
        [(sums, whole(sums.shape)), (b2, whole((seq, width))), (queries, block(queries.shape)), (keys, block(keys.shape)),
         (values, block(values.shape)), (keys_t, block(keys_t.shape)), (lse, block(lse.shape)),
         (ot, block(ot.shape)), *packs],
        [(sds(queries.shape, BF), block(queries.shape)), (sds(dkv, BF), block(dkv)),
         (sds(sums.shape, F32), whole(sums.shape))],
        [pack_scratch(width), pltpu.VMEM((pieces, piece, hw), F32), pltpu.VMEM((pieces, piece, hw), F32),
         pltpu.VMEM((total_keys, seq), BF), pltpu.VMEM((hw, seq), F32)],
        count * (2 * seq * width * hw + 10 * seq * total_keys * 256 * heads // 2),
        (place,),
        deps,
        carried,
    )


def cross_rows_back(place, sums, dq, dkv, g2, first, pack, own, params, valid, dims, deps=()):
    seq, width, blocks, hw = dims
    _, pieces, piece, _ = dkv.shape
    frames = (pieces, piece, width)
    kept = (pieces, valid, width)

    def body(place_ref, old_ref, dq_ref, dkv_ref, g2_ref, first_ref, *refs):
        w_refs, refs = refs[: len(pack)], refs[len(pack) :]
        prm_ref, genc_ref, g1_ref, b1_ref, sum_ref, w_scr, genc_scr, acc_scr = refs
        t = pl.program_id(0)
        assemble(w_refs, own, place_ref, w_scr)

        @pl.when(t == 0)
        def _():
            acc_scr[...] = jnp.zeros_like(acc_scr)
            genc_scr[...] = jnp.zeros_like(genc_scr)
            sum_ref[...] = old_ref[...]

        wkv = w_scr[:, : 2 * hw]
        for c in range(pieces):
            genc_scr[c] += dot(dkv_ref[0, c], wkv, 1, 1)
        acc_scr[...] += dot(dq_ref[0], w_scr[:, 2 * hw : 3 * hw], 1, 1)

        @pl.when(t == blocks - 1)
        def _():
            for c in range(pieces):
                genc_ref[lax.rem(place_ref[1] + pieces - c, pieces)] = genc_scr[c, :valid].astype(BF)
            grad = acc_scr[...]
            unit, inverse = layer_norm_parts(first_ref[...])
            sum_ref[1:2] = column_sum(grad * unit)
            sum_ref[5:6] = column_sum(grad)
            grad_first = g2_ref[...] + norm_back(grad, unit, inverse, prm_ref[1:2])
            g1_ref[...] = grad_first
            branch = grad_first.astype(BF)
            b1_ref[...] = branch
            sum_ref[10:11] = column_sum(branch.astype(F32))

    full = whole((seq, width))
    return call(
        body, "cross_rows_back", blocks,
        [(sums, whole(sums.shape)), (dq, per_block(dq.shape)), (dkv, per_block(dkv.shape)), (g2, full), (first, full), *pack_in(pack),
         (params, whole(params.shape))],
        [(sds(kept, BF), whole(kept)), (sds((seq, width), F32), full), (sds((seq, width), BF), full),
         (sds(sums.shape, F32), whole(sums.shape))],
        [pack_scratch(width), pltpu.VMEM(frames, F32), pltpu.VMEM((seq, width), F32)],
        2 * seq * width * width + 4 * pieces * piece * width * width,
        (place,),
        deps,
    )


def cross_grads(place, dq, dkv, mixed, b2, n2, frames, grad_shape, dims, deps=()):
    seq, width, blocks, hw = dims
    _, pieces, piece, _ = dkv.shape
    total_keys = pieces * piece

    def body(place_ref, dq_ref, dkv_ref, mix_ref, b2_ref, n2_ref, e_ref, *refs):
        grad_refs, (et_scr, b2t_scr, n2t_scr) = refs[:-3], refs[-3:]

        @pl.when(pl.program_id(0) == 0)
        def _():
            for c in range(pieces):
                et_scr[:, c * piece : (c + 1) * piece] = e_ref[c].T
            b2t_scr[...] = b2_ref[...].T
            n2t_scr[...] = n2_ref[...].T

        grad_kv = dot(et_scr[...], dkv_ref[0].reshape(total_keys, 2 * hw))
        grad_q = dot(n2t_scr[...], dq_ref[0])
        grad_o = dot(b2t_scr[...], mix_ref[0])
        store_pack(grad_refs, jnp.concatenate([grad_kv, grad_q, grad_o], 1).astype(BF), place_ref)

    full = whole((seq, width))
    return call(
        body, "cross_grads", blocks,
        [(dq, per_block(dq.shape)), (dkv, per_block(dkv.shape)), (mixed, per_block(mixed.shape)), (b2, full),
         (n2, full), (frames, whole(frames.shape))],
        grad_outs(grad_shape),
        [pltpu.VMEM((width, total_keys), BF), pltpu.VMEM((width, seq), BF), pltpu.VMEM((width, seq), BF)],
        4 * seq * width * width + 4 * total_keys * width * width,
        (place,),
        deps,
    )


def self_attend_back(length, place, sums, b1, queries, keys, values, lse, ot, pack, own, dims, deps=()):
    seq, width, blocks, hw = dims
    heads = hw // HD

    def body(len_ref, place_ref, old_ref, b1_ref, q_ref, k_ref, v_ref, lse_ref, ot_ref, *refs):
        w_refs, refs = refs[: len(pack)], refs[len(pack) :]
        dqkv_ref, sum_ref, w_scr, bias_scr, dqt_scr = refs
        t = pl.program_id(0)
        assemble(w_refs, own, place_ref, w_scr)

        @pl.when(t == 0)
        def _():
            sum_ref[...] = old_ref[...]
            key = lax.broadcasted_iota(jnp.int32, (seq, seq), 0)
            query = lax.broadcasted_iota(jnp.int32, (seq, seq), 1)
            bias_scr[...] = jnp.where((key <= query) & (key < len_ref[0]), 0.0, NEGATIVE)

        q = q_ref[0]
        k = k_ref[0]
        v = v_ref[0]
        kt = k.T
        gm = project_back(b1_ref[...], w_scr, hw).astype(BF)
        weighted = gm.astype(F32).T * ot_ref[0]
        dk = jnp.zeros((seq, hw), F32)
        dv = jnp.zeros((seq, hw), F32)
        for j in range(heads):
            delta = jnp.sum(weighted[j * HD : (j + 1) * HD], 0, keepdims=True)
            qm = head_lanes(q, j, HD)
            gj = head_lanes(gm, j, HD)
            p = jnp.exp(dot(k, qm, 1, 1) + bias_scr[...] - lse_ref[0, j : j + 1])
            ds = (p * (dot(v, gj, 1, 1) - delta)).astype(BF)
            dv += dot(p.astype(BF), gj)
            dk += dot(ds, qm)
            dqt_scr[j * HD : (j + 1) * HD] = dot(kt[j * HD : (j + 1) * HD], ds)
        dq = dqt_scr[...].T.astype(BF).astype(F32) * HD**-0.5
        dv = dv.astype(BF)
        put_heads(sum_ref, 8, t, blocks, column_sum(dq))
        put_heads(sum_ref, 9, t, blocks, column_sum(dv.astype(F32)))
        dqkv_ref[0] = jnp.concatenate([dq.astype(BF), dk.astype(BF), dv], 1)

    hb = per_block((blocks, seq, hw))
    dqkv = (blocks, seq, 3 * hw)
    return call(
        body, "self_attend_back", blocks,
        [(sums, whole(sums.shape)), (b1, whole((seq, width))), (queries, hb), (keys, hb), (values, hb), (lse, per_block(lse.shape)),
         (ot, per_block(ot.shape)), *pack_in(pack)],
        [(sds(dqkv, BF), per_block(dqkv)), (sds(sums.shape, F32), whole(sums.shape))],
        [pack_scratch(width), pltpu.VMEM((seq, seq), F32), pltpu.VMEM((hw, seq), F32)],
        2 * seq * width * width + 40 * seq * seq * width,
        (length, place),
        deps,
    )


def self_grads(place, dqkv, mixed, b1, n1, grad_shape, dims, deps=()):
    seq, width, blocks, hw = dims

    def body(place_ref, dqkv_ref, mix_ref, b1_ref, n1_ref, *refs):
        grad_refs, (b1t_scr, n1t_scr) = refs[:-2], refs[-2:]

        @pl.when(pl.program_id(0) == 0)
        def _():
            b1t_scr[...] = b1_ref[...].T
            n1t_scr[...] = n1_ref[...].T

        grad_qkv = dot(n1t_scr[...], dqkv_ref[0])
        grad_o = dot(b1t_scr[...], mix_ref[0])
        store_pack(grad_refs, jnp.concatenate([grad_qkv, grad_o], 1).astype(BF), place_ref)

    full = whole((seq, width))
    return call(
        body, "self_grads", blocks,
        [(dqkv, per_block(dqkv.shape)), (mixed, per_block(mixed.shape)), (b1, full), (n1, full)],
        grad_outs(grad_shape),
        [pltpu.VMEM((width, seq), BF), pltpu.VMEM((width, seq), BF)],
        8 * seq * width * width,
        (place,),
        deps,
    )


def self_rows_back(place, sums, dqkv, g1, rows, pack, own, params, dims, deps=()):
    seq, width, blocks, hw = dims

    def body(place_ref, old_ref, dqkv_ref, g1_ref, x_ref, *refs):
        w_refs, refs = refs[: len(pack)], refs[len(pack) :]
        prm_ref, gin_ref, sum_ref, w_scr, acc_scr = refs
        t = pl.program_id(0)
        assemble(w_refs, own, place_ref, w_scr)

        @pl.when(t == 0)
        def _():
            acc_scr[...] = jnp.zeros_like(acc_scr)
            sum_ref[...] = old_ref[...]

        acc_scr[...] += dot(dqkv_ref[0], w_scr[:, : 3 * hw], 1, 1)

        @pl.when(t == blocks - 1)
        def _():
            grad = acc_scr[...]
            unit, inverse = layer_norm_parts(x_ref[...].astype(F32))
            sum_ref[0:1] = column_sum(grad * unit)
            sum_ref[4:5] = column_sum(grad)
            gin_ref[...] = g1_ref[...] + norm_back(grad, unit, inverse, prm_ref[0:1])

    full = whole((seq, width))
    return call(
        body, "self_rows_back", blocks,
        [(sums, whole(sums.shape)), (dqkv, per_block(dqkv.shape)), (g1, full), (rows, full), *pack_in(pack), (params, whole(params.shape))],
        [(sds((seq, width), F32), full), (sds(sums.shape, F32), whole(sums.shape))],
        [pack_scratch(width), pltpu.VMEM((seq, width), F32)],
        6 * seq * width * width,
        (place,),
        deps,
    )


def pad_rows(rows, count):
    return jnp.pad(rows, ((0, count - rows.shape[0]),) + ((0, 0),) * (rows.ndim - 1))


def swap(array, step):
    count = lax.axis_size("fsdp")
    return lax.ppermute(array, "fsdp", [(i, i ^ step) for i in range(count)])


def around(array, hop):
    count = lax.axis_size("tp")
    return lax.ppermute(array, "tp", [(i, (i + hop) % count) for i in range(count)])


def native_gather(shard):
    whole_pack = lax.all_gather(shard, ("fsdp", "tp"), axis=0, tiled=False)
    return whole_pack.reshape((lax.axis_size("fsdp"), lax.axis_size("tp")) + shard.shape)


def in_order(pieces, here):
    count = len(pieces)
    stacked = jnp.stack(pieces)
    return jnp.stack(
        [lax.dynamic_index_in_dim(stacked, (here - t) % count, 0, keepdims=False) for t in range(count)]
    )


def gate(array, things):
    return lax.optimization_barrier((array,) + tuple(things))[0] if things else array


class Gather:
    def __init__(self, shard):
        self.shard = shard

    def direct(self):
        come = [around(self.shard, hop) for hop in range(1, 4)]
        line = in_order([self.shard] + come, lax.axis_index("tp"))
        self.low, self.high = line[None, :2], line[None, 2:]
        return tuple(come)

    def first(self):
        self.low_x, self.high_y = swap(self.low, 2), swap(self.high, 4)
        return self.low_x, self.high_y

    def second(self):
        self.low_two = jnp.concatenate([self.low, self.low_x])
        self.high_two = jnp.concatenate([self.high, self.high_y])
        self.low_y, self.high_x = swap(self.low_two, 4), swap(self.high_two, 2)
        return self.low_y, self.high_x

    def core(self):
        low = jnp.concatenate([self.low_two, self.low_y])
        high = jnp.stack([self.high_two[0], self.high_x[0], self.high_two[1], self.high_x[1]])
        mine = jnp.concatenate([low, high], 1)
        self.pack = (mine, swap(mine, 1))
        return self.pack[1:]


def wide(array):
    return array.astype(F32)


class Scatter:
    def __init__(self, halves):
        self.kept, self.sent = halves
        self.tp = self.kept.shape[1]
        self.half = self.tp // 2

    def core(self):
        self.come = swap(self.sent, 1)
        return self.come

    def first(self):
        def both(q, t):
            return (wide(self.kept[q, t]) + wide(self.come[q, t])).astype(BF)

        low, high = slice(0, self.half), slice(self.half, self.tp)
        self.low_y = swap(both(slice(2, 4), low), 4)
        self.high_x = swap(both(slice(1, 4, 2), high), 2)
        return self.low_y, self.high_x

    def second(self):
        low, high = slice(0, self.half), slice(self.half, self.tp)

        def three(q, t, more):
            return wide(self.kept[q, t]) + wide(self.come[q, t]) + wide(more)

        self.low_x = swap(three(1, low, self.low_y[1]).astype(BF), 2)
        self.high_y = swap(three(2, high, self.high_x[1]).astype(BF), 4)
        return self.low_x, self.high_y

    def line(self):
        def total(t, more, last):
            return wide(self.kept[0, t]) + wide(self.come[0, t]) + wide(more) + wide(last)

        low, high = slice(0, self.half), slice(self.half, self.tp)
        sums = jnp.concatenate(
            [total(low, self.low_y[0], self.low_x), total(high, self.high_x[0], self.high_y)]
        ).astype(BF)
        here = lax.axis_index("tp")
        self.own = lax.dynamic_index_in_dim(sums, here, 0, keepdims=False)
        self.parts = [
            around(lax.dynamic_index_in_dim(sums, (here + hop) % self.tp, 0, keepdims=False), hop)
            for hop in range(1, self.tp)
        ]
        return tuple(self.parts)

    def total(self):
        result = wide(self.own)
        for part in self.parts:
            result += wide(part)
        return result


def butterfly_scatter(grads, own, narrow=BF):
    fsdp, tp = lax.axis_size("fsdp"), lax.axis_size("tp")
    if grads.shape[0] != fsdp:
        blocks, width = grads.shape[1], grads.shape[3]
        grads = grads.reshape(blocks, fsdp, own, width).transpose(1, 0, 2, 3)
    place = lax.axis_index("fsdp")
    step = 1
    while step < fsdp:
        pairs = grads.reshape((grads.shape[0] // 2, 2) + grads.shape[1:])
        bit = (place // step) % 2
        kept = lax.dynamic_index_in_dim(pairs, bit, 1, keepdims=False)
        sent = lax.dynamic_index_in_dim(pairs, 1 - bit, 1, keepdims=False)
        grads = (wide(kept) + wide(swap(sent, step))).astype(narrow)
        step *= 2
    grads = grads[0]
    here = lax.axis_index("tp")
    total = wide(lax.dynamic_index_in_dim(grads, here, 0, keepdims=False))
    for hop in range(1, tp):
        sent = lax.dynamic_index_in_dim(grads, (here + hop) % tp, 0, keepdims=False)
        total += wide(around(sent, hop))
    return total


def local(
    inputs,
    encoder,
    lengths,
    self_qkv,
    self_out,
    cross_q,
    cross_kv,
    cross_out,
    fc_in,
    fc_out,
    norm_gain,
    norm_bias,
    proj_bias,
    fc_in_bias,
    cotangent,
):
    fsdp, tp = lax.axis_size("fsdp"), lax.axis_size("tp")
    devices = fsdp * tp
    tp_place = lax.axis_index("tp")
    place = jnp.stack([lax.axis_index("fsdp"), tp_place])
    seqs, seq, width = inputs.shape
    assert seqs == 1
    own, hw = cross_q.shape
    dims = (seq, width, tp, hw)
    frames_own = encoder.shape[1]
    small_own = norm_gain.shape[1]
    ff_own = fc_in_bias.shape[0]
    chained = fsdp == 8 and tp == 4 and own % 16 == 0

    small = jnp.concatenate(
        [a.reshape(-1) for a in (norm_gain, norm_bias, proj_bias, fc_in_bias)]
    )
    small = jnp.pad(small, (0, width - small.size))
    high = small.astype(BF)
    low = (small - high.astype(F32)).astype(BF)
    extra = pad_rows(jnp.stack([high, low]), 16)

    pack_self = jnp.concatenate([self_qkv[0], self_qkv[1], self_qkv[2], self_out.T], 1)
    pack_self = jnp.concatenate([pack_self, extra], 0)
    pack_cross = jnp.concatenate([cross_kv[0], cross_kv[1], cross_q, cross_out.T], 1)
    x = inputs[0]
    length = lax.dynamic_slice_in_dim(lengths, tp_place, 1)
    chains = {}
    sends = {"direct": "shard", "first": "low high", "second": "low_x high_y", "core": "low_y high_x"}

    def move(after, *steps):
        out = ()
        for text in steps if chained else ():
            name, step = text.split(".")
            chain = chains[name]
            for array in sends[step].split():
                setattr(chain, array, gate(getattr(chain, array), after))
            out += getattr(chain, step)()
        return out

    frames = [
        lax.dynamic_index_in_dim(encoder, (tp_place + hop) % tp, 0, keepdims=False) for hop in range(tp)
    ]
    before = turn = ()
    if chained:
        for name, shard in (("self", pack_self), ("cross", pack_cross), ("in", fc_in), ("out", fc_out.T)):
            chains[name] = Gather(shard)
        turn = move((), "self.direct") + tuple(frames)
        turn = move(turn, "self.first", "cross.direct")
        turn = move(turn, "self.second", "in.direct")
        frames[1] = around(gate(frames[1], turn), 1)
        turn = move(turn, "self.core", "cross.first") + (frames[1],)
        before = turn
        edge = frames_own // 32 * 16
        frames[3] = around(gate(frames[3], turn), 3)
        near, far = frames[2][:edge], frames[2][edge:]
        near = around(gate(near, turn), 2)
        turn = move(turn, "cross.second", "in.first") + (frames[3], near)
        w_self = chains["self"].pack
        own_rows = own
        grad_shape = (fsdp // 2, tp, own, width)
        blocks = jnp.stack([part[:, :, own : own + 2] for part in w_self], 1)
        blocks = blocks.reshape(fsdp, tp, 2, width)
        table = jnp.stack(
            [lax.dynamic_index_in_dim(blocks, f ^ place[0], 0, keepdims=False) for f in range(fsdp)]
        )
        table = wide(table).sum(2).reshape(devices, width)
    else:
        w_self = native_gather(pack_self)
        table = wide(w_self[:, :, own : own + 2]).sum(2).reshape(devices, width)
        own_rows = own * fsdp
        grad_shape = (1, tp, own_rows, width)

        def end_to_end(pack):
            return pack[:, :, :own].transpose(1, 0, 2, 3).reshape(1, tp, own_rows, width)

        w_self = (end_to_end(w_self),)
        w_cross = (end_to_end(native_gather(pack_cross)),)
        w_in = (end_to_end(native_gather(fc_in)),)
        w_out = (end_to_end(native_gather(fc_out.T)),)

    rows = norm_gain.shape[0] + norm_bias.shape[0] + proj_bias.shape[0]
    params = table[:, : rows * small_own].reshape(devices, rows, small_own)
    params = params.transpose(1, 0, 2).reshape(rows, width)
    fc_bias = table[:, rows * small_own : rows * small_own + ff_own].reshape(tp, width)
    head_bias = jnp.stack([params[8], params[9], params[11], params[12]])
    head_bias = head_bias.reshape(4, tp, hw).transpose(1, 0, 2)
    head_bias = jnp.pad(head_bias, ((0, 0), (0, 4), (0, 0)))
    params = pad_rows(jnp.concatenate([params, fc_bias], 0), 24)

    piece = -(-frames_own // 128) * 128
    half = tp // 2

    q1, k1, v1, lse1, ot1, mixed1, n1, first, n2 = self_forward(
        length, place, 0, tp, x, x, w_self, own_rows, params, head_bias, dims, before
    )
    turn += (n2,)
    if chained:
        far = around(gate(far, turn), 2)
        turn = move(turn, "cross.core", "in.second") + (far,)
        w_cross = chains["cross"].pack
        frames = [(frames[0],), (frames[1],), (near, far), (frames[3],)]
    else:
        frames = [(around(array, hop) if hop else array,) for hop, array in enumerate(frames)]
    k2, v2, k2t, v2t, frames = frame_keys(place, frames, w_cross, own_rows, head_bias, piece, dims, turn)
    turn = move(turn, "in.core", "out.direct") + (k2,)
    shared = (w_cross, own_rows, params, head_bias, k2, v2t, frames_own, dims)
    *kept, part, _ = cross_forward(place, 0, half, n2, first, *shared, turn)
    turn = move(turn, "out.first") + (part,)
    q2, lse2, ot2, mixed2, second, n3 = cross_forward(place, half, tp - half, n2, part, *shared, turn, kept)
    turn = move(turn, "out.second") + (n3,)
    move(turn, "out.core")
    if chained:
        w_in, w_out = chains["in"].pack, chains["out"].pack
    hidden, slope, layer_out, g3, b3, sums = feed_forward(
        place, n3, second, w_in, w_out, own_rows, params, cotangent[0], dims
    )
    scatters = {}

    def begin(name, halves):
        if chained:
            scatters[name] = Scatter(halves)

    def go(name, step):
        if not chained:
            return ()
        out = getattr(scatters[name], step)()
        return out if isinstance(out, tuple) else (out,)

    grad_out = feed_out_grads(place, b3, hidden, grad_shape, dims)
    begin("out", grad_out)
    step1 = go("out", "core")
    *grad_in, g2, b2, sums = feed_backward(
        place, b3, g3, slope, w_in, w_out, own_rows, n3, second, params, sums, grad_shape, dims, (grad_out[0],)
    )
    begin("in", grad_in)
    step2 = go("out", "first") + go("in", "core")
    shared = (b2, q2, k2, v2, k2t, lse2, ot2, w_cross, own_rows, frames_own, dims)
    *kept, sums = cross_attend_back(place, 0, half, sums, *shared, step1)
    step3 = go("out", "second") + go("in", "first")
    dq2, dkv2, sums = cross_attend_back(place, half, tp - half, sums, *shared, step2, kept)
    step4 = go("out", "line") + go("in", "second")
    grad_frames, g1, b1, sums = cross_rows_back(
        place, sums, dq2, dkv2, g2, first, w_cross, own_rows, params, frames_own, dims, step3
    )
    grad_cross = cross_grads(place, dq2, dkv2, mixed2, b2, n2, frames, grad_shape, dims, step4 + (b1,))
    step5 = go("in", "line")
    begin("cross", grad_cross)
    frames_back = lax.all_to_all(gate(grad_frames, (grad_cross[0], *step5)), "tp", 0, 0, tiled=True)
    step6 = go("cross", "core")
    dqkv1, sums = self_attend_back(
        length, place, sums, b1, q1, k1, v1, lse1, ot1, w_self, own_rows, dims, step5 + (grad_cross[0],)
    )
    step7 = go("cross", "first")
    grad_self = self_grads(place, dqkv1, mixed1, b1, n1, grad_shape, dims, step6)
    begin("self", grad_self)
    go("self", "core")
    grad_inputs, sums = self_rows_back(
        place, sums, dqkv1, g1, x, w_self, own_rows, params, dims, step7 + (grad_self[0],)
    )
    turns = [(), (), (), ()]
    if chained:
        scatters["cross"].low_y = gate(scatters["cross"].low_y, (grad_self[0],))
        step8 = go("cross", "second")
        scatters["self"].come = gate(scatters["self"].come, (sums, *step8))
        scatters["cross"].low_x = gate(scatters["cross"].low_x, (sums, *step8))
        turns[2] = go("self", "first") + go("cross", "line")
        scatters["self"].low_y = gate(scatters["self"].low_y, turns[2])
        turns[3] = go("self", "second")
    step = 1
    while step < fsdp:
        sums = sums + swap(gate(sums, turns.pop(0) if turns else ()), step)
        step *= 2
    sums = gate(sums, turns.pop(0) if turns else ())
    sums = sum([around(sums, hop) for hop in range(1, tp)], sums)
    device = lax.axis_index("fsdp") * tp + tp_place
    mine = lax.dynamic_slice_in_dim(sums[:rows], device * small_own, small_own, 1)
    gains = norm_gain.shape[0]
    own_gain, own_shift, own_bias = mine[:gains], mine[gains : 2 * gains], mine[2 * gains :]
    per_row = width // ff_own
    own_fc_bias = lax.dynamic_slice(
        sums, (rows + device // per_row, (device % per_row) * ff_own), (1, ff_own)
    )[0]

    if chained:
        go("self", "line")
        total_out, total_in, total_cross, total_self = (
            scatters[name].total() for name in ("out", "in", "cross", "self")
        )
    else:
        total_out, total_in, total_cross, total_self = (
            butterfly_scatter(grads[0], own) for grads in (grad_out, grad_in, grad_cross, grad_self)
        )

    def part(total, index):
        return total[:, index * hw : (index + 1) * hw]

    return (
        layer_out[None],
        grad_inputs[None],
        frames_back.astype(F32),
        jnp.stack([part(total_self, 0), part(total_self, 1), part(total_self, 2)]),
        part(total_self, 3).T,
        part(total_cross, 2),
        jnp.stack([part(total_cross, 0), part(total_cross, 1)]),
        part(total_cross, 3).T,
        total_in,
        total_out.T,
        own_gain,
        own_shift,
        own_bias,
        own_fc_bias,
    )


def solution(mesh):
    return jax.shard_map(
        local,
        mesh=mesh,
        in_specs=(
            P(("fsdp", "tp"), None, None),
            P("fsdp", "tp", None),
            P("fsdp"),
            P(None, "fsdp", "tp"),
            P("tp", "fsdp"),
            P("fsdp", "tp"),
            P(None, "fsdp", "tp"),
            P("tp", "fsdp"),
            P("fsdp", "tp"),
            P("tp", "fsdp"),
            P(None, ("fsdp", "tp")),
            P(None, ("fsdp", "tp")),
            P(None, ("fsdp", "tp")),
            P(("fsdp", "tp")),
            P(("fsdp", "tp"), None, None),
        ),
        out_specs=(
            P(("fsdp", "tp"), None, None),
            P(("fsdp", "tp"), None, None),
            P("fsdp", "tp", None),
            P(None, "fsdp", "tp"),
            P("tp", "fsdp"),
            P("fsdp", "tp"),
            P(None, "fsdp", "tp"),
            P("tp", "fsdp"),
            P("fsdp", "tp"),
            P("tp", "fsdp"),
            P(None, ("fsdp", "tp")),
            P(None, ("fsdp", "tp")),
            P(None, ("fsdp", "tp")),
            P(("fsdp", "tp")),
        ),
        check_vma=False,
    )
```

```python
import functools

import jax
import jax.numpy as jnp
from jax import lax
from jax.experimental import pallas as pl
from jax.experimental.pallas import tpu as pltpu
from jax.sharding import PartitionSpec as P

HD = 64
EPSILON = 1e-05
NEGATIVE = -1e30
VMEM_LIMIT = 60 * 2**20
HINT = 20
BF = jnp.bfloat16
F32 = jnp.float32


def dot(left, right, left_dim=1, right_dim=0):
    return lax.dot_general(
        left, right, (((left_dim,), (right_dim,)), ((), ())), preferred_element_type=F32
    )


def layer_norm_parts(rows):
    center = rows - jnp.mean(rows, -1, keepdims=True)
    inverse = lax.rsqrt(jnp.mean(center * center, -1, keepdims=True) + EPSILON)
    return center * inverse, inverse


def norm_back(grad_rows, unit, inverse, gain):
    scaled = grad_rows * gain
    return inverse * (
        scaled
        - jnp.mean(scaled, -1, keepdims=True)
        - unit * jnp.mean(scaled * unit, -1, keepdims=True)
    )


def put_heads(sum_ref, row, block, count, value):
    size = value.shape[1]
    for t in range(count):

        @pl.when(block == t)
        def _():
            sum_ref[row : row + 1, t * size : (t + 1) * size] = value


def column_sum(rows):
    return jnp.sum(rows, 0, keepdims=True)


def whole(shape):
    zeros = (0,) * len(shape)
    return pl.BlockSpec(shape, lambda t, *_: zeros)


def per_block(shape):
    rest = (0,) * (len(shape) - 1)
    return pl.BlockSpec((1,) + tuple(shape[1:]), lambda t, *_: (t,) + rest)


def packed(shape):
    return pl.BlockSpec((shape[0], 1) + tuple(shape[2:]), lambda t, *_: (0, t, 0, 0))


def sds(shape, dtype):
    return jax.ShapeDtypeStruct(tuple(shape), dtype)


def call(body, name, grid, ins, outs, scratch, flops, scalars=(), deps=(), carried=()):
    moved = sum(a.size * a.dtype.itemsize for a, _ in ins)
    moved += sum(o.size * o.dtype.itemsize for o, _ in outs)
    first = len(scalars) + len(ins)
    extra = list(carried) + list(deps)

    def inner(*refs):
        return body(*refs[:first], *refs[first + len(extra) :])

    return pl.pallas_call(
        inner,
        out_shape=[o for o, _ in outs],
        grid_spec=pltpu.PrefetchScalarGridSpec(
            num_scalar_prefetch=len(scalars),
            grid=(grid,),
            in_specs=[s for _, s in ins] + [pl.BlockSpec(memory_space=pl.ANY)] * len(extra),
            out_specs=[s for _, s in outs],
            scratch_shapes=scratch,
        ),
        compiler_params=pltpu.CompilerParams(
            dimension_semantics=("arbitrary",), vmem_limit_bytes=VMEM_LIMIT
        ),
        input_output_aliases={first + i: i for i in range(len(carried))},
        cost_estimate=pl.CostEstimate(flops=HINT * flops, bytes_accessed=moved, transcendentals=0),
        name=name,
    )(*scalars, *[a for a, _ in ins], *extra)


def head_lanes(rows, head, block):
    lane = lax.broadcasted_iota(jnp.int32, rows.shape, 1)
    return jnp.where((lane >= head * block) & (lane < (head + 1) * block), rows, jnp.zeros_like(rows))


def pack_in(pack):
    return pack_at(pack, 0)


def at_block(shape, start):
    rest = (0,) * (len(shape) - 1)
    return pl.BlockSpec((1,) + tuple(shape[1:]), lambda t, *_: (start + t,) + rest)


def pack_at(pack, start):
    return [
        (a, pl.BlockSpec((a.shape[0], 1) + a.shape[2:], lambda t, *_: (0, start + t, 0, 0))) for a in pack
    ]


def pack_scratch(width):
    return pltpu.VMEM((width, width), BF)


def assemble(refs, rows, place_ref, scr):
    if len(refs) == 1:
        parts = refs[0][:, 0, :rows, :]
        scr[...] = parts.reshape(parts.shape[0] * rows, parts.shape[2])
        return
    count = 2 * refs[0].shape[0]
    for f in range(count):
        distance = f ^ place_ref[0]
        source = distance >> 1
        for bit in range(2):

            @pl.when((distance & 1) == bit)
            def _():
                scr[f * rows : (f + 1) * rows] = refs[bit][source, 0, :rows, :]


def grad_outs(shape):
    return [(sds(shape, BF), packed(shape))] * (1 if shape[0] == 1 else 2)


def store_pack(refs, value, place_ref):
    rows = refs[0].shape[2]
    if len(refs) == 1:
        refs[0][0, 0] = value
        return
    for f in range(2 * refs[0].shape[0]):
        distance = f ^ place_ref[0]
        target = distance >> 1
        for bit in range(2):

            @pl.when((distance & 1) == bit)
            def _():
                refs[bit][target, 0] = value[f * rows : (f + 1) * rows]


def tail_start(hw):
    return (3 * hw) // 128 * 128


def project_out(mixed, w_scr, hw):
    start = tail_start(hw)
    extra = 3 * hw - start
    if extra:
        mixed = jnp.concatenate([jnp.zeros((mixed.shape[0], extra), mixed.dtype), mixed], 1)
    return dot(mixed, w_scr[:, start:], 1, 1)


def project_back(branch, w_scr, hw):
    start = tail_start(hw)
    return dot(branch, w_scr[:, start:])[:, 3 * hw - start :]


def self_forward(length, place, start, count, rows, part, pack, own, params, head_bias, dims, deps=(), carried=()):
    seq, width, blocks, hw = dims
    heads = hw // HD

    def body(len_ref, place_ref, x_ref, part_ref, *refs):
        w_refs, refs = refs[: len(pack)], refs[len(pack) :]
        (prm_ref, hb_ref, q_ref, k_ref, v_ref, lse_ref, ot_ref, mix_ref, n1_ref, first_ref, n2_ref,
         bias_scr, acc_scr, w_scr) = refs
        t = pl.program_id(0)
        assemble(w_refs, own, place_ref, w_scr)

        @pl.when(t == 0)
        def _():
            unit, _ = layer_norm_parts(x_ref[...].astype(F32))
            n1_ref[...] = (unit * prm_ref[0:1] + prm_ref[4:5]).astype(BF)
            key = lax.broadcasted_iota(jnp.int32, (seq, seq), 0)
            query = lax.broadcasted_iota(jnp.int32, (seq, seq), 1)
            bias_scr[...] = jnp.where((key <= query) & (key < len_ref[0]), 0.0, NEGATIVE)
            acc_scr[...] = part_ref[...].astype(F32) + prm_ref[10:11] if start == 0 else part_ref[...]

        qkv = dot(n1_ref[...], w_scr[:, : 3 * hw])
        q = ((qkv[:, :hw] + hb_ref[0, 0:1]) * HD**-0.5).astype(BF)
        k = qkv[:, hw : 2 * hw].astype(BF)
        v = (qkv[:, 2 * hw :] + hb_ref[0, 1:2]).astype(BF)
        q_ref[0] = q
        k_ref[0] = k
        v_ref[0] = v
        vt = v.T
        for j in range(heads):
            s = dot(k, head_lanes(q, j, HD), 1, 1) + bias_scr[...]
            m = jnp.max(s, 0, keepdims=True)
            p = jnp.exp(s - m)
            total = jnp.sum(p, 0, keepdims=True)
            lse_ref[0, j : j + 1] = m + jnp.log(total)
            ot_ref[0, j * HD : (j + 1) * HD] = dot(vt[j * HD : (j + 1) * HD], p.astype(BF)) / total
        mixed = ot_ref[0].T.astype(BF)
        mix_ref[0] = mixed
        acc_scr[...] += project_out(mixed, w_scr, hw)

        @pl.when(t == count - 1)
        def _():
            first = acc_scr[...]
            first_ref[...] = first
            unit, _ = layer_norm_parts(first)
            n2_ref[...] = (unit * prm_ref[1:2] + prm_ref[5:6]).astype(BF)

    full = whole((seq, width))
    hb = sds((blocks, seq, hw), BF)

    def block(shape):
        return at_block(shape, start)

    return call(
        body, "self_forward", count,
        [(rows, full), (part, full), *pack_at(pack, start), (params, whole(params.shape)),
         (head_bias, block(head_bias.shape))],
        [(hb, block(hb.shape))] * 3
        + [(sds((blocks, 8, seq), F32), block((blocks, 8, seq))),
           (sds((blocks, hw, seq), F32), block((blocks, hw, seq))),
           (hb, block(hb.shape)),
           (sds((seq, width), BF), full),
           (sds((seq, width), F32), full),
           (sds((seq, width), BF), full)],
        [pltpu.VMEM((seq, seq), F32), pltpu.VMEM((seq, width), F32), pack_scratch(width)],
        count * (8 * seq * width * hw + 16 * seq * seq * hw),
        (length, place),
        deps,
        carried,
    )


def frame_keys(place, frames, pack, own, head_bias, piece, dims, deps=()):
    seq, width, blocks, hw = dims
    pieces = len(frames)
    valid = frames[0].shape[0]
    total = pieces * piece
    edge = valid // 16 * 16

    def body(place_ref, *refs):
        f_refs, refs = refs[:pieces], refs[pieces:]
        w_refs, refs = refs[: len(pack)], refs[len(pack) :]
        hb_ref, k_ref, v_ref, kt_ref, vt_ref, e_ref, w_scr = refs
        assemble(w_refs, own, place_ref, w_scr)

        @pl.when(pl.program_id(0) == 0)
        def _():
            for c in range(pieces):
                e_ref[c, edge:] = jnp.zeros((piece - edge, width), BF)
                e_ref[c, :valid] = f_refs[c][...]

        w = w_scr[:, : 2 * hw]
        for c in range(pieces):
            kv = dot(e_ref[c], w)
            k = kv[:, :hw].astype(BF)
            v = (kv[:, hw:] + hb_ref[0, 3:4]).astype(BF)
            k_ref[0, c] = k
            v_ref[0, c] = v
            kt_ref[0, :, c * piece : (c + 1) * piece] = k.T
            vt_ref[0, :, c * piece : (c + 1) * piece] = v.T

    kv = sds((blocks, pieces, piece, hw), BF)
    kvt = sds((blocks, hw, total), BF)
    padded = sds((pieces, piece, width), BF)
    return call(
        body, "frame_keys", blocks,
        [(f, whole(f.shape)) for f in frames] + [*pack_in(pack), (head_bias, per_block(head_bias.shape))],
        [(kv, per_block(kv.shape))] * 2 + [(kvt, per_block(kvt.shape))] * 2 + [(padded, whole(padded.shape))],
        [pack_scratch(width)],
        4 * total * width * width,
        (place,),
        deps,
    )


def cross_forward(place, start, count, n2, first, pack, own, params, head_bias, keys, values_t, valid, dims, deps=(),
                  carried=()):
    seq, width, blocks, hw = dims
    heads = hw // HD
    _, pieces, piece, _ = keys.shape
    total_keys = pieces * piece

    def body(place_ref, n2_ref, first_ref, *refs):
        w_refs, refs = refs[: len(pack)], refs[len(pack) :]
        (prm_ref, hb_ref, k_ref, vt_ref, q_ref, lse_ref, ot_ref, mix_ref, second_ref, n3_ref, s_scr,
         p_scr, acc_scr, w_scr) = refs
        t = pl.program_id(0)
        assemble(w_refs, own, place_ref, w_scr)

        @pl.when(t == 0)
        def _():
            acc_scr[...] = first_ref[...] + prm_ref[13:14] if start == 0 else first_ref[...]

        q = ((dot(n2_ref[...], w_scr[:, 2 * hw : 3 * hw]) + hb_ref[0, 2:3]) * HD**-0.5).astype(BF)
        q_ref[0] = q
        row = lax.broadcasted_iota(jnp.int32, (piece, 1), 0)
        pad = jnp.where(row < valid, 0.0, NEGATIVE)

        for j in range(heads):
            qm = head_lanes(q, j, HD)

            def score(c, m):
                s = dot(k_ref[0, c], qm, 1, 1) + pad
                s_scr[c] = s
                return jnp.maximum(m, jnp.max(s, 0, keepdims=True))

            m = lax.fori_loop(0, pieces, score, jnp.full((1, seq), NEGATIVE, F32))

            def weigh(c, total):
                p = jnp.exp(s_scr[c] - m)
                p_scr[pl.ds(pl.multiple_of(c * piece, piece), piece)] = p.astype(BF)
                return total + jnp.sum(p, 0, keepdims=True)

            total = lax.fori_loop(0, pieces, weigh, jnp.zeros((1, seq), F32))
            lse_ref[0, j : j + 1] = m + jnp.log(total)
            at = j * HD
            ot_ref[0, at : at + HD] = dot(vt_ref[0, at : at + HD], p_scr[...]) / total

        mixed = ot_ref[0].T.astype(BF)
        mix_ref[0] = mixed
        acc_scr[...] += project_out(mixed, w_scr, hw)

        @pl.when(t == count - 1)
        def _():
            second = acc_scr[...]
            second_ref[...] = second
            unit, _ = layer_norm_parts(second)
            n3_ref[...] = (unit * prm_ref[2:3] + prm_ref[6:7]).astype(BF)

    full = whole((seq, width))
    hb = sds((blocks, seq, hw), BF)

    def block(shape):
        return at_block(shape, start)

    packs = pack_at(pack, start)
    return call(
        body, "cross_forward", count,
        [(n2, full), (first, full), *packs, (params, whole(params.shape)), (head_bias, block(head_bias.shape)),
         (keys, block(keys.shape)), (values_t, block(values_t.shape))],
        [(hb, block(hb.shape)), (sds((blocks, 8, seq), F32), block((blocks, 8, seq))),
         (sds((blocks, hw, seq), F32), block((blocks, hw, seq))), (hb, block(hb.shape)),
         (sds((seq, width), F32), full), (sds((seq, width), BF), full)],
        [pltpu.VMEM((pieces, piece, seq), F32), pltpu.VMEM((total_keys, seq), BF),
         pltpu.VMEM((seq, width), F32), pack_scratch(width)],
        count * (4 * seq * width * hw + 4 * seq * total_keys * 256 * heads),
        (place,),
        deps,
        carried,
    )


def feed_forward(place, n3, second, w_in, w_out, own, params, cotangent, dims, deps=()):
    seq, width, blocks, hw = dims

    def body(place_ref, n3_ref, second_ref, *refs):
        wi_refs, wo_refs, refs = refs[: len(w_in)], refs[len(w_in) : 2 * len(w_in)], refs[2 * len(w_in) :]
        (prm_ref, cot_ref, hid_ref, slope_ref, out_ref, g3_ref, b3_ref, sum_ref, wi_scr, wo_scr,
         acc_scr) = refs
        t = pl.program_id(0)
        assemble(wi_refs, own, place_ref, wi_scr)
        assemble(wo_refs, own, place_ref, wo_scr)

        @pl.when(t == 0)
        def _():
            acc_scr[...] = second_ref[...] + prm_ref[14:15]

        before = dot(n3_ref[...], wi_scr[...]) + prm_ref[pl.ds(15 + t, 1)]
        phi = 0.5 + 0.5 * lax.erf(before * 2**-0.5)
        hidden = (before * phi).astype(BF)
        hid_ref[0] = hidden
        slope_ref[0] = phi + before * (jnp.exp(-0.5 * before * before) * 0.3989422804014327)
        acc_scr[...] += dot(hidden, wo_scr[...], 1, 1)

        @pl.when(t == blocks - 1)
        def _():
            unit, inverse = layer_norm_parts(acc_scr[...])
            out_ref[...] = (unit * prm_ref[3:4] + prm_ref[7:8]).astype(BF)
            cot = cot_ref[...].astype(F32)
            grad = norm_back(cot, unit, inverse, prm_ref[3:4])
            g3_ref[...] = grad
            branch = grad.astype(BF)
            b3_ref[...] = branch
            sum_ref[...] = jnp.zeros_like(sum_ref)
            sum_ref[3:4] = column_sum(cot * unit)
            sum_ref[7:8] = column_sum(cot)
            sum_ref[14:15] = column_sum(branch.astype(F32))

    full = whole((seq, width))
    wide = (blocks, seq, width)
    return call(
        body, "feed_forward", blocks,
        [(n3, full), (second, full), *pack_in(w_in), *pack_in(w_out),
         (params, whole(params.shape)), (cotangent, full)],
        [(sds(wide, BF), per_block(wide)), (sds(wide, F32), per_block(wide)),
         (sds((seq, width), BF), full), (sds((seq, width), F32), full),
         (sds((seq, width), BF), full), (sds(params.shape, F32), whole(params.shape))],
        [pack_scratch(width), pack_scratch(width), pltpu.VMEM((seq, width), F32)],
        16 * seq * width * width,
        (place,),
        deps,
    )


def feed_out_grads(place, b3, hidden, grad_shape, dims, deps=()):
    seq, width, blocks, hw = dims

    def body(place_ref, b3_ref, hid_ref, *refs):
        grad_refs, (b3t_scr,) = refs[:-1], refs[-1:]

        @pl.when(pl.program_id(0) == 0)
        def _():
            b3t_scr[...] = b3_ref[...].T

        store_pack(grad_refs, dot(b3t_scr[...], hid_ref[0]).astype(BF), place_ref)

    wide = (blocks, seq, width)
    return call(
        body, "feed_out_grads", blocks,
        [(b3, whole((seq, width))), (hidden, per_block(wide))],
        grad_outs(grad_shape),
        [pltpu.VMEM((width, seq), BF)],
        8 * seq * width * width,
        (place,),
        deps,
    )


def feed_backward(place, b3, g3, slope, w_in, w_out, own, n3, second, params, sums, grad_shape, dims, deps=()):
    seq, width, blocks, hw = dims
    grads = grad_outs(grad_shape)

    def body(place_ref, b3_ref, g3_ref, slope_ref, *refs):
        wi_refs, wo_refs, refs = refs[: len(w_in)], refs[len(w_in) : 2 * len(w_in)], refs[2 * len(w_in) :]
        (n3_ref, second_ref, prm_ref, old_ref), refs = refs[:4], refs[4:]
        grad_refs, refs = refs[: len(grads)], refs[len(grads) :]
        g2_ref, b2_ref, sum_ref, wi_scr, wo_scr, n3t_scr, acc_scr = refs
        t = pl.program_id(0)
        assemble(wi_refs, own, place_ref, wi_scr)
        assemble(wo_refs, own, place_ref, wo_scr)

        @pl.when(t == 0)
        def _():
            sum_ref[...] = old_ref[...]
            n3t_scr[...] = n3_ref[...].T
            acc_scr[...] = jnp.zeros_like(acc_scr)

        grad_before = (dot(b3_ref[...], wo_scr[...]) * slope_ref[0]).astype(BF)
        sum_ref[pl.ds(15 + t, 1)] = column_sum(grad_before.astype(F32))
        store_pack(grad_refs, dot(n3t_scr[...], grad_before).astype(BF), place_ref)
        acc_scr[...] += dot(grad_before, wi_scr[...], 1, 1)

        @pl.when(t == blocks - 1)
        def _():
            grad = acc_scr[...]
            unit, inverse = layer_norm_parts(second_ref[...])
            sum_ref[2:3] = column_sum(grad * unit)
            sum_ref[6:7] = column_sum(grad)
            grad_second = g3_ref[...] + norm_back(grad, unit, inverse, prm_ref[2:3])
            g2_ref[...] = grad_second
            branch = grad_second.astype(BF)
            b2_ref[...] = branch
            sum_ref[13:14] = column_sum(branch.astype(F32))

    full = whole((seq, width))
    wide = (blocks, seq, width)
    return call(
        body, "feed_backward", blocks,
        [(b3, full), (g3, full), (slope, per_block(wide)), *pack_in(w_in), *pack_in(w_out), (n3, full),
         (second, full), (params, whole(params.shape)), (sums, whole(sums.shape))],
        grads
        + [(sds((seq, width), F32), full), (sds((seq, width), BF), full),
           (sds(sums.shape, F32), whole(sums.shape))],
        [pack_scratch(width), pack_scratch(width), pltpu.VMEM((width, seq), BF), pltpu.VMEM((seq, width), F32)],
        24 * seq * width * width,
        (place,),
        deps,
    )


def cross_attend_back(place, start, count, sums, b2, queries, keys, values, keys_t, lse, ot, pack, own, valid,
                      dims, deps=(), carried=()):
    seq, width, blocks, hw = dims
    heads = hw // HD
    _, pieces, piece, _ = keys.shape
    total_keys = pieces * piece

    def body(place_ref, old_ref, b2_ref, q_ref, k_ref, v_ref, kt_ref, lse_ref, ot_ref, *refs):
        w_refs, refs = refs[: len(pack)], refs[len(pack) :]
        dq_ref, dkv_ref, sum_ref, w_scr, dk_scr, dv_scr, ds_scr, dqt_scr = refs
        t = pl.program_id(0)
        assemble(w_refs, own, place_ref, w_scr)

        @pl.when(t == 0)
        def _():
            sum_ref[...] = old_ref[...]

        q = q_ref[0]
        gm = project_back(b2_ref[...], w_scr, hw).astype(BF)
        weighted = gm.astype(F32).T * ot_ref[0]
        row = lax.broadcasted_iota(jnp.int32, (piece, 1), 0)
        pad = jnp.where(row < valid, 0.0, NEGATIVE)
        dk_scr[...] = jnp.zeros_like(dk_scr)
        dv_scr[...] = jnp.zeros_like(dv_scr)
        for j in range(heads):
            delta = jnp.sum(weighted[j * HD : (j + 1) * HD], 0, keepdims=True)
            shift = lse_ref[0, j : j + 1]
            qm = head_lanes(q, j, HD)
            gj = head_lanes(gm, j, HD)

            def one_piece(c, carry):
                s = dot(k_ref[0, c], qm, 1, 1) + pad
                p = jnp.exp(s - shift)
                ds = (p * (dot(v_ref[0, c], gj, 1, 1) - delta)).astype(BF)
                dv_scr[c] += dot(p.astype(BF), gj)
                dk_scr[c] += dot(ds, qm)
                ds_scr[pl.ds(pl.multiple_of(c * piece, piece), piece)] = ds
                return carry

            lax.fori_loop(0, pieces, one_piece, 0)
            dqt_scr[j * HD : (j + 1) * HD] = dot(kt_ref[0, j * HD : (j + 1) * HD], ds_scr[...])
        dq = dqt_scr[...].T.astype(BF).astype(F32) * HD**-0.5
        put_heads(sum_ref, 11, start + t, blocks, column_sum(dq))
        dq_ref[0] = dq.astype(BF)
        bias = jnp.zeros((1, hw), F32)
        for c in range(pieces):
            dv = dv_scr[c].astype(BF)
            bias += column_sum(dv.astype(F32))
            dkv_ref[0, c] = jnp.concatenate([dk_scr[c].astype(BF), dv], 1)
        put_heads(sum_ref, 12, start + t, blocks, bias)

    def block(shape):
        return at_block(shape, start)

    packs = pack_at(pack, start)
    dkv = (blocks, pieces, piece, 2 * hw)
    return call(
        body, "cross_attend_back", count,
        [(sums, whole(sums.shape)), (b2, whole((seq, width))), (queries, block(queries.shape)), (keys, block(keys.shape)),
         (values, block(values.shape)), (keys_t, block(keys_t.shape)), (lse, block(lse.shape)),
         (ot, block(ot.shape)), *packs],
        [(sds(queries.shape, BF), block(queries.shape)), (sds(dkv, BF), block(dkv)),
         (sds(sums.shape, F32), whole(sums.shape))],
        [pack_scratch(width), pltpu.VMEM((pieces, piece, hw), F32), pltpu.VMEM((pieces, piece, hw), F32),
         pltpu.VMEM((total_keys, seq), BF), pltpu.VMEM((hw, seq), F32)],
        count * (2 * seq * width * hw + 10 * seq * total_keys * 256 * heads // 2),
        (place,),
        deps,
        carried,
    )


def cross_rows_back(place, sums, dq, dkv, g2, first, pack, own, params, valid, dims, deps=()):
    seq, width, blocks, hw = dims
    _, pieces, piece, _ = dkv.shape
    frames = (pieces, piece, width)
    kept = (valid, width)

    def body(place_ref, old_ref, dq_ref, dkv_ref, g2_ref, first_ref, *refs):
        w_refs, refs = refs[: len(pack)], refs[len(pack) :]
        prm_ref, *genc_refs, g1_ref, b1_ref, sum_ref, w_scr, genc_scr, acc_scr = refs
        t = pl.program_id(0)
        assemble(w_refs, own, place_ref, w_scr)

        @pl.when(t == 0)
        def _():
            acc_scr[...] = jnp.zeros_like(acc_scr)
            genc_scr[...] = jnp.zeros_like(genc_scr)
            sum_ref[...] = old_ref[...]

        wkv = w_scr[:, : 2 * hw]
        for c in range(pieces):
            genc_scr[c] += dot(dkv_ref[0, c], wkv, 1, 1)
        acc_scr[...] += dot(dq_ref[0], w_scr[:, 2 * hw : 3 * hw], 1, 1)

        @pl.when(t == blocks - 1)
        def _():
            for c in range(pieces):
                genc_refs[c][...] = genc_scr[c, :valid].astype(BF)
            grad = acc_scr[...]
            unit, inverse = layer_norm_parts(first_ref[...])
            sum_ref[1:2] = column_sum(grad * unit)
            sum_ref[5:6] = column_sum(grad)
            grad_first = g2_ref[...] + norm_back(grad, unit, inverse, prm_ref[1:2])
            g1_ref[...] = grad_first
            branch = grad_first.astype(BF)
            b1_ref[...] = branch
            sum_ref[10:11] = column_sum(branch.astype(F32))

    full = whole((seq, width))
    return call(
        body, "cross_rows_back", blocks,
        [(sums, whole(sums.shape)), (dq, per_block(dq.shape)), (dkv, per_block(dkv.shape)), (g2, full), (first, full), *pack_in(pack),
         (params, whole(params.shape))],
        [(sds(kept, BF), whole(kept))] * pieces
        + [(sds((seq, width), F32), full), (sds((seq, width), BF), full),
         (sds(sums.shape, F32), whole(sums.shape))],
        [pack_scratch(width), pltpu.VMEM(frames, F32), pltpu.VMEM((seq, width), F32)],
        2 * seq * width * width + 4 * pieces * piece * width * width,
        (place,),
        deps,
    )


def cross_grads(place, dq, dkv, mixed, b2, n2, frames, grad_shape, dims, deps=()):
    seq, width, blocks, hw = dims
    _, pieces, piece, _ = dkv.shape
    total_keys = pieces * piece

    def body(place_ref, dq_ref, dkv_ref, mix_ref, b2_ref, n2_ref, e_ref, *refs):
        grad_refs, (et_scr, b2t_scr, n2t_scr) = refs[:-3], refs[-3:]

        @pl.when(pl.program_id(0) == 0)
        def _():
            for c in range(pieces):
                et_scr[:, c * piece : (c + 1) * piece] = e_ref[c].T
            b2t_scr[...] = b2_ref[...].T
            n2t_scr[...] = n2_ref[...].T

        grad_kv = dot(et_scr[...], dkv_ref[0].reshape(total_keys, 2 * hw))
        grad_q = dot(n2t_scr[...], dq_ref[0])
        grad_o = dot(b2t_scr[...], mix_ref[0])
        store_pack(grad_refs, jnp.concatenate([grad_kv, grad_q, grad_o], 1).astype(BF), place_ref)

    full = whole((seq, width))
    return call(
        body, "cross_grads", blocks,
        [(dq, per_block(dq.shape)), (dkv, per_block(dkv.shape)), (mixed, per_block(mixed.shape)), (b2, full),
         (n2, full), (frames, whole(frames.shape))],
        grad_outs(grad_shape),
        [pltpu.VMEM((width, total_keys), BF), pltpu.VMEM((width, seq), BF), pltpu.VMEM((width, seq), BF)],
        4 * seq * width * width + 4 * total_keys * width * width,
        (place,),
        deps,
    )


def self_attend_back(length, place, sums, b1, n1, queries, keys, values, mixed, lse, ot, pack, own, grad_shape, dims,
                     deps=()):
    seq, width, blocks, hw = dims
    heads = hw // HD
    grads = grad_outs(grad_shape)

    def body(len_ref, place_ref, old_ref, b1_ref, n1_ref, q_ref, k_ref, v_ref, mix_ref, lse_ref, ot_ref, *refs):
        w_refs, refs = refs[: len(pack)], refs[len(pack) :]
        grad_refs, refs = refs[: len(grads)], refs[len(grads) :]
        dqkv_ref, sum_ref, w_scr, bias_scr, dqt_scr, b1t_scr, n1t_scr = refs
        t = pl.program_id(0)
        assemble(w_refs, own, place_ref, w_scr)

        @pl.when(t == 0)
        def _():
            sum_ref[...] = old_ref[...]
            b1t_scr[...] = b1_ref[...].T
            n1t_scr[...] = n1_ref[...].T
            key = lax.broadcasted_iota(jnp.int32, (seq, seq), 0)
            query = lax.broadcasted_iota(jnp.int32, (seq, seq), 1)
            bias_scr[...] = jnp.where((key <= query) & (key < len_ref[0]), 0.0, NEGATIVE)

        q = q_ref[0]
        k = k_ref[0]
        v = v_ref[0]
        kt = k.T
        gm = project_back(b1_ref[...], w_scr, hw).astype(BF)
        weighted = gm.astype(F32).T * ot_ref[0]
        dk = jnp.zeros((seq, hw), F32)
        dv = jnp.zeros((seq, hw), F32)
        for j in range(heads):
            delta = jnp.sum(weighted[j * HD : (j + 1) * HD], 0, keepdims=True)
            qm = head_lanes(q, j, HD)
            gj = head_lanes(gm, j, HD)
            p = jnp.exp(dot(k, qm, 1, 1) + bias_scr[...] - lse_ref[0, j : j + 1])
            ds = (p * (dot(v, gj, 1, 1) - delta)).astype(BF)
            dv += dot(p.astype(BF), gj)
            dk += dot(ds, qm)
            dqt_scr[j * HD : (j + 1) * HD] = dot(kt[j * HD : (j + 1) * HD], ds)
        dq = dqt_scr[...].T.astype(BF).astype(F32) * HD**-0.5
        dv = dv.astype(BF)
        put_heads(sum_ref, 8, t, blocks, column_sum(dq))
        put_heads(sum_ref, 9, t, blocks, column_sum(dv.astype(F32)))
        dqkv = jnp.concatenate([dq.astype(BF), dk.astype(BF), dv], 1)
        dqkv_ref[0] = dqkv
        grad = jnp.concatenate([dot(n1t_scr[...], dqkv), dot(b1t_scr[...], mix_ref[0])], 1)
        store_pack(grad_refs, grad.astype(BF), place_ref)

    hb = per_block((blocks, seq, hw))
    dqkv = (blocks, seq, 3 * hw)
    return call(
        body, "self_attend_back", blocks,
        [(sums, whole(sums.shape)), (b1, whole((seq, width))), (n1, whole((seq, width))), (queries, hb), (keys, hb),
         (values, hb), (mixed, hb), (lse, per_block(lse.shape)), (ot, per_block(ot.shape)), *pack_in(pack)],
        grads + [(sds(dqkv, BF), per_block(dqkv)), (sds(sums.shape, F32), whole(sums.shape))],
        [pack_scratch(width), pltpu.VMEM((seq, seq), F32), pltpu.VMEM((hw, seq), F32), pltpu.VMEM((width, seq), BF),
         pltpu.VMEM((width, seq), BF)],
        10 * seq * width * width + 40 * seq * seq * width,
        (length, place),
        deps,
    )


def self_rows_back(place, sums, dqkv, g1, rows, pack, own, params, dims, deps=()):
    seq, width, blocks, hw = dims

    def body(place_ref, old_ref, dqkv_ref, g1_ref, x_ref, *refs):
        w_refs, refs = refs[: len(pack)], refs[len(pack) :]
        prm_ref, gin_ref, sum_ref, w_scr, acc_scr = refs
        t = pl.program_id(0)
        assemble(w_refs, own, place_ref, w_scr)

        @pl.when(t == 0)
        def _():
            acc_scr[...] = jnp.zeros_like(acc_scr)
            sum_ref[...] = old_ref[...]

        acc_scr[...] += dot(dqkv_ref[0], w_scr[:, : 3 * hw], 1, 1)

        @pl.when(t == blocks - 1)
        def _():
            grad = acc_scr[...]
            unit, inverse = layer_norm_parts(x_ref[...].astype(F32))
            sum_ref[0:1] = column_sum(grad * unit)
            sum_ref[4:5] = column_sum(grad)
            gin_ref[...] = g1_ref[...] + norm_back(grad, unit, inverse, prm_ref[0:1])

    full = whole((seq, width))
    return call(
        body, "self_rows_back", blocks,
        [(sums, whole(sums.shape)), (dqkv, per_block(dqkv.shape)), (g1, full), (rows, full), *pack_in(pack), (params, whole(params.shape))],
        [(sds((seq, width), F32), full), (sds(sums.shape, F32), whole(sums.shape))],
        [pack_scratch(width), pltpu.VMEM((seq, width), F32)],
        6 * seq * width * width,
        (place,),
        deps,
    )


def pad_rows(rows, count):
    return jnp.pad(rows, ((0, count - rows.shape[0]),) + ((0, 0),) * (rows.ndim - 1))


def swap(array, step):
    count = lax.axis_size("fsdp")
    return lax.ppermute(array, "fsdp", [(i, i ^ step) for i in range(count)])


def around(array, hop):
    count = lax.axis_size("tp")
    return lax.ppermute(array, "tp", [(i, (i + hop) % count) for i in range(count)])


def native_gather(shard):
    whole_pack = lax.all_gather(shard, ("fsdp", "tp"), axis=0, tiled=False)
    return whole_pack.reshape((lax.axis_size("fsdp"), lax.axis_size("tp")) + shard.shape)


def in_order(pieces, here):
    count = len(pieces)
    stacked = jnp.stack(pieces)
    return jnp.stack(
        [lax.dynamic_index_in_dim(stacked, (here - t) % count, 0, keepdims=False) for t in range(count)]
    )


def gate(array, things):
    return lax.optimization_barrier((array,) + tuple(things))[0] if things else array


class Gather:
    def __init__(self, shard):
        self.shard = shard

    def direct(self):
        come = [around(self.shard, hop) for hop in range(1, 4)]
        line = in_order([self.shard] + come, lax.axis_index("tp"))
        self.low, self.high = line[None, :2], line[None, 2:]
        return tuple(come)

    def first(self):
        self.low_x, self.high_y = swap(self.low, 2), swap(self.high, 4)
        return self.low_x, self.high_y

    def second(self):
        self.low_two = jnp.concatenate([self.low, self.low_x])
        self.high_two = jnp.concatenate([self.high, self.high_y])
        self.low_y, self.high_x = swap(self.low_two, 4), swap(self.high_two, 2)
        return self.low_y, self.high_x

    def core(self):
        low = jnp.concatenate([self.low_two, self.low_y])
        high = jnp.stack([self.high_two[0], self.high_x[0], self.high_two[1], self.high_x[1]])
        mine = jnp.concatenate([low, high], 1)
        self.pack = (mine, swap(mine, 1))
        return self.pack[1:]


def wide(array):
    return array.astype(F32)


class Scatter:
    def __init__(self, halves):
        self.kept, self.sent = halves
        self.tp = self.kept.shape[1]
        self.half = self.tp // 2

    def core(self):
        self.come = swap(self.sent, 1)
        return self.come

    def first(self):
        def both(q, t):
            return (wide(self.kept[q, t]) + wide(self.come[q, t])).astype(BF)

        low, high = slice(0, self.half), slice(self.half, self.tp)
        self.low_y = swap(both(slice(2, 4), low), 4)
        self.high_x = swap(both(slice(1, 4, 2), high), 2)
        return self.low_y, self.high_x

    def second(self):
        low, high = slice(0, self.half), slice(self.half, self.tp)

        def three(q, t, more):
            return wide(self.kept[q, t]) + wide(self.come[q, t]) + wide(more)

        self.low_x = swap(three(1, low, self.low_y[1]).astype(BF), 2)
        self.high_y = swap(three(2, high, self.high_x[1]).astype(BF), 4)
        return self.low_x, self.high_y

    def sides(self):
        def total(t, more, last):
            return wide(self.kept[0, t]) + wide(self.come[0, t]) + wide(more) + wide(last)

        low, high = slice(0, self.half), slice(self.half, self.tp)
        self.sums = jnp.concatenate(
            [total(low, self.low_y[0], self.low_x), total(high, self.high_x[0], self.high_y)]
        ).astype(BF)
        self.own = lax.dynamic_index_in_dim(self.sums, lax.axis_index("tp"), 0, keepdims=False)
        self.parts = [self.part(hop) for hop in range(1, self.tp, 2)]
        return tuple(self.parts)

    def across(self):
        more = [self.part(hop) for hop in range(2, self.tp, 2)]
        self.parts += more
        return tuple(more)

    def line(self):
        return self.sides() + self.across()

    def part(self, hop):
        place = (lax.axis_index("tp") + hop) % self.tp
        return around(lax.dynamic_index_in_dim(self.sums, place, 0, keepdims=False), hop)

    def total(self):
        result = wide(self.own)
        for part in self.parts:
            result += wide(part)
        return result


def butterfly_scatter(grads, own, narrow=BF):
    fsdp, tp = lax.axis_size("fsdp"), lax.axis_size("tp")
    if grads.shape[0] != fsdp:
        blocks, width = grads.shape[1], grads.shape[3]
        grads = grads.reshape(blocks, fsdp, own, width).transpose(1, 0, 2, 3)
    place = lax.axis_index("fsdp")
    step = 1
    while step < fsdp:
        pairs = grads.reshape((grads.shape[0] // 2, 2) + grads.shape[1:])
        bit = (place // step) % 2
        kept = lax.dynamic_index_in_dim(pairs, bit, 1, keepdims=False)
        sent = lax.dynamic_index_in_dim(pairs, 1 - bit, 1, keepdims=False)
        grads = (wide(kept) + wide(swap(sent, step))).astype(narrow)
        step *= 2
    grads = grads[0]
    here = lax.axis_index("tp")
    total = wide(lax.dynamic_index_in_dim(grads, here, 0, keepdims=False))
    for hop in range(1, tp):
        sent = lax.dynamic_index_in_dim(grads, (here + hop) % tp, 0, keepdims=False)
        total += wide(around(sent, hop))
    return total


def local(
    inputs,
    encoder,
    lengths,
    self_qkv,
    self_out,
    cross_q,
    cross_kv,
    cross_out,
    fc_in,
    fc_out,
    norm_gain,
    norm_bias,
    proj_bias,
    fc_in_bias,
    cotangent,
):
    fsdp, tp = lax.axis_size("fsdp"), lax.axis_size("tp")
    devices = fsdp * tp
    tp_place = lax.axis_index("tp")
    place = jnp.stack([lax.axis_index("fsdp"), tp_place])
    seqs, seq, width = inputs.shape
    assert seqs == 1
    own, hw = cross_q.shape
    dims = (seq, width, tp, hw)
    frames_own = encoder.shape[1]
    small_own = norm_gain.shape[1]
    ff_own = fc_in_bias.shape[0]
    chained = fsdp == 8 and tp == 4 and own % 16 == 0

    small = jnp.concatenate(
        [a.reshape(-1) for a in (norm_gain, norm_bias, proj_bias, fc_in_bias)]
    )
    small = jnp.pad(small, (0, width - small.size))
    high = small.astype(BF)
    low = (small - high.astype(F32)).astype(BF)
    extra = pad_rows(jnp.stack([high, low]), 16)

    pack_self = jnp.concatenate([self_qkv[0], self_qkv[1], self_qkv[2], self_out.T], 1)
    pack_self = jnp.concatenate([pack_self, extra], 0)
    pack_cross = jnp.concatenate([cross_kv[0], cross_kv[1], cross_q, cross_out.T], 1)
    x = inputs[0]
    length = lax.dynamic_slice_in_dim(lengths, tp_place, 1)
    chains = {}
    sends = {"direct": "shard", "first": "low high", "second": "low_x high_y", "core": "low_y high_x"}

    def move(after, *steps):
        out = ()
        for text in steps if chained else ():
            name, step = text.split(".")
            chain = chains[name]
            for array in sends[step].split():
                setattr(chain, array, gate(getattr(chain, array), after))
            out += getattr(chain, step)()
        return out

    frames = [
        lax.dynamic_index_in_dim(encoder, (tp_place + hop) % tp, 0, keepdims=False) for hop in range(tp)
    ]
    before = turn = ()
    if chained:
        for name, shard in (("self", pack_self), ("cross", pack_cross), ("in", fc_in), ("out", fc_out.T)):
            chains[name] = Gather(shard)
        turn = move((), "self.direct") + tuple(frames)
        turn = move(turn, "self.first", "cross.direct")
        turn = move(turn, "self.second", "in.direct")
        frames[1] = around(gate(frames[1], turn), 1)
        before = turn = move(turn, "self.core", "cross.first")
        frames[2] = around(gate(frames[2], turn), 2)
        turn = move(turn, "cross.second", "in.first") + (frames[1], frames[2])
        w_self = chains["self"].pack
        own_rows = own
        grad_shape = (fsdp // 2, tp, own, width)
        blocks = jnp.stack([part[:, :, own : own + 2] for part in w_self], 1)
        blocks = blocks.reshape(fsdp, tp, 2, width)
        table = jnp.stack(
            [lax.dynamic_index_in_dim(blocks, f ^ place[0], 0, keepdims=False) for f in range(fsdp)]
        )
        table = wide(table).sum(2).reshape(devices, width)
    else:
        w_self = native_gather(pack_self)
        table = wide(w_self[:, :, own : own + 2]).sum(2).reshape(devices, width)
        own_rows = own * fsdp
        grad_shape = (1, tp, own_rows, width)

        def end_to_end(pack):
            return pack[:, :, :own].transpose(1, 0, 2, 3).reshape(1, tp, own_rows, width)

        w_self = (end_to_end(w_self),)
        w_cross = (end_to_end(native_gather(pack_cross)),)
        w_in = (end_to_end(native_gather(fc_in)),)
        w_out = (end_to_end(native_gather(fc_out.T)),)

    rows = norm_gain.shape[0] + norm_bias.shape[0] + proj_bias.shape[0]
    params = table[:, : rows * small_own].reshape(devices, rows, small_own)
    params = params.transpose(1, 0, 2).reshape(rows, width)
    fc_bias = table[:, rows * small_own : rows * small_own + ff_own].reshape(tp, width)
    head_bias = jnp.stack([params[8], params[9], params[11], params[12]])
    head_bias = head_bias.reshape(4, tp, hw).transpose(1, 0, 2)
    head_bias = jnp.pad(head_bias, ((0, 0), (0, 4), (0, 0)))
    params = pad_rows(jnp.concatenate([params, fc_bias], 0), 24)

    piece = -(-frames_own // 128) * 128
    half = tp // 2

    q1, k1, v1, lse1, ot1, mixed1, n1, first, n2 = self_forward(
        length, place, 0, tp, x, x, w_self, own_rows, params, head_bias, dims, before
    )
    turn += (n2,)
    if chained:
        frames[3] = around(gate(frames[3], turn), 3)
        turn = move(turn, "cross.core", "in.second") + (frames[3],)
        w_cross = chains["cross"].pack
    else:
        frames = [around(array, hop) if hop else array for hop, array in enumerate(frames)]
    k2, v2, k2t, v2t, frames = frame_keys(place, frames, w_cross, own_rows, head_bias, piece, dims, turn)
    turn = move(turn, "in.core", "out.direct") + (k2,)
    shared = (w_cross, own_rows, params, head_bias, k2, v2t, frames_own, dims)
    *kept, part, _ = cross_forward(place, 0, half, n2, first, *shared, turn)
    turn = move(turn, "out.first") + (part,)
    q2, lse2, ot2, mixed2, second, n3 = cross_forward(place, half, tp - half, n2, part, *shared, turn, kept)
    turn = move(turn, "out.second") + (n3,)
    move(turn, "out.core")
    if chained:
        w_in, w_out = chains["in"].pack, chains["out"].pack
    hidden, slope, layer_out, g3, b3, sums = feed_forward(
        place, n3, second, w_in, w_out, own_rows, params, cotangent[0], dims
    )
    scatters = {}

    def begin(name, halves):
        if chained:
            scatters[name] = Scatter(halves)

    def go(name, step):
        if not chained:
            return ()
        out = getattr(scatters[name], step)()
        return out if isinstance(out, tuple) else (out,)

    grad_out = feed_out_grads(place, b3, hidden, grad_shape, dims)
    begin("out", grad_out)
    step1 = go("out", "core")
    *grad_in, g2, b2, sums = feed_backward(
        place, b3, g3, slope, w_in, w_out, own_rows, n3, second, params, sums, grad_shape, dims, (grad_out[0],)
    )
    begin("in", grad_in)
    step2 = go("out", "first") + go("in", "core")
    shared = (b2, q2, k2, v2, k2t, lse2, ot2, w_cross, own_rows, frames_own, dims)
    *kept, sums = cross_attend_back(place, 0, half, sums, *shared, step1)
    step3 = go("out", "second") + go("in", "first")
    dq2, dkv2, sums = cross_attend_back(place, half, tp - half, sums, *shared, step2, kept)
    grad_cross = cross_grads(place, dq2, dkv2, mixed2, b2, n2, frames, grad_shape, dims, step3)
    step4 = go("out", "line") + go("in", "second")
    begin("cross", grad_cross)
    step5 = go("cross", "core")
    *grad_frames, g1, b1, sums = cross_rows_back(
        place, sums, dq2, dkv2, g2, first, w_cross, own_rows, params, frames_own, dims, step4 + (grad_cross[0],)
    )
    step5 += go("in", "line")
    backs = [around(gate(grad_frames[c], step5), tp - c) if c % 2 else grad_frames[c] for c in range(tp)]
    step6 = go("cross", "first") + tuple(backs[1::2])
    *grad_self, dqkv1, sums = self_attend_back(
        length, place, sums, b1, n1, q1, k1, v1, mixed1, lse1, ot1, w_self, own_rows, grad_shape, dims, step5
    )
    begin("self", grad_self)
    go("self", "core")
    grad_inputs, sums = self_rows_back(
        place, sums, dqkv1, g1, x, w_self, own_rows, params, dims, step6 + (grad_self[0],)
    )

    for c in range(2, tp, 2):
        backs[c] = around(gate(backs[c], step6 + (grad_self[0],)), tp - c)

    turns = [()]
    if chained:
        scatters["cross"].low_y = gate(scatters["cross"].low_y, (grad_self[0],))
        step7 = go("cross", "second")
        scatters["self"].come = gate(scatters["self"].come, (sums, *step7))
        turns = [go("self", "first")]
        scatters["cross"].low_x = gate(scatters["cross"].low_x, (sums, *step7))
        go("cross", "sides")
        for name in ("out", "in"):
            scatters[name].own = gate(scatters[name].own, turns[0])
        scatters["self"].low_y = gate(scatters["self"].low_y, (backs[2],))
        turns.append(go("self", "second"))
        scatters["cross"].sums = gate(scatters["cross"].sums, turns[0])
        scatters["self"].low_x = gate(scatters["self"].low_x, go("cross", "across"))
    sums = gate(sums, turns[0])
    sums = sums + swap(sums, 1)
    sums = sum([around(sums, hop) for hop in range(1, tp)], sums)
    sums = gate(sums, turns[-1])
    step = 2
    while step < fsdp:
        sums = sums + swap(sums, step)
        step *= 2
    frames_back = in_order([backs[-hop % tp] for hop in range(tp)], tp_place)
    device = lax.axis_index("fsdp") * tp + tp_place
    mine = lax.dynamic_slice_in_dim(sums[:rows], device * small_own, small_own, 1)
    gains = norm_gain.shape[0]
    own_gain, own_shift, own_bias = mine[:gains], mine[gains : 2 * gains], mine[2 * gains :]
    per_row = width // ff_own
    own_fc_bias = lax.dynamic_slice(
        sums, (rows + device // per_row, (device % per_row) * ff_own), (1, ff_own)
    )[0]

    if chained:
        go("self", "line")
        total_out, total_in, total_cross, total_self = (
            scatters[name].total() for name in ("out", "in", "cross", "self")
        )
    else:
        total_out, total_in, total_cross, total_self = (
            butterfly_scatter(grads[0], own) for grads in (grad_out, grad_in, grad_cross, grad_self)
        )

    def part(total, index):
        return total[:, index * hw : (index + 1) * hw]

    return (
        layer_out[None],
        grad_inputs[None],
        frames_back.astype(F32),
        jnp.stack([part(total_self, 0), part(total_self, 1), part(total_self, 2)]),
        part(total_self, 3).T,
        part(total_cross, 2),
        jnp.stack([part(total_cross, 0), part(total_cross, 1)]),
        part(total_cross, 3).T,
        total_in,
        total_out.T,
        own_gain,
        own_shift,
        own_bias,
        own_fc_bias,
    )


def solution(mesh):
    return jax.shard_map(
        local,
        mesh=mesh,
        in_specs=(
            P(("fsdp", "tp"), None, None),
            P("fsdp", "tp", None),
            P("fsdp"),
            P(None, "fsdp", "tp"),
            P("tp", "fsdp"),
            P("fsdp", "tp"),
            P(None, "fsdp", "tp"),
            P("tp", "fsdp"),
            P("fsdp", "tp"),
            P("tp", "fsdp"),
            P(None, ("fsdp", "tp")),
            P(None, ("fsdp", "tp")),
            P(None, ("fsdp", "tp")),
            P(("fsdp", "tp")),
            P(("fsdp", "tp"), None, None),
        ),
        out_specs=(
            P(("fsdp", "tp"), None, None),
            P(("fsdp", "tp"), None, None),
            P("fsdp", "tp", None),
            P(None, "fsdp", "tp"),
            P("tp", "fsdp"),
            P("fsdp", "tp"),
            P(None, "fsdp", "tp"),
            P("tp", "fsdp"),
            P("fsdp", "tp"),
            P("tp", "fsdp"),
            P(None, ("fsdp", "tp")),
            P(None, ("fsdp", "tp")),
            P(None, ("fsdp", "tp")),
            P(("fsdp", "tp")),
        ),
        check_vma=False,
    )
```

```python
import functools

import jax
import jax.numpy as jnp
from jax import lax
from jax.experimental import pallas as pl
from jax.experimental.pallas import tpu as pltpu
from jax.sharding import PartitionSpec as P

HD = 64
EPSILON = 1e-05
NEGATIVE = -1e30
VMEM_LIMIT = 60 * 2**20
HINT = 20
BF = jnp.bfloat16
F32 = jnp.float32


def dot(left, right, left_dim=1, right_dim=0):
    return lax.dot_general(
        left, right, (((left_dim,), (right_dim,)), ((), ())), preferred_element_type=F32
    )


def layer_norm_parts(rows):
    center = rows - jnp.mean(rows, -1, keepdims=True)
    inverse = lax.rsqrt(jnp.mean(center * center, -1, keepdims=True) + EPSILON)
    return center * inverse, inverse


def norm_back(grad_rows, unit, inverse, gain):
    scaled = grad_rows * gain
    return inverse * (
        scaled
        - jnp.mean(scaled, -1, keepdims=True)
        - unit * jnp.mean(scaled * unit, -1, keepdims=True)
    )


def put_heads(sum_ref, row, block, count, value):
    size = value.shape[1]
    for t in range(count):

        @pl.when(block == t)
        def _():
            sum_ref[row : row + 1, t * size : (t + 1) * size] = value


def column_sum(rows):
    return jnp.sum(rows, 0, keepdims=True)


def whole(shape):
    zeros = (0,) * len(shape)
    return pl.BlockSpec(shape, lambda t, *_: zeros)


def per_block(shape):
    rest = (0,) * (len(shape) - 1)
    return pl.BlockSpec((1,) + tuple(shape[1:]), lambda t, *_: (t,) + rest)


def packed(shape):
    return pl.BlockSpec((shape[0], 1) + tuple(shape[2:]), lambda t, *_: (0, t, 0, 0))


def sds(shape, dtype):
    return jax.ShapeDtypeStruct(tuple(shape), dtype)


def call(body, name, grid, ins, outs, scratch, flops, scalars=(), deps=(), carried=()):
    moved = sum(a.size * a.dtype.itemsize for a, _ in ins)
    moved += sum(o.size * o.dtype.itemsize for o, _ in outs)
    first = len(scalars) + len(ins)
    extra = list(carried) + list(deps)

    def inner(*refs):
        return body(*refs[:first], *refs[first + len(extra) :])

    return pl.pallas_call(
        inner,
        out_shape=[o for o, _ in outs],
        grid_spec=pltpu.PrefetchScalarGridSpec(
            num_scalar_prefetch=len(scalars),
            grid=(grid,),
            in_specs=[s for _, s in ins] + [pl.BlockSpec(memory_space=pl.ANY)] * len(extra),
            out_specs=[s for _, s in outs],
            scratch_shapes=scratch,
        ),
        compiler_params=pltpu.CompilerParams(
            dimension_semantics=("arbitrary",), vmem_limit_bytes=VMEM_LIMIT
        ),
        input_output_aliases={first + i: i for i in range(len(carried))},
        cost_estimate=pl.CostEstimate(flops=HINT * flops, bytes_accessed=moved, transcendentals=0),
        name=name,
    )(*scalars, *[a for a, _ in ins], *extra)


def head_lanes(rows, head, block):
    lane = lax.broadcasted_iota(jnp.int32, rows.shape, 1)
    return jnp.where((lane >= head * block) & (lane < (head + 1) * block), rows, jnp.zeros_like(rows))


def pack_in(pack):
    return pack_at(pack, 0)


def at_block(shape, start):
    rest = (0,) * (len(shape) - 1)
    return pl.BlockSpec((1,) + tuple(shape[1:]), lambda t, *_: (start + t,) + rest)


def pack_at(pack, start):
    return [
        (a, pl.BlockSpec((a.shape[0], 1) + a.shape[2:], lambda t, *_: (0, start + t, 0, 0))) for a in pack
    ]


def pack_scratch(width):
    return pltpu.VMEM((width, width), BF)


def assemble(refs, rows, place_ref, scr):
    if len(refs) == 1:
        parts = refs[0][:, 0, :rows, :]
        scr[...] = parts.reshape(parts.shape[0] * rows, parts.shape[2])
        return
    count = 2 * refs[0].shape[0]
    for f in range(count):
        distance = f ^ place_ref[0]
        source = distance >> 1
        for bit in range(2):

            @pl.when((distance & 1) == bit)
            def _():
                scr[f * rows : (f + 1) * rows] = refs[bit][source, 0, :rows, :]


def grad_outs(shape):
    return [(sds(shape, BF), packed(shape))] * (1 if shape[0] == 1 else 2)


def store_pack(refs, value, place_ref):
    rows = refs[0].shape[2]
    if len(refs) == 1:
        refs[0][0, 0] = value
        return
    for f in range(2 * refs[0].shape[0]):
        distance = f ^ place_ref[0]
        target = distance >> 1
        for bit in range(2):

            @pl.when((distance & 1) == bit)
            def _():
                refs[bit][target, 0] = value[f * rows : (f + 1) * rows]


def tail_start(hw):
    return (3 * hw) // 128 * 128


def project_out(mixed, w_scr, hw):
    start = tail_start(hw)
    extra = 3 * hw - start
    if extra:
        mixed = jnp.concatenate([jnp.zeros((mixed.shape[0], extra), mixed.dtype), mixed], 1)
    return dot(mixed, w_scr[:, start:], 1, 1)


def project_back(branch, w_scr, hw):
    start = tail_start(hw)
    return dot(branch, w_scr[:, start:])[:, 3 * hw - start :]


def self_forward(length, place, start, count, rows, part, pack, own, params, head_bias, dims, deps=(), carried=()):
    seq, width, blocks, hw = dims
    heads = hw // HD

    def body(len_ref, place_ref, x_ref, part_ref, *refs):
        w_refs, refs = refs[: len(pack)], refs[len(pack) :]
        (prm_ref, hb_ref, q_ref, k_ref, v_ref, lse_ref, ot_ref, mix_ref, n1_ref, first_ref, n2_ref,
         bias_scr, acc_scr, w_scr) = refs
        t = pl.program_id(0)
        assemble(w_refs, own, place_ref, w_scr)

        @pl.when(t == 0)
        def _():
            unit, _ = layer_norm_parts(x_ref[...].astype(F32))
            n1_ref[...] = (unit * prm_ref[0:1] + prm_ref[4:5]).astype(BF)
            key = lax.broadcasted_iota(jnp.int32, (seq, seq), 0)
            query = lax.broadcasted_iota(jnp.int32, (seq, seq), 1)
            bias_scr[...] = jnp.where((key <= query) & (key < len_ref[0]), 0.0, NEGATIVE)
            acc_scr[...] = part_ref[...].astype(F32) + prm_ref[10:11] if start == 0 else part_ref[...]

        qkv = dot(n1_ref[...], w_scr[:, : 3 * hw])
        q = ((qkv[:, :hw] + hb_ref[0, 0:1]) * HD**-0.5).astype(BF)
        k = qkv[:, hw : 2 * hw].astype(BF)
        v = (qkv[:, 2 * hw :] + hb_ref[0, 1:2]).astype(BF)
        q_ref[0] = q
        k_ref[0] = k
        v_ref[0] = v
        vt = v.T
        for j in range(heads):
            s = dot(k, head_lanes(q, j, HD), 1, 1) + bias_scr[...]
            m = jnp.max(s, 0, keepdims=True)
            p = jnp.exp(s - m)
            total = jnp.sum(p, 0, keepdims=True)
            lse_ref[0, j : j + 1] = m + jnp.log(total)
            ot_ref[0, j * HD : (j + 1) * HD] = dot(vt[j * HD : (j + 1) * HD], p.astype(BF)) / total
        mixed = ot_ref[0].T.astype(BF)
        mix_ref[0] = mixed
        acc_scr[...] += project_out(mixed, w_scr, hw)

        @pl.when(t == count - 1)
        def _():
            first = acc_scr[...]
            first_ref[...] = first
            unit, _ = layer_norm_parts(first)
            n2_ref[...] = (unit * prm_ref[1:2] + prm_ref[5:6]).astype(BF)

    full = whole((seq, width))
    hb = sds((blocks, seq, hw), BF)

    def block(shape):
        return at_block(shape, start)

    return call(
        body, "self_forward", count,
        [(rows, full), (part, full), *pack_at(pack, start), (params, whole(params.shape)),
         (head_bias, block(head_bias.shape))],
        [(hb, block(hb.shape))] * 3
        + [(sds((blocks, 8, seq), F32), block((blocks, 8, seq))),
           (sds((blocks, hw, seq), F32), block((blocks, hw, seq))),
           (hb, block(hb.shape)),
           (sds((seq, width), BF), full),
           (sds((seq, width), F32), full),
           (sds((seq, width), BF), full)],
        [pltpu.VMEM((seq, seq), F32), pltpu.VMEM((seq, width), F32), pack_scratch(width)],
        count * (8 * seq * width * hw + 16 * seq * seq * hw),
        (length, place),
        deps,
        carried,
    )


def frame_keys(place, frames, pack, own, head_bias, piece, dims, deps=()):
    seq, width, blocks, hw = dims
    pieces = len(frames)
    valid = frames[0].shape[0]
    total = pieces * piece
    edge = valid // 16 * 16

    def body(place_ref, *refs):
        f_refs, refs = refs[:pieces], refs[pieces:]
        w_refs, refs = refs[: len(pack)], refs[len(pack) :]
        hb_ref, k_ref, v_ref, kt_ref, vt_ref, e_ref, w_scr = refs
        assemble(w_refs, own, place_ref, w_scr)

        @pl.when(pl.program_id(0) == 0)
        def _():
            for c in range(pieces):
                e_ref[c, edge:] = jnp.zeros((piece - edge, width), BF)
                e_ref[c, :valid] = f_refs[c][...]

        w = w_scr[:, : 2 * hw]
        for c in range(pieces):
            kv = dot(e_ref[c], w)
            k = kv[:, :hw].astype(BF)
            v = (kv[:, hw:] + hb_ref[0, 3:4]).astype(BF)
            k_ref[0, c] = k
            v_ref[0, c] = v
            kt_ref[0, :, c * piece : (c + 1) * piece] = k.T
            vt_ref[0, :, c * piece : (c + 1) * piece] = v.T

    kv = sds((blocks, pieces, piece, hw), BF)
    kvt = sds((blocks, hw, total), BF)
    padded = sds((pieces, piece, width), BF)
    return call(
        body, "frame_keys", blocks,
        [(f, whole(f.shape)) for f in frames] + [*pack_in(pack), (head_bias, per_block(head_bias.shape))],
        [(kv, per_block(kv.shape))] * 2 + [(kvt, per_block(kvt.shape))] * 2 + [(padded, whole(padded.shape))],
        [pack_scratch(width)],
        4 * total * width * width,
        (place,),
        deps,
    )


def cross_forward(place, start, count, n2, first, pack, own, params, head_bias, keys, values_t, valid, dims, deps=(),
                  carried=()):
    seq, width, blocks, hw = dims
    heads = hw // HD
    _, pieces, piece, _ = keys.shape
    total_keys = pieces * piece

    def body(place_ref, n2_ref, first_ref, *refs):
        w_refs, refs = refs[: len(pack)], refs[len(pack) :]
        (prm_ref, hb_ref, k_ref, vt_ref, q_ref, lse_ref, ot_ref, mix_ref, second_ref, n3_ref, s_scr,
         p_scr, acc_scr, w_scr) = refs
        t = pl.program_id(0)
        assemble(w_refs, own, place_ref, w_scr)

        @pl.when(t == 0)
        def _():
            acc_scr[...] = first_ref[...] + prm_ref[13:14] if start == 0 else first_ref[...]

        q = ((dot(n2_ref[...], w_scr[:, 2 * hw : 3 * hw]) + hb_ref[0, 2:3]) * HD**-0.5).astype(BF)
        q_ref[0] = q
        row = lax.broadcasted_iota(jnp.int32, (piece, 1), 0)
        pad = jnp.where(row < valid, 0.0, NEGATIVE)

        for j in range(heads):
            qm = head_lanes(q, j, HD)

            def score(c, m):
                s = dot(k_ref[0, c], qm, 1, 1) + pad
                s_scr[c] = s
                return jnp.maximum(m, jnp.max(s, 0, keepdims=True))

            m = lax.fori_loop(0, pieces, score, jnp.full((1, seq), NEGATIVE, F32))

            def weigh(c, total):
                p = jnp.exp(s_scr[c] - m)
                p_scr[pl.ds(pl.multiple_of(c * piece, piece), piece)] = p.astype(BF)
                return total + jnp.sum(p, 0, keepdims=True)

            total = lax.fori_loop(0, pieces, weigh, jnp.zeros((1, seq), F32))
            lse_ref[0, j : j + 1] = m + jnp.log(total)
            at = j * HD
            ot_ref[0, at : at + HD] = dot(vt_ref[0, at : at + HD], p_scr[...]) / total

        mixed = ot_ref[0].T.astype(BF)
        mix_ref[0] = mixed
        acc_scr[...] += project_out(mixed, w_scr, hw)

        @pl.when(t == count - 1)
        def _():
            second = acc_scr[...]
            second_ref[...] = second
            unit, _ = layer_norm_parts(second)
            n3_ref[...] = (unit * prm_ref[2:3] + prm_ref[6:7]).astype(BF)

    full = whole((seq, width))
    hb = sds((blocks, seq, hw), BF)

    def block(shape):
        return at_block(shape, start)

    packs = pack_at(pack, start)
    return call(
        body, "cross_forward", count,
        [(n2, full), (first, full), *packs, (params, whole(params.shape)), (head_bias, block(head_bias.shape)),
         (keys, block(keys.shape)), (values_t, block(values_t.shape))],
        [(hb, block(hb.shape)), (sds((blocks, 8, seq), F32), block((blocks, 8, seq))),
         (sds((blocks, hw, seq), F32), block((blocks, hw, seq))), (hb, block(hb.shape)),
         (sds((seq, width), F32), full), (sds((seq, width), BF), full)],
        [pltpu.VMEM((pieces, piece, seq), F32), pltpu.VMEM((total_keys, seq), BF),
         pltpu.VMEM((seq, width), F32), pack_scratch(width)],
        count * (4 * seq * width * hw + 4 * seq * total_keys * 256 * heads),
        (place,),
        deps,
        carried,
    )


def feed_forward(place, n3, second, w_in, w_out, own, params, cotangent, dims, deps=()):
    seq, width, blocks, hw = dims

    def body(place_ref, n3_ref, second_ref, *refs):
        wi_refs, wo_refs, refs = refs[: len(w_in)], refs[len(w_in) : 2 * len(w_in)], refs[2 * len(w_in) :]
        (prm_ref, cot_ref, hid_ref, slope_ref, out_ref, g3_ref, b3_ref, sum_ref, wi_scr, wo_scr,
         acc_scr) = refs
        t = pl.program_id(0)
        assemble(wi_refs, own, place_ref, wi_scr)
        assemble(wo_refs, own, place_ref, wo_scr)

        @pl.when(t == 0)
        def _():
            acc_scr[...] = second_ref[...] + prm_ref[14:15]

        before = dot(n3_ref[...], wi_scr[...]) + prm_ref[pl.ds(15 + t, 1)]
        phi = 0.5 + 0.5 * lax.erf(before * 2**-0.5)
        hidden = (before * phi).astype(BF)
        hid_ref[0] = hidden
        slope_ref[0] = phi + before * (jnp.exp(-0.5 * before * before) * 0.3989422804014327)
        acc_scr[...] += dot(hidden, wo_scr[...], 1, 1)

        @pl.when(t == blocks - 1)
        def _():
            unit, inverse = layer_norm_parts(acc_scr[...])
            out_ref[...] = (unit * prm_ref[3:4] + prm_ref[7:8]).astype(BF)
            cot = cot_ref[...].astype(F32)
            grad = norm_back(cot, unit, inverse, prm_ref[3:4])
            g3_ref[...] = grad
            branch = grad.astype(BF)
            b3_ref[...] = branch
            sum_ref[...] = jnp.zeros_like(sum_ref)
            sum_ref[3:4] = column_sum(cot * unit)
            sum_ref[7:8] = column_sum(cot)
            sum_ref[14:15] = column_sum(branch.astype(F32))

    full = whole((seq, width))
    wide = (blocks, seq, width)
    return call(
        body, "feed_forward", blocks,
        [(n3, full), (second, full), *pack_in(w_in), *pack_in(w_out),
         (params, whole(params.shape)), (cotangent, full)],
        [(sds(wide, BF), per_block(wide)), (sds(wide, F32), per_block(wide)),
         (sds((seq, width), BF), full), (sds((seq, width), F32), full),
         (sds((seq, width), BF), full), (sds(params.shape, F32), whole(params.shape))],
        [pack_scratch(width), pack_scratch(width), pltpu.VMEM((seq, width), F32)],
        16 * seq * width * width,
        (place,),
        deps,
    )


def feed_out_grads(place, b3, hidden, grad_shape, dims, deps=()):
    seq, width, blocks, hw = dims

    def body(place_ref, b3_ref, hid_ref, *refs):
        grad_refs, (b3t_scr,) = refs[:-1], refs[-1:]

        @pl.when(pl.program_id(0) == 0)
        def _():
            b3t_scr[...] = b3_ref[...].T

        store_pack(grad_refs, dot(b3t_scr[...], hid_ref[0]).astype(BF), place_ref)

    wide = (blocks, seq, width)
    return call(
        body, "feed_out_grads", blocks,
        [(b3, whole((seq, width))), (hidden, per_block(wide))],
        grad_outs(grad_shape),
        [pltpu.VMEM((width, seq), BF)],
        8 * seq * width * width,
        (place,),
        deps,
    )


def feed_backward(place, b3, g3, slope, w_in, w_out, own, n3, second, params, sums, grad_shape, dims, deps=()):
    seq, width, blocks, hw = dims
    grads = grad_outs(grad_shape)

    def body(place_ref, b3_ref, g3_ref, slope_ref, *refs):
        wi_refs, wo_refs, refs = refs[: len(w_in)], refs[len(w_in) : 2 * len(w_in)], refs[2 * len(w_in) :]
        (n3_ref, second_ref, prm_ref, old_ref), refs = refs[:4], refs[4:]
        grad_refs, refs = refs[: len(grads)], refs[len(grads) :]
        g2_ref, b2_ref, sum_ref, wi_scr, wo_scr, n3t_scr, acc_scr = refs
        t = pl.program_id(0)
        assemble(wi_refs, own, place_ref, wi_scr)
        assemble(wo_refs, own, place_ref, wo_scr)

        @pl.when(t == 0)
        def _():
            sum_ref[...] = old_ref[...]
            n3t_scr[...] = n3_ref[...].T
            acc_scr[...] = jnp.zeros_like(acc_scr)

        grad_before = (dot(b3_ref[...], wo_scr[...]) * slope_ref[0]).astype(BF)
        sum_ref[pl.ds(15 + t, 1)] = column_sum(grad_before.astype(F32))
        store_pack(grad_refs, dot(n3t_scr[...], grad_before).astype(BF), place_ref)
        acc_scr[...] += dot(grad_before, wi_scr[...], 1, 1)

        @pl.when(t == blocks - 1)
        def _():
            grad = acc_scr[...]
            unit, inverse = layer_norm_parts(second_ref[...])
            sum_ref[2:3] = column_sum(grad * unit)
            sum_ref[6:7] = column_sum(grad)
            grad_second = g3_ref[...] + norm_back(grad, unit, inverse, prm_ref[2:3])
            g2_ref[...] = grad_second
            branch = grad_second.astype(BF)
            b2_ref[...] = branch
            sum_ref[13:14] = column_sum(branch.astype(F32))

    full = whole((seq, width))
    wide = (blocks, seq, width)
    return call(
        body, "feed_backward", blocks,
        [(b3, full), (g3, full), (slope, per_block(wide)), *pack_in(w_in), *pack_in(w_out), (n3, full),
         (second, full), (params, whole(params.shape)), (sums, whole(sums.shape))],
        grads
        + [(sds((seq, width), F32), full), (sds((seq, width), BF), full),
           (sds(sums.shape, F32), whole(sums.shape))],
        [pack_scratch(width), pack_scratch(width), pltpu.VMEM((width, seq), BF), pltpu.VMEM((seq, width), F32)],
        24 * seq * width * width,
        (place,),
        deps,
    )


def cross_attend_back(place, start, count, sums, b2, queries, keys, values, keys_t, lse, ot, pack, own, valid,
                      dims, deps=(), carried=()):
    seq, width, blocks, hw = dims
    heads = hw // HD
    _, pieces, piece, _ = keys.shape
    total_keys = pieces * piece

    def body(place_ref, old_ref, b2_ref, q_ref, k_ref, v_ref, kt_ref, lse_ref, ot_ref, *refs):
        w_refs, refs = refs[: len(pack)], refs[len(pack) :]
        dq_ref, dkv_ref, sum_ref, w_scr, dk_scr, dv_scr, ds_scr, dqt_scr = refs
        t = pl.program_id(0)
        assemble(w_refs, own, place_ref, w_scr)

        @pl.when(t == 0)
        def _():
            sum_ref[...] = old_ref[...]

        q = q_ref[0]
        gm = project_back(b2_ref[...], w_scr, hw).astype(BF)
        weighted = gm.astype(F32).T * ot_ref[0]
        row = lax.broadcasted_iota(jnp.int32, (piece, 1), 0)
        pad = jnp.where(row < valid, 0.0, NEGATIVE)
        dk_scr[...] = jnp.zeros_like(dk_scr)
        dv_scr[...] = jnp.zeros_like(dv_scr)
        for j in range(heads):
            delta = jnp.sum(weighted[j * HD : (j + 1) * HD], 0, keepdims=True)
            shift = lse_ref[0, j : j + 1]
            qm = head_lanes(q, j, HD)
            gj = head_lanes(gm, j, HD)

            def one_piece(c, carry):
                s = dot(k_ref[0, c], qm, 1, 1) + pad
                p = jnp.exp(s - shift)
                ds = (p * (dot(v_ref[0, c], gj, 1, 1) - delta)).astype(BF)
                dv_scr[c] += dot(p.astype(BF), gj)
                dk_scr[c] += dot(ds, qm)
                ds_scr[pl.ds(pl.multiple_of(c * piece, piece), piece)] = ds
                return carry

            lax.fori_loop(0, pieces, one_piece, 0)
            dqt_scr[j * HD : (j + 1) * HD] = dot(kt_ref[0, j * HD : (j + 1) * HD], ds_scr[...])
        dq = dqt_scr[...].T.astype(BF).astype(F32) * HD**-0.5
        put_heads(sum_ref, 11, start + t, blocks, column_sum(dq))
        dq_ref[0] = dq.astype(BF)
        bias = jnp.zeros((1, hw), F32)
        for c in range(pieces):
            dv = dv_scr[c].astype(BF)
            bias += column_sum(dv.astype(F32))
            dkv_ref[0, c] = jnp.concatenate([dk_scr[c].astype(BF), dv], 1)
        put_heads(sum_ref, 12, start + t, blocks, bias)

    def block(shape):
        return at_block(shape, start)

    packs = pack_at(pack, start)
    dkv = (blocks, pieces, piece, 2 * hw)
    return call(
        body, "cross_attend_back", count,
        [(sums, whole(sums.shape)), (b2, whole((seq, width))), (queries, block(queries.shape)), (keys, block(keys.shape)),
         (values, block(values.shape)), (keys_t, block(keys_t.shape)), (lse, block(lse.shape)),
         (ot, block(ot.shape)), *packs],
        [(sds(queries.shape, BF), block(queries.shape)), (sds(dkv, BF), block(dkv)),
         (sds(sums.shape, F32), whole(sums.shape))],
        [pack_scratch(width), pltpu.VMEM((pieces, piece, hw), F32), pltpu.VMEM((pieces, piece, hw), F32),
         pltpu.VMEM((total_keys, seq), BF), pltpu.VMEM((hw, seq), F32)],
        count * (2 * seq * width * hw + 10 * seq * total_keys * 256 * heads // 2),
        (place,),
        deps,
        carried,
    )


def cross_rows_back(place, sums, dq, dkv, g2, first, pack, own, params, valid, dims, deps=()):
    seq, width, blocks, hw = dims
    _, pieces, piece, _ = dkv.shape
    frames = (pieces, piece, width)
    kept = (valid, width)

    def body(place_ref, old_ref, dq_ref, dkv_ref, g2_ref, first_ref, *refs):
        w_refs, refs = refs[: len(pack)], refs[len(pack) :]
        prm_ref, *genc_refs, g1_ref, b1_ref, sum_ref, w_scr, genc_scr, acc_scr = refs
        t = pl.program_id(0)
        assemble(w_refs, own, place_ref, w_scr)

        @pl.when(t == 0)
        def _():
            acc_scr[...] = jnp.zeros_like(acc_scr)
            genc_scr[...] = jnp.zeros_like(genc_scr)
            sum_ref[...] = old_ref[...]

        wkv = w_scr[:, : 2 * hw]
        for c in range(pieces):
            genc_scr[c] += dot(dkv_ref[0, c], wkv, 1, 1)
        acc_scr[...] += dot(dq_ref[0], w_scr[:, 2 * hw : 3 * hw], 1, 1)

        @pl.when(t == blocks - 1)
        def _():
            for c in range(pieces):
                genc_refs[c][...] = genc_scr[c, :valid].astype(BF)
            grad = acc_scr[...]
            unit, inverse = layer_norm_parts(first_ref[...])
            sum_ref[1:2] = column_sum(grad * unit)
            sum_ref[5:6] = column_sum(grad)
            grad_first = g2_ref[...] + norm_back(grad, unit, inverse, prm_ref[1:2])
            g1_ref[...] = grad_first
            branch = grad_first.astype(BF)
            b1_ref[...] = branch
            sum_ref[10:11] = column_sum(branch.astype(F32))

    full = whole((seq, width))
    return call(
        body, "cross_rows_back", blocks,
        [(sums, whole(sums.shape)), (dq, per_block(dq.shape)), (dkv, per_block(dkv.shape)), (g2, full), (first, full), *pack_in(pack),
         (params, whole(params.shape))],
        [(sds(kept, BF), whole(kept))] * pieces
        + [(sds((seq, width), F32), full), (sds((seq, width), BF), full),
         (sds(sums.shape, F32), whole(sums.shape))],
        [pack_scratch(width), pltpu.VMEM(frames, F32), pltpu.VMEM((seq, width), F32)],
        2 * seq * width * width + 4 * pieces * piece * width * width,
        (place,),
        deps,
    )


def cross_grads(place, dq, dkv, mixed, b2, n2, frames, grad_shape, dims, deps=()):
    seq, width, blocks, hw = dims
    _, pieces, piece, _ = dkv.shape
    total_keys = pieces * piece

    def body(place_ref, dq_ref, dkv_ref, mix_ref, b2_ref, n2_ref, e_ref, *refs):
        grad_refs, (et_scr, b2t_scr, n2t_scr) = refs[:-3], refs[-3:]

        @pl.when(pl.program_id(0) == 0)
        def _():
            for c in range(pieces):
                et_scr[:, c * piece : (c + 1) * piece] = e_ref[c].T
            b2t_scr[...] = b2_ref[...].T
            n2t_scr[...] = n2_ref[...].T

        grad_kv = dot(et_scr[...], dkv_ref[0].reshape(total_keys, 2 * hw))
        grad_q = dot(n2t_scr[...], dq_ref[0])
        grad_o = dot(b2t_scr[...], mix_ref[0])
        store_pack(grad_refs, jnp.concatenate([grad_kv, grad_q, grad_o], 1).astype(BF), place_ref)

    full = whole((seq, width))
    return call(
        body, "cross_grads", blocks,
        [(dq, per_block(dq.shape)), (dkv, per_block(dkv.shape)), (mixed, per_block(mixed.shape)), (b2, full),
         (n2, full), (frames, whole(frames.shape))],
        grad_outs(grad_shape),
        [pltpu.VMEM((width, total_keys), BF), pltpu.VMEM((width, seq), BF), pltpu.VMEM((width, seq), BF)],
        4 * seq * width * width + 4 * total_keys * width * width,
        (place,),
        deps,
    )


def self_attend_back(length, place, sums, b1, n1, queries, keys, values, mixed, lse, ot, pack, own, grad_shape, dims,
                     deps=()):
    seq, width, blocks, hw = dims
    heads = hw // HD
    grads = grad_outs(grad_shape)

    def body(len_ref, place_ref, old_ref, b1_ref, n1_ref, q_ref, k_ref, v_ref, mix_ref, lse_ref, ot_ref, *refs):
        w_refs, refs = refs[: len(pack)], refs[len(pack) :]
        grad_refs, refs = refs[: len(grads)], refs[len(grads) :]
        dqkv_ref, sum_ref, w_scr, bias_scr, dqt_scr, b1t_scr, n1t_scr = refs
        t = pl.program_id(0)
        assemble(w_refs, own, place_ref, w_scr)

        @pl.when(t == 0)
        def _():
            sum_ref[...] = old_ref[...]
            b1t_scr[...] = b1_ref[...].T
            n1t_scr[...] = n1_ref[...].T
            key = lax.broadcasted_iota(jnp.int32, (seq, seq), 0)
            query = lax.broadcasted_iota(jnp.int32, (seq, seq), 1)
            bias_scr[...] = jnp.where((key <= query) & (key < len_ref[0]), 0.0, NEGATIVE)

        q = q_ref[0]
        k = k_ref[0]
        v = v_ref[0]
        kt = k.T
        gm = project_back(b1_ref[...], w_scr, hw).astype(BF)
        weighted = gm.astype(F32).T * ot_ref[0]
        dk = jnp.zeros((seq, hw), F32)
        dv = jnp.zeros((seq, hw), F32)
        for j in range(heads):
            delta = jnp.sum(weighted[j * HD : (j + 1) * HD], 0, keepdims=True)
            qm = head_lanes(q, j, HD)
            gj = head_lanes(gm, j, HD)
            p = jnp.exp(dot(k, qm, 1, 1) + bias_scr[...] - lse_ref[0, j : j + 1])
            ds = (p * (dot(v, gj, 1, 1) - delta)).astype(BF)
            dv += dot(p.astype(BF), gj)
            dk += dot(ds, qm)
            dqt_scr[j * HD : (j + 1) * HD] = dot(kt[j * HD : (j + 1) * HD], ds)
        dq = dqt_scr[...].T.astype(BF).astype(F32) * HD**-0.5
        dv = dv.astype(BF)
        put_heads(sum_ref, 8, t, blocks, column_sum(dq))
        put_heads(sum_ref, 9, t, blocks, column_sum(dv.astype(F32)))
        dqkv = jnp.concatenate([dq.astype(BF), dk.astype(BF), dv], 1)
        dqkv_ref[0] = dqkv
        grad = jnp.concatenate([dot(n1t_scr[...], dqkv), dot(b1t_scr[...], mix_ref[0])], 1)
        store_pack(grad_refs, grad.astype(BF), place_ref)

    hb = per_block((blocks, seq, hw))
    dqkv = (blocks, seq, 3 * hw)
    return call(
        body, "self_attend_back", blocks,
        [(sums, whole(sums.shape)), (b1, whole((seq, width))), (n1, whole((seq, width))), (queries, hb), (keys, hb),
         (values, hb), (mixed, hb), (lse, per_block(lse.shape)), (ot, per_block(ot.shape)), *pack_in(pack)],
        grads + [(sds(dqkv, BF), per_block(dqkv)), (sds(sums.shape, F32), whole(sums.shape))],
        [pack_scratch(width), pltpu.VMEM((seq, seq), F32), pltpu.VMEM((hw, seq), F32), pltpu.VMEM((width, seq), BF),
         pltpu.VMEM((width, seq), BF)],
        10 * seq * width * width + 40 * seq * seq * width,
        (length, place),
        deps,
    )


def self_rows_back(place, sums, dqkv, g1, rows, pack, own, params, dims, deps=()):
    seq, width, blocks, hw = dims

    def body(place_ref, old_ref, dqkv_ref, g1_ref, x_ref, *refs):
        w_refs, refs = refs[: len(pack)], refs[len(pack) :]
        prm_ref, gin_ref, sum_ref, w_scr, acc_scr = refs
        t = pl.program_id(0)
        assemble(w_refs, own, place_ref, w_scr)

        @pl.when(t == 0)
        def _():
            acc_scr[...] = jnp.zeros_like(acc_scr)
            sum_ref[...] = old_ref[...]

        acc_scr[...] += dot(dqkv_ref[0], w_scr[:, : 3 * hw], 1, 1)

        @pl.when(t == blocks - 1)
        def _():
            grad = acc_scr[...]
            unit, inverse = layer_norm_parts(x_ref[...].astype(F32))
            sum_ref[0:1] = column_sum(grad * unit)
            sum_ref[4:5] = column_sum(grad)
            gin_ref[...] = g1_ref[...] + norm_back(grad, unit, inverse, prm_ref[0:1])

    full = whole((seq, width))
    return call(
        body, "self_rows_back", blocks,
        [(sums, whole(sums.shape)), (dqkv, per_block(dqkv.shape)), (g1, full), (rows, full), *pack_in(pack), (params, whole(params.shape))],
        [(sds((seq, width), F32), full), (sds(sums.shape, F32), whole(sums.shape))],
        [pack_scratch(width), pltpu.VMEM((seq, width), F32)],
        6 * seq * width * width,
        (place,),
        deps,
    )


def pad_rows(rows, count):
    return jnp.pad(rows, ((0, count - rows.shape[0]),) + ((0, 0),) * (rows.ndim - 1))


def swap(array, step):
    count = lax.axis_size("fsdp")
    return lax.ppermute(array, "fsdp", [(i, i ^ step) for i in range(count)])


def around(array, hop):
    count = lax.axis_size("tp")
    return lax.ppermute(array, "tp", [(i, (i + hop) % count) for i in range(count)])


def native_gather(shard):
    whole_pack = lax.all_gather(shard, ("fsdp", "tp"), axis=0, tiled=False)
    return whole_pack.reshape((lax.axis_size("fsdp"), lax.axis_size("tp")) + shard.shape)


def in_order(pieces, here):
    count = len(pieces)
    stacked = jnp.stack(pieces)
    return jnp.stack(
        [lax.dynamic_index_in_dim(stacked, (here - t) % count, 0, keepdims=False) for t in range(count)]
    )


def gate(array, things):
    return lax.optimization_barrier((array,) + tuple(things))[0] if things else array


class Gather:
    def __init__(self, shard):
        self.shard = shard

    def direct(self):
        come = [around(self.shard, hop) for hop in range(1, 4)]
        line = in_order([self.shard] + come, lax.axis_index("tp"))
        self.low, self.high = line[None, :2], line[None, 2:]
        return tuple(come)

    def first(self):
        self.low_x, self.high_y = swap(self.low, 2), swap(self.high, 4)
        return self.low_x, self.high_y

    def second(self):
        self.low_two = jnp.concatenate([self.low, self.low_x])
        self.high_two = jnp.concatenate([self.high, self.high_y])
        self.low_y, self.high_x = swap(self.low_two, 4), swap(self.high_two, 2)
        return self.low_y, self.high_x

    def core(self):
        low = jnp.concatenate([self.low_two, self.low_y])
        high = jnp.stack([self.high_two[0], self.high_x[0], self.high_two[1], self.high_x[1]])
        mine = jnp.concatenate([low, high], 1)
        self.pack = (mine, swap(mine, 1))
        return self.pack[1:]


def wide(array):
    return array.astype(F32)


class Scatter:
    def __init__(self, halves):
        self.kept, self.sent = halves
        self.tp = self.kept.shape[1]
        self.half = self.tp // 2

    def core(self):
        self.come = swap(self.sent, 1)
        return self.come

    def first(self):
        def both(q, t):
            return (wide(self.kept[q, t]) + wide(self.come[q, t])).astype(BF)

        low, high = slice(0, self.half), slice(self.half, self.tp)
        self.low_y = swap(both(slice(2, 4), low), 4)
        self.high_x = swap(both(slice(1, 4, 2), high), 2)
        return self.low_y, self.high_x

    def second(self):
        low, high = slice(0, self.half), slice(self.half, self.tp)

        def three(q, t, more):
            return wide(self.kept[q, t]) + wide(self.come[q, t]) + wide(more)

        self.low_x = swap(three(1, low, self.low_y[1]).astype(BF), 2)
        self.high_y = swap(three(2, high, self.high_x[1]).astype(BF), 4)
        return self.low_x, self.high_y

    def sides(self):
        def total(t, more, last):
            return wide(self.kept[0, t]) + wide(self.come[0, t]) + wide(more) + wide(last)

        low, high = slice(0, self.half), slice(self.half, self.tp)
        self.sums = jnp.concatenate(
            [total(low, self.low_y[0], self.low_x), total(high, self.high_x[0], self.high_y)]
        ).astype(BF)
        self.own = lax.dynamic_index_in_dim(self.sums, lax.axis_index("tp"), 0, keepdims=False)
        self.parts = [self.part(hop) for hop in range(1, self.tp, 2)]
        return tuple(self.parts)

    def across(self):
        more = [self.part(hop) for hop in range(2, self.tp, 2)]
        self.parts += more
        return tuple(more)

    def line(self):
        return self.sides() + self.across()

    def part(self, hop):
        place = (lax.axis_index("tp") + hop) % self.tp
        return around(lax.dynamic_index_in_dim(self.sums, place, 0, keepdims=False), hop)

    def total(self):
        result = wide(self.own)
        for part in self.parts:
            result += wide(part)
        return result


def butterfly_scatter(grads, own, narrow=BF):
    fsdp, tp = lax.axis_size("fsdp"), lax.axis_size("tp")
    if grads.shape[0] != fsdp:
        blocks, width = grads.shape[1], grads.shape[3]
        grads = grads.reshape(blocks, fsdp, own, width).transpose(1, 0, 2, 3)
    place = lax.axis_index("fsdp")
    step = 1
    while step < fsdp:
        pairs = grads.reshape((grads.shape[0] // 2, 2) + grads.shape[1:])
        bit = (place // step) % 2
        kept = lax.dynamic_index_in_dim(pairs, bit, 1, keepdims=False)
        sent = lax.dynamic_index_in_dim(pairs, 1 - bit, 1, keepdims=False)
        grads = (wide(kept) + wide(swap(sent, step))).astype(narrow)
        step *= 2
    grads = grads[0]
    here = lax.axis_index("tp")
    total = wide(lax.dynamic_index_in_dim(grads, here, 0, keepdims=False))
    for hop in range(1, tp):
        sent = lax.dynamic_index_in_dim(grads, (here + hop) % tp, 0, keepdims=False)
        total += wide(around(sent, hop))
    return total


def local(
    inputs,
    encoder,
    lengths,
    self_qkv,
    self_out,
    cross_q,
    cross_kv,
    cross_out,
    fc_in,
    fc_out,
    norm_gain,
    norm_bias,
    proj_bias,
    fc_in_bias,
    cotangent,
):
    fsdp, tp = lax.axis_size("fsdp"), lax.axis_size("tp")
    devices = fsdp * tp
    tp_place = lax.axis_index("tp")
    place = jnp.stack([lax.axis_index("fsdp"), tp_place])
    seqs, seq, width = inputs.shape
    assert seqs == 1
    own, hw = cross_q.shape
    dims = (seq, width, tp, hw)
    frames_own = encoder.shape[1]
    small_own = norm_gain.shape[1]
    ff_own = fc_in_bias.shape[0]
    chained = fsdp == 8 and tp == 4 and own % 16 == 0

    small = jnp.concatenate(
        [a.reshape(-1) for a in (norm_gain, norm_bias, proj_bias, fc_in_bias)]
    )
    small = jnp.pad(small, (0, width - small.size))
    high = small.astype(BF)
    low = (small - high.astype(F32)).astype(BF)
    extra = pad_rows(jnp.stack([high, low]), 16)

    pack_self = jnp.concatenate([self_qkv[0], self_qkv[1], self_qkv[2], self_out.T], 1)
    pack_self = jnp.concatenate([pack_self, extra], 0)
    pack_cross = jnp.concatenate([cross_kv[0], cross_kv[1], cross_q, cross_out.T], 1)
    x = inputs[0]
    length = lax.dynamic_slice_in_dim(lengths, tp_place, 1)
    chains = {}
    sends = {"direct": "shard", "first": "low high", "second": "low_x high_y", "core": "low_y high_x"}

    def move(after, *steps):
        out = ()
        for text in steps if chained else ():
            name, step = text.split(".")
            chain = chains[name]
            for array in sends[step].split():
                setattr(chain, array, gate(getattr(chain, array), after))
            out += getattr(chain, step)()
        return out

    frames = [
        lax.dynamic_index_in_dim(encoder, (tp_place + hop) % tp, 0, keepdims=False) for hop in range(tp)
    ]
    before = turn = ()
    if chained:
        for name, shard in (("self", pack_self), ("cross", pack_cross), ("in", fc_in), ("out", fc_out.T)):
            chains[name] = Gather(shard)
        turn = move((), "self.direct") + tuple(frames)
        turn = move(turn, "self.first", "cross.direct")
        turn = move(turn, "self.second", "in.direct")
        frames[1] = around(gate(frames[1], turn), 1)
        before = turn = move(turn, "self.core", "cross.first")
        frames[2] = around(gate(frames[2], turn), 2)
        turn = move(turn, "cross.second", "in.first") + (frames[1], frames[2])
        w_self = chains["self"].pack
        own_rows = own
        grad_shape = (fsdp // 2, tp, own, width)
        blocks = jnp.stack([part[:, :, own : own + 2] for part in w_self], 1)
        blocks = blocks.reshape(fsdp, tp, 2, width)
        table = jnp.stack(
            [lax.dynamic_index_in_dim(blocks, f ^ place[0], 0, keepdims=False) for f in range(fsdp)]
        )
        table = wide(table).sum(2).reshape(devices, width)
    else:
        w_self = native_gather(pack_self)
        table = wide(w_self[:, :, own : own + 2]).sum(2).reshape(devices, width)
        own_rows = own * fsdp
        grad_shape = (1, tp, own_rows, width)

        def end_to_end(pack):
            return pack[:, :, :own].transpose(1, 0, 2, 3).reshape(1, tp, own_rows, width)

        w_self = (end_to_end(w_self),)
        w_cross = (end_to_end(native_gather(pack_cross)),)
        w_in = (end_to_end(native_gather(fc_in)),)
        w_out = (end_to_end(native_gather(fc_out.T)),)

    rows = norm_gain.shape[0] + norm_bias.shape[0] + proj_bias.shape[0]
    params = table[:, : rows * small_own].reshape(devices, rows, small_own)
    params = params.transpose(1, 0, 2).reshape(rows, width)
    fc_bias = table[:, rows * small_own : rows * small_own + ff_own].reshape(tp, width)
    head_bias = jnp.stack([params[8], params[9], params[11], params[12]])
    head_bias = head_bias.reshape(4, tp, hw).transpose(1, 0, 2)
    head_bias = jnp.pad(head_bias, ((0, 0), (0, 4), (0, 0)))
    params = pad_rows(jnp.concatenate([params, fc_bias], 0), 24)

    piece = -(-frames_own // 128) * 128
    half = tp // 2

    q1, k1, v1, lse1, ot1, mixed1, n1, first, n2 = self_forward(
        length, place, 0, tp, x, x, w_self, own_rows, params, head_bias, dims, before
    )
    turn += (n2,)
    if chained:
        frames[3] = around(gate(frames[3], turn), 3)
        turn = move(turn, "cross.core", "in.second") + (frames[3],)
        w_cross = chains["cross"].pack
    else:
        frames = [around(array, hop) if hop else array for hop, array in enumerate(frames)]
    k2, v2, k2t, v2t, frames = frame_keys(place, frames, w_cross, own_rows, head_bias, piece, dims, turn)
    turn = move(turn, "in.core", "out.direct") + (k2,)
    shared = (w_cross, own_rows, params, head_bias, k2, v2t, frames_own, dims)
    *kept, part, _ = cross_forward(place, 0, half, n2, first, *shared, turn)
    turn = move(turn, "out.first") + (part,)
    q2, lse2, ot2, mixed2, second, n3 = cross_forward(place, half, tp - half, n2, part, *shared, turn, kept)
    turn = move(turn, "out.second") + (n3,)
    move(turn, "out.core")
    if chained:
        w_in, w_out = chains["in"].pack, chains["out"].pack
    hidden, slope, layer_out, g3, b3, sums = feed_forward(
        place, n3, second, w_in, w_out, own_rows, params, cotangent[0], dims
    )
    scatters = {}

    def begin(name, halves):
        if chained:
            scatters[name] = Scatter(halves)

    def go(name, step):
        if not chained:
            return ()
        out = getattr(scatters[name], step)()
        return out if isinstance(out, tuple) else (out,)

    grad_out = feed_out_grads(place, b3, hidden, grad_shape, dims)
    begin("out", grad_out)
    step1 = go("out", "core")
    *grad_in, g2, b2, sums = feed_backward(
        place, b3, g3, slope, w_in, w_out, own_rows, n3, second, params, sums, grad_shape, dims, (grad_out[0],)
    )
    begin("in", grad_in)
    step2 = go("out", "first") + go("in", "core")
    shared = (b2, q2, k2, v2, k2t, lse2, ot2, w_cross, own_rows, frames_own, dims)
    *kept, sums = cross_attend_back(place, 0, half, sums, *shared, step1)
    step3 = go("out", "second") + go("in", "first")
    dq2, dkv2, sums = cross_attend_back(place, half, tp - half, sums, *shared, step2, kept)
    grad_cross = cross_grads(place, dq2, dkv2, mixed2, b2, n2, frames, grad_shape, dims, step3)
    step4 = go("out", "line") + go("in", "second")
    begin("cross", grad_cross)
    step5 = go("cross", "core")
    *grad_frames, g1, b1, sums = cross_rows_back(
        place, sums, dq2, dkv2, g2, first, w_cross, own_rows, params, frames_own, dims, step4 + (grad_cross[0],)
    )
    step5 += go("in", "line")
    backs = [around(gate(grad_frames[c], step5), tp - c) if c % 2 else grad_frames[c] for c in range(tp)]
    step6 = go("cross", "first") + tuple(backs[1::2])
    *grad_self, dqkv1, sums = self_attend_back(
        length, place, sums, b1, n1, q1, k1, v1, mixed1, lse1, ot1, w_self, own_rows, grad_shape, dims, step5
    )
    begin("self", grad_self)
    go("self", "core")
    grad_inputs, sums = self_rows_back(
        place, sums, dqkv1, g1, x, w_self, own_rows, params, dims, step6 + (grad_self[0],)
    )

    for c in range(2, tp, 2):
        backs[c] = around(gate(backs[c], step6 + (grad_self[0],)), tp - c)

    turns = [()]
    if chained:
        scatters["cross"].low_y = gate(scatters["cross"].low_y, (grad_self[0],))
        step7 = go("cross", "second")
        scatters["self"].come = gate(scatters["self"].come, (sums, *step7))
        turns = [go("self", "first")]
        scatters["cross"].low_x = gate(scatters["cross"].low_x, (sums, *step7))
        go("cross", "sides")
        for name in ("out", "in"):
            scatters[name].own = gate(scatters[name].own, turns[0])
        scatters["self"].low_y = gate(scatters["self"].low_y, (backs[2],))
        turns.append(go("self", "second"))
        scatters["cross"].sums = gate(scatters["cross"].sums, turns[0])
        scatters["self"].low_x = gate(scatters["self"].low_x, go("cross", "across"))
    sums = gate(sums, turns[0])
    sums = sums + swap(sums, 1)
    step = 1
    while step < tp:
        sums = sums + lax.ppermute(sums, "tp", [(i, i ^ step) for i in range(tp)])
        step *= 2
    sums = gate(sums, turns[-1])
    step = 2
    while step < fsdp:
        sums = sums + swap(sums, step)
        step *= 2
    frames_back = in_order([backs[-hop % tp] for hop in range(tp)], tp_place)
    device = lax.axis_index("fsdp") * tp + tp_place
    mine = lax.dynamic_slice_in_dim(sums[:rows], device * small_own, small_own, 1)
    gains = norm_gain.shape[0]
    own_gain, own_shift, own_bias = mine[:gains], mine[gains : 2 * gains], mine[2 * gains :]
    per_row = width // ff_own
    own_fc_bias = lax.dynamic_slice(
        sums, (rows + device // per_row, (device % per_row) * ff_own), (1, ff_own)
    )[0]

    if chained:
        go("self", "line")
        total_out, total_in, total_cross, total_self = (
            scatters[name].total() for name in ("out", "in", "cross", "self")
        )
    else:
        total_out, total_in, total_cross, total_self = (
            butterfly_scatter(grads[0], own) for grads in (grad_out, grad_in, grad_cross, grad_self)
        )

    def part(total, index):
        return total[:, index * hw : (index + 1) * hw]

    return (
        layer_out[None],
        grad_inputs[None],
        frames_back.astype(F32),
        jnp.stack([part(total_self, 0), part(total_self, 1), part(total_self, 2)]),
        part(total_self, 3).T,
        part(total_cross, 2),
        jnp.stack([part(total_cross, 0), part(total_cross, 1)]),
        part(total_cross, 3).T,
        total_in,
        total_out.T,
        own_gain,
        own_shift,
        own_bias,
        own_fc_bias,
    )


def solution(mesh):
    return jax.shard_map(
        local,
        mesh=mesh,
        in_specs=(
            P(("fsdp", "tp"), None, None),
            P("fsdp", "tp", None),
            P("fsdp"),
            P(None, "fsdp", "tp"),
            P("tp", "fsdp"),
            P("fsdp", "tp"),
            P(None, "fsdp", "tp"),
            P("tp", "fsdp"),
            P("fsdp", "tp"),
            P("tp", "fsdp"),
            P(None, ("fsdp", "tp")),
            P(None, ("fsdp", "tp")),
            P(None, ("fsdp", "tp")),
            P(("fsdp", "tp")),
            P(("fsdp", "tp"), None, None),
        ),
        out_specs=(
            P(("fsdp", "tp"), None, None),
            P(("fsdp", "tp"), None, None),
            P("fsdp", "tp", None),
            P(None, "fsdp", "tp"),
            P("tp", "fsdp"),
            P("fsdp", "tp"),
            P(None, "fsdp", "tp"),
            P("tp", "fsdp"),
            P("fsdp", "tp"),
            P("tp", "fsdp"),
            P(None, ("fsdp", "tp")),
            P(None, ("fsdp", "tp")),
            P(None, ("fsdp", "tp")),
            P(("fsdp", "tp")),
        ),
        check_vma=False,
    )
```
